256 devices in a mesh: dp: 2 (over core), ctx: 32 (over z, y), head: 4 (over x).
Axes of the slice: x: 4, y: 4, z: 8, core: 2. Of those that a mesh axis runs over, the one named last changes fastest.
Arguments:
- x_raw: bfloat16 [2, 8192, 8192], P('dp', 'ctx', 'head'), may hold values from -6 to 6
- bc_raw: bfloat16 [2, 8192, 2, 1024], P('dp', 'ctx', None, 'head'), may hold values from -6 to 6
- z_gate: bfloat16 [2, 8192, 8192], P('dp', 'ctx', 'head'), may hold values from -20 to 20
- dt_raw: bfloat16 [2, 128, 8192], P('dp', 'head', 'ctx'), may hold values from -4 to 4
- resets: int32 [2, 8192], P('dp', 'ctx'), may hold values 0 or 1
- conv_x_weight: float32 [4, 8192], P(None, 'head'), may hold values from -3 to 3
- conv_x_bias: float32 [8192], P('head'), may hold values from -1.5 to 1.5
- conv_bc_weight: float32 [4, 2, 1024], P(None, None, 'head'), may hold values from -3 to 3
- conv_bc_bias: float32 [2, 1024], P(None, 'head'), may hold values from -1.5 to 1.5
- a_log: float32 [128], P('head'), may hold values from -9 to 1
- dt_bias: float32 [128], P('head'), may hold values from -13 to -3
- skip_weight: float32 [128], P('head'), may hold values from 0.5 to 2
- norm_gain: float32 [8192], P('head'), may hold values from 0.1 to 1.9
- grad_out: bfloat16 [2, 8192, 8192], P('dp', 'ctx', 'head'), may hold values from -6 to 6
Outputs:
- grad_x: bfloat16 [2, 8192, 8192], P('dp', 'ctx', 'head')
- grad_bc: bfloat16 [2, 8192, 2, 1024], P('dp', 'ctx', None, 'head')
- grad_z: bfloat16 [2, 8192, 8192], P('dp', 'ctx', 'head')
- grad_dt: float32 [2, 128, 8192], P('dp', 'head', 'ctx')
- grad_conv_x_weight: float32 [4, 8192], P(None, 'head')
- grad_conv_x_bias: float32 [8192], P('head')
- grad_conv_bc_weight: float32 [4, 2, 1024], P(None, None, 'head')
- grad_conv_bc_bias: float32 [2, 1024], P(None, 'head')
- grad_a_log: float32 [128], P('head')
- grad_dt_bias: float32 [128], P('head')
- grad_skip: float32 [128], P('head')
- grad_gain: float32 [8192], P('head')
The draws below stay inside these ranges and needn't reach their ends.
All inputs are finite; a program needn't handle non-finite values. No bound on the sum of `resets` on one device may be relied on, other than what follows from the above.
Results may differ from the reference program's by a relative error of at most 0.01595.
Values may be sent and summed in bfloat16 or wider, within the bound.
A program may use at most 256 MiB of HBM per device.

```python
import functools
import jax
import jax.numpy as jnp
from jax import lax

HEADS = 128
HEAD_DIM = 64
NSTATE = 128
GROUPS = 8
CONV = 4
STRETCH = 128
INNER = 8192
BATCH = 2
LENGTH = 8192


def draw_a_log(key, part):
    values = jax.random.uniform(key, (HEADS,), jnp.float32, -2.0, 1.0)
    return values


def draw_z_gate(key, part):
    key_a = jax.random.fold_in(key, 11)
    key_b = jax.random.fold_in(key, 12)
    channel = jnp.exp(jax.random.uniform(key_b, (INNER,), jnp.float32, -1.15, 1.15))
    values = jax.random.normal(key_a, (BATCH, LENGTH, INNER), jnp.float32) * channel
    return jnp.clip(values, -20.0, 20.0).astype(jnp.bfloat16)


def place_ends(values, stream_key, least, top_value):
    extent = values.shape
    spot = [jax.random.randint(jax.random.fold_in(stream_key, axis), (), 0, extent[axis]) for axis in range(len(extent))]
    values = values.at[tuple(spot)].set(least)
    longest = extent.index(max(extent))
    spot[longest] = (spot[longest] + 1) % extent[longest]
    return values.at[tuple(spot)].set(top_value)


def level_of(key, dims, split, smallest, high):
    factor_of, own = 1.0, jax.random.fold_in(key, 6)
    for dim, parts in split:
        heights = jnp.exp(jax.random.uniform(jax.random.fold_in(own, dim), (parts,), jnp.float32, smallest / len(split), high / len(split)))
        factor_of = factor_of * jnp.repeat(heights, dims[dim] // parts).reshape([-1 if axis == dim else 1 for axis in range(len(dims))])
    return factor_of


def noise(stream_key, shape, deviation, bound, cuts=(), dtype=jnp.bfloat16):
    drawn = deviation * jax.random.normal(stream_key, shape, jnp.float32)
    if cuts:
        drawn = drawn * level_of(stream_key, shape, cuts, -0.22, 0.18)
    return jnp.clip(drawn, -bound, bound).astype(dtype)


def setup_inputs(seed: int = 0) -> dict:
    splits = jax.random.split(jax.random.key(seed), 15)
    return {
        "x_raw": noise(splits[0], (BATCH, LENGTH, INNER), 1.0, 6.0, ((0, 2), (1, 32), (2, 4))),
        "bc_raw": noise(splits[1], (BATCH, LENGTH, 2, GROUPS * NSTATE), 1.0, 6.0, ((0, 2), (1, 32), (3, 4))),
        "z_gate": draw_z_gate(jax.random.fold_in(splits[14], 71), 0),
        "dt_raw": noise(splits[3], (BATCH, HEADS, LENGTH), 1.0, 4.0, ((0, 2), (1, 4), (2, 32))),
        "resets": place_ends((jax.random.randint(splits[4], (BATCH, LENGTH), 0, LENGTH) < 4).astype(jnp.int32), jax.random.fold_in(splits[4], 1), 0, 1),
        "conv_x_weight": noise(splits[5], (CONV, INNER), CONV ** -0.5, 3.0, ((1, 4),), jnp.float32),
        "conv_x_bias": noise(splits[6], (INNER,), 0.3, 1.5, ((0, 4),), jnp.float32),
        "conv_bc_weight": noise(splits[7], (CONV, 2, GROUPS * NSTATE), CONV ** -0.5, 3.0, ((2, 4),), jnp.float32),
        "conv_bc_bias": noise(splits[8], (2, GROUPS * NSTATE), 0.3, 1.5, ((1, 4),), jnp.float32),
        "a_log": draw_a_log(jax.random.fold_in(splits[14], 71), 0),
        "dt_bias": jnp.clip(-13.0 + 10.0 * jax.random.uniform(splits[10], (HEADS,), jnp.float32) ** level_of(splits[10], (HEADS,), ((0, 4),), -0.2, 0.2), -13.0, -3.0),
        "skip_weight": jnp.clip(0.5 + 1.5 * jax.random.uniform(splits[11], (HEADS,), jnp.float32) ** level_of(splits[11], (HEADS,), ((0, 4),), -0.2, 0.2), 0.5, 2.0),
        "norm_gain": jnp.clip(1.0 + 0.18 * jax.random.normal(splits[12], (INNER,), jnp.float32), 0.1, 1.9),
        "grad_out": noise(splits[13], (BATCH, LENGTH, INNER), 1.0, 6.0, ((0, 2), (1, 32), (2, 4))),
    }


norm_eps = 1e-05

def kept(value):
    return lax.optimization_barrier(value)

def causal_conv(extended, counts, weight, conv_bias):
    pad_rows = CONV - 1
    row_count = extended.shape[0] - pad_rows
    shape_tail = (1,) * (extended.ndim - 1)
    summed = conv_bias + weight[0] * extended[pad_rows:]
    for lag_step in range(1, CONV):
        lower = pad_rows - lag_step
        live_mask = (counts[pad_rows:] == counts[lower:lower + row_count]).astype(jnp.float32)
        summed = summed + weight[lag_step] * extended[lower:lower + row_count] * live_mask.reshape((row_count,) + shape_tail)
    return kept(jax.nn.silu(summed).astype(jnp.bfloat16))

def rows_to_blocks(array_rows):
    return array_rows.reshape((array_rows.shape[0] // STRETCH, STRETCH) + array_rows.shape[1:])

def steps_to_blocks(steps_dt):
    shape_now = steps_dt.shape
    reshaped = steps_dt.reshape(shape_now[0], shape_now[1], shape_now[2] // STRETCH, STRETCH)
    return jnp.transpose(reshaped, (2, 0, 1, 3))

def from_before(block_c, prior_state, running, resets_seen):
    from_start = jnp.where(resets_seen == 0.0, jnp.exp(running), 0.0)
    state_half = kept(prior_state.astype(jnp.bfloat16))
    carried = jnp.einsum('tgn,ghpn->tghp', block_c.astype(jnp.float32), state_half.astype(jnp.float32))
    return carried * jnp.transpose(from_start, (2, 0, 1))[..., None]

def keep_factor(running, resets_seen):
    return jnp.where(resets_seen[-1] == 0.0, jnp.exp(running[..., -1]), 0.0)

def block_end(block_x, block_b, block_dt, running, resets_seen):
    to_end = jnp.where(resets_seen == resets_seen[-1], jnp.exp(running[..., -1:] - running), 0.0)
    scaled = kept((block_x.astype(jnp.float32) * jnp.transpose(block_dt * to_end, (2, 0, 1))[..., None]).astype(jnp.bfloat16))
    return jnp.einsum('sghp,sgn->ghpn', scaled.astype(jnp.float32), block_b.astype(jnp.float32))

def block_terms(prior_state, block_piece, decay_rate):
    block_x, block_b, block_c, block_dt, block_flags = block_piece
    running = jnp.cumsum(-decay_rate[:, :, None] * block_dt, axis=-1)
    resets_seen = jnp.cumsum(block_flags)
    position = jnp.arange(block_flags.shape[0])
    same_doc = (resets_seen[:, None] == resets_seen[None, :]) & (position[:, None] >= position[None, :])
    spread = running[..., :, None] - running[..., None, :]
    segment = jnp.where(same_doc, jnp.exp(jnp.where(same_doc, spread, 0.0)), 0.0)
    scores = jnp.einsum('tgn,sgn->gts', block_c.astype(jnp.float32), block_b.astype(jnp.float32))
    weights = kept((scores[:, None] * segment * block_dt[:, :, None, :]).astype(jnp.bfloat16))
    within = jnp.einsum('ghts,sghp->tghp', weights.astype(jnp.float32), block_x.astype(jnp.float32))
    carried = from_before(block_c, prior_state, running, resets_seen)
    fresh_state = block_end(block_x, block_b, block_dt, running, resets_seen)
    next_state = keep_factor(running, resets_seen)[..., None, None] * prior_state + fresh_state
    return (next_state, within + carried)

def scan_blocks(inputs, b_rows, c_rows, steps_dt, decay_rate, reset_flags, state_in):
    row_count = inputs.shape[0]
    pieces = (rows_to_blocks(inputs), rows_to_blocks(b_rows), rows_to_blocks(c_rows), steps_to_blocks(steps_dt), rows_to_blocks(reset_flags))
    stepper = jax.checkpoint(functools.partial(block_terms, decay_rate=decay_rate))
    final_state, outputs = lax.scan(stepper, state_in, pieces)
    return (outputs.reshape((row_count,) + inputs.shape[1:]), final_state)

def gate_output(y_ssd, inputs, z_in, skip_weight):
    row_count = inputs.shape[0]
    skip_term = skip_weight.reshape(inputs.shape[1], inputs.shape[2])[None, :, :, None] * inputs.astype(jnp.float32)
    mixed = kept((y_ssd + skip_term).astype(jnp.bfloat16))
    return mixed.astype(jnp.float32).reshape(row_count, -1) * jax.nn.silu(z_in)

def sequence_out(x_in, bc_in, z_in, dt_in, conv_x_weight, conv_x_bias, conv_bc_weight, conv_bc_bias, a_log, dt_bias, skip_weight, norm_gain, reset_flags):
    pad_rows = CONV - 1
    row_count = x_in.shape[0]
    per_group = HEADS // GROUPS
    counts = jnp.cumsum(reset_flags)
    padded_counts = jnp.concatenate([jnp.zeros((pad_rows,), jnp.float32), counts])
    x_ext = jnp.concatenate([jnp.zeros((pad_rows, x_in.shape[1]), jnp.float32), x_in])
    bc_ext = jnp.concatenate([jnp.zeros((pad_rows,) + bc_in.shape[1:], jnp.float32), bc_in])
    inputs = causal_conv(x_ext, padded_counts, conv_x_weight, conv_x_bias).reshape(row_count, GROUPS, per_group, HEAD_DIM)
    bc_conv = causal_conv(bc_ext, padded_counts, conv_bc_weight, conv_bc_bias)
    b_rows = bc_conv[:, 0].reshape(row_count, GROUPS, NSTATE)
    c_rows = bc_conv[:, 1].reshape(row_count, GROUPS, NSTATE)
    steps_dt = jax.nn.softplus(dt_in + dt_bias[:, None]).reshape(GROUPS, per_group, row_count)
    decay_rate = jnp.exp(a_log).reshape(GROUPS, per_group)
    state_zero = jnp.zeros((GROUPS, per_group, HEAD_DIM, NSTATE), jnp.float32)
    y_ssd, final_state = scan_blocks(inputs, b_rows, c_rows, steps_dt, decay_rate, reset_flags, state_zero)
    gated = gate_output(y_ssd, inputs, z_in, skip_weight)
    inv_rms = lax.rsqrt(lax.optimization_barrier(jnp.mean(gated * gated, axis=-1, keepdims=True)) + norm_eps)
    return gated * inv_rms * norm_gain

def reference(x_raw, bc_raw, z_gate, dt_raw, resets, conv_x_weight, conv_x_bias, conv_bc_weight, conv_bc_bias, a_log, dt_bias, skip_weight, norm_gain, grad_out):
    act_grads = ([], [], [], [])
    params = (conv_x_weight, conv_x_bias, conv_bc_weight, conv_bc_bias, a_log, dt_bias, skip_weight, norm_gain)
    param_sums = jax.tree.map(jnp.zeros_like, params)
    for seq_index in range(BATCH):
        forward = functools.partial(sequence_out, reset_flags=resets[seq_index].astype(jnp.float32))
        primals = (x_raw[seq_index].astype(jnp.float32), bc_raw[seq_index].astype(jnp.float32), z_gate[seq_index].astype(jnp.float32), dt_raw[seq_index].astype(jnp.float32)) + params
        normed, pullback = jax.vjp(forward, *primals)
        gradients = pullback(grad_out[seq_index].astype(jnp.float32))
        for slot_index in range(4):
            act_grads[slot_index].append(gradients[slot_index])
        param_sums = jax.tree.map(jnp.add, param_sums, tuple(gradients[4:]))
    grad_scale = float(BATCH * LENGTH) ** (-0.5)
    return (jnp.stack(act_grads[0]).astype(jnp.bfloat16), jnp.stack(act_grads[1]).astype(jnp.bfloat16), jnp.stack(act_grads[2]).astype(jnp.bfloat16), jnp.stack(act_grads[3]), param_sums[0] * grad_scale, param_sums[1] * grad_scale, param_sums[2] * grad_scale, param_sums[3] * grad_scale, param_sums[4] * grad_scale, param_sums[5] * grad_scale, param_sums[6] * grad_scale, param_sums[7] * grad_scale)
```

```python
import functools

import jax
import jax.numpy as jnp
from jax import lax
from jax.experimental import pallas as pl
from jax.experimental.pallas import tpu as pltpu
from jax.sharding import PartitionSpec as P

F32 = jnp.float32
BF16 = jnp.bfloat16
HIGHEST = lax.Precision.HIGHEST
MESH = pl.DeviceIdType.MESH

HEAD_DIM = 64
NSTATE = 128
CONV = 4
INNER = 8192
EPS = 1e-05

T = 256
B = 128
H = 32
D = 2048
DB = 512
NT = D // 128
NG = 2
TPG = NT // NG
ROWS = 16
VM = pl.BlockSpec(memory_space=pltpu.VMEM)
SM = pl.BlockSpec(memory_space=pltpu.SMEM)
VLIM = 60 * 1024 * 1024


def dnn(a, b):
    return lax.dot_general(a, b, (((1,), (0,)), ((), ())), preferred_element_type=F32)


def dnt(a, b):
    return lax.dot_general(a, b, (((1,), (1,)), ((), ())), preferred_element_type=F32)


def dtn(a, b):
    return lax.dot_general(a, b, (((0,), (0,)), ((), ())), preferred_element_type=F32)


def dnn_full(a, b):
    return lax.dot_general(
        a, b, (((1,), (0,)), ((), ())), precision=HIGHEST, preferred_element_type=F32
    )


def dnt_full(a, b):
    return lax.dot_general(
        a, b, (((1,), (1,)), ((), ())), precision=HIGHEST, preferred_element_type=F32
    )


def iota(shape, dim):
    return lax.broadcasted_iota(jnp.int32, shape, dim)


def high_low(v):
    high = v.astype(BF16).astype(F32)
    return high, v - high


def sigmoid(v):
    return 1.0 / (1.0 + jnp.exp(-v))


def softplus(v):
    y = jnp.exp(-jnp.abs(v))
    series = y * (1.0 - y * (0.5 - y * (1.0 / 3.0 - y * (0.25 - 0.2 * y))))
    return jnp.maximum(v, 0.0) + jnp.where(y < 0.02, series, jnp.log(1.0 + y))


def lanes(j):
    return pl.ds(pl.multiple_of(j * 128, 128), 128)


def spread_two(j):
    row = iota((2 * H, 128), 0) % H
    lane = iota((2 * H, 128), 1)
    return (row == 2 * j + lane // HEAD_DIM).astype(BF16)


def spread_pair(j):
    row = iota((128, 256), 0)
    lane = iota((128, 256), 1)
    return ((row % H == 2 * j + lane // 128) & (row < 3 * H)).astype(BF16)


def collect_two(j):
    row = iota((H, 128), 0)
    lane = iota((H, 128), 1)
    return (row == 2 * j + lane // HEAD_DIM).astype(BF16)


def head_sums(j, v):
    high = v.astype(BF16)
    low = (v - high.astype(F32)).astype(BF16)
    e = collect_two(j)
    return dnt(e, high) + dnt(e, low)


def shift_extend(ext, main, halo):
    ext[0:8, :] = halo
    ext[8 : 8 + T, :] = main


def conv_input(ext, live, w, bias):
    u = bias + w[0] * ext[8 : 8 + T, :]
    for k in range(1, CONV):
        u = u + w[k] * ext[8 - k : 8 - k + T, :] * live[k - 1]
    return u


def live_masks(cnt, live):
    now = cnt[8 : 8 + T, :]
    for k in range(1, CONV):
        live[k - 1] = (now == cnt[8 - k : 8 - k + T, :]).astype(F32)


def block_mask(rt, q, c):
    qc = rt[c * B : (c + 1) * B, H : H + 1]
    qr = q[0:1, c * B : (c + 1) * B]
    ok = (qc == qr) & (iota((B, B), 0) >= iota((B, B), 1))
    return jnp.where(ok, 0.0, -1e30)


def row_state(ref, j, n, lead):
    ncq = n // 8
    tpc = NT // ncq
    cq = j // tpc
    lane = lanes(j % tpc)
    return jnp.concatenate([ref[rz * ncq + cq, :, lane] for rz in range(8)], axis=0)


def put_state(ref, j, n, v):
    ncq = n // 8
    tpc = NT // ncq
    cq = j // tpc
    lane = lanes(j % tpc)
    for rz in range(8):
        ref[rz * ncq + cq, :, lane] = v[rz * ROWS : (rz + 1) * ROWS]


def k1_body(
    n, x, bc, halo, dtr, flg, hp, cxw, cxb, cbw, cbb,
    xc_o, bcc_o, dt_o, r_o, mt_o, rt_o, rs_o, q_o, st_o, kr_o, fr_o,
    ext, cnt, live,
):
    rate = jnp.exp(hp[:, 0:1])
    bias = hp[:, 1:2]
    tri = (iota((B, B), 0) <= iota((B, B), 1)).astype(F32)
    before = jnp.zeros((8, 1), F32)
    cnt[0:8, :] = jnp.zeros((8, 128), F32)
    for c in range(2):
        sl = slice(c * B, (c + 1) * B)
        dtv = softplus(dtr[:, sl].astype(F32) + bias)
        r = dnn_full(-rate * dtv, tri)
        q = dnn(jnp.broadcast_to(flg[:, sl].astype(F32), (8, B)), tri)
        rl = r[:, B - 1 : B]
        ql = q[:, B - 1 : B]
        dtte = dtv * jnp.where(q[0:1] == ql[0:1], jnp.exp(rl - r), 0.0)
        fs = jnp.where(q[0:1] == 0.0, jnp.exp(r), 0.0)
        dt_o[c] = dtv
        r_o[c] = r
        q_o[:, sl] = q
        a1, a2 = high_low(dtte)
        b1, b2 = high_low(fs)
        mt_o[sl, :] = jnp.concatenate([a1, a2, b1, b2], axis=0).T.astype(BF16)
        dev = q + before
        before = dev[:, B - 1 : B]
        rt = jnp.concatenate([r, q, dev, jnp.zeros((80, B), F32)], axis=0).T
        rt_o[sl, :] = rt
        r1, r2 = high_low(r)
        r2, r3 = high_low(r2)
        rs_o[sl, :] = jnp.concatenate([r1, r2, r3, jnp.zeros((H, B), F32)], axis=0).T.astype(BF16)
        cnt[8 + c * B : 8 + (c + 1) * B, :] = jnp.broadcast_to(rt[:, H + 8 : H + 9], (B, 128))
    live_masks(cnt, live)

    for j in range(4):
        sl = slice(j * 128, (j + 1) * 128)
        shift_extend(ext, bc[:, sl].astype(F32), halo[:, D + j * 128 : D + (j + 1) * 128].astype(F32))
        u = conv_input(ext, live, [cbw[k : k + 1, sl] for k in range(CONV)], cbb[0:1, sl])
        bcc_o[:, sl] = (u * sigmoid(u)).astype(BF16)

    for g in range(NG):
        bt = [
            bcc_o[c * B : (c + 1) * B, g * 128 : (g + 1) * 128].astype(F32).T.astype(BF16)
            for c in range(2)
        ]

        def tile(jj, carry, g=g, bt=bt):
            j = g * TPG + jj
            sl = lanes(j)
            shift_extend(ext, x[:, sl].astype(F32), halo[:, sl].astype(F32))
            u = conv_input(ext, live, [cxw[k : k + 1, sl] for k in range(CONV)], cxb[0:1, sl])
            xc = (u * sigmoid(u)).astype(BF16)
            xc_o[:, sl] = xc
            e2 = spread_two(j)
            dtte = dnn(mt_o[:, 0 : 2 * H], e2)
            uu = (xc.astype(F32) * dtte).astype(BF16)
            k0 = dnn(mt_o[B - 16 : B, 2 * H : 4 * H], e2)[15:16]
            k1 = dnn(mt_o[T - 16 : T, 2 * H : 4 * H], e2)[15:16]
            fresh0 = dnn(bt[0], uu[0:B])
            fresh1 = dnn(bt[1], uu[B:T])
            fr_o[:, sl] = fresh0
            put_state(st_o, j, n, (k1 * fresh0 + fresh1).astype(BF16))
            ncq = n // 8
            tpc = NT // ncq
            kr_o[j // tpc, :, lanes(j % tpc)] = k0 * k1
            return carry

        lax.fori_loop(0, TPG, tile, 0)


def scan_body(n, first, *refs):
    if first:
        st, kr, out, kall, rb, pb, ob, kb, s1, r1, s2, r2, sk, rk = refs
    else:
        st, kall, out, rb, pb, ob, s1, r1, s2, r2 = refs
    ncq = n // 8
    me = lax.axis_index("ctx")
    barrier = pltpu.get_barrier_semaphore()

    def greet(k, carry):
        pl.semaphore_signal(
            barrier, inc=1, device_id={"ctx": lax.rem(me + k, n)}, device_id_type=MESH
        )
        return carry

    lax.fori_loop(1, n, greet, 0)
    rb[me] = st[me]
    if first:
        kb[me] = kr[lax.rem(me, ncq)]
    pl.semaphore_wait(barrier, n - 1)

    def state_copy(src, dst_slot, dev, sem_s, sem_r):
        return pltpu.make_async_remote_copy(
            src_ref=src, dst_ref=dst_slot, send_sem=sem_s, recv_sem=sem_r,
            device_id={"ctx": dev}, device_id_type=MESH,
        )

    def send(k, carry):
        to = lax.rem(me + k, n)
        state_copy(st.at[to], rb.at[me], to, s1.at[to], r1.at[me]).start()
        if first:
            state_copy(kr.at[lax.rem(to, ncq)], kb.at[me], to, sk.at[to], rk.at[me]).start()
        return carry

    lax.fori_loop(1, n, send, 0)

    def step(i, acc):
        d = i if first else n - 1 - i

        @pl.when(d != me)
        def _():
            state_copy(st.at[d], rb.at[d], d, s1.at[d], r1.at[d]).wait_recv()
            if first:
                state_copy(kr.at[0], kb.at[d], d, sk.at[d], rk.at[d]).wait_recv()

        pb[d] = acc.astype(BF16)

        @pl.when(d != me)
        def _():
            state_copy(pb.at[d], ob.at[me], d, s2.at[d], r2.at[me]).start()

        decay = kb[d] if first else kall[d]
        return decay * acc + rb[d].astype(F32)

    lax.fori_loop(0, n, step, jnp.zeros(rb.shape[1:], F32))
    ob[me] = pb[me]

    def finish(k, carry):
        d = lax.rem(me + k, n)
        state_copy(st.at[d], rb.at[d], d, s1.at[d], r1.at[d]).wait_send()
        if first:
            state_copy(kr.at[0], kb.at[d], d, sk.at[d], rk.at[d]).wait_send()
        state_copy(pb.at[d], ob.at[d], d, s2.at[d], r2.at[d]).wait()
        return carry

    lax.fori_loop(1, n, finish, 0)
    out[...] = ob[...]
    if first:
        kall[...] = kb[...]


def k2_body(
    n, xc, bcc, dt, r, rt, rs, mt, q, sin, fr, z, g_in, gain, skip,
    y_o, mixed_o, sums_o, sb1_o, acc,
):
    acc[...] = jnp.zeros_like(acc)
    half = iota((B, 128), 1) < HEAD_DIM
    for g in range(NG):
        for c in range(2):
            sl = slice(c * B, (c + 1) * B)
            mask = block_mask(rt, q, c)
            bb = bcc[sl, g * 128 : (g + 1) * 128]
            cc = bcc[sl, 256 + g * 128 : 256 + (g + 1) * 128]
            gm = dnt(cc, bb)

            def tile(jj, carry, g=g, c=c, sl=sl, mask=mask, cc=cc, gm=gm):
                j = g * TPG + jj
                ln = lanes(j)
                e2 = spread_two(j)
                rb2 = dnn(rs[sl, :], spread_pair(j))
                ws = []
                for i in range(2):
                    h = 2 * j + i
                    lm = jnp.exp(rb2[:, i * B : (i + 1) * B] - r[c, pl.ds(h, 1), :] + mask)
                    ws.append((gm * lm * dt[c, pl.ds(h, 1), :]).astype(BF16))
                xt = xc[sl, ln]
                zero = jnp.zeros_like(xt)
                xbd = jnp.concatenate([jnp.where(half, xt, zero), jnp.where(half, zero, xt)], axis=0)
                within = dnn(jnp.concatenate(ws, axis=1), xbd)
                sb = row_state(sin, j, n, 0)
                if c == 1:
                    k0 = dnn(mt[B - 16 : B, 2 * H : 4 * H], e2)[15:16]
                    sb = (k0 * sb.astype(F32) + fr[:, ln]).astype(BF16)
                    sb1_o[:, ln] = sb
                fs = dnn(mt[sl, 2 * H : 4 * H], e2)
                y = within + dnn(cc, sb) * fs
                y_o[sl, ln] = y
                lane = iota((1, 128), 1)
                sk = jnp.where(lane < HEAD_DIM, skip[2 * j], skip[2 * j + 1])
                mixed = (y + sk * xt.astype(F32)).astype(BF16)
                mixed_o[sl, ln] = mixed
                zf = z[sl, ln].astype(F32)
                gated = mixed.astype(F32) * (zf * sigmoid(zf))
                gained = g_in[sl, ln].astype(F32) * gain[0:1, ln]
                acc[0, sl, :] += gated * gated
                acc[1, sl, :] += gated * gained
                return carry

            lax.fori_loop(0, TPG, tile, 0)
    ones = jnp.ones((8, 128), F32)
    sums_o[0:8, :] = dnt_full(ones, acc[0])
    sums_o[8:16, :] = dnt_full(ones, acc[1])


def norm_body(n, s_in, out, buf, ss, rr):
    me = lax.axis_index("head")
    barrier = pltpu.get_barrier_semaphore()
    for k in range(1, n):
        pl.semaphore_signal(
            barrier, inc=1, device_id={"head": lax.rem(me + k, n)}, device_id_type=MESH
        )
    pl.semaphore_wait(barrier, n - 1)
    copies = []
    for k in range(1, n):
        copies.append(
            pltpu.make_async_remote_copy(
                src_ref=s_in, dst_ref=buf.at[k], send_sem=ss.at[k], recv_sem=rr.at[k],
                device_id={"head": lax.rem(me + k, n)}, device_id_type=MESH,
            )
        )
        copies[-1].start()
    for cp in copies:
        cp.wait()
    parts = [s_in[...]] + [buf[k] for k in range(1, n)]
    total = jnp.zeros_like(parts[0])
    for d in range(n):
        for k in range(n):
            total = total + jnp.where(lax.rem(me - k + n, n) == d, parts[k], 0.0)
    out[...] = total


def k3_body(
    n, sums, mixed, z, g_in, gain, y, xc, mt, bcc,
    dz_o, dy_o, rho_o, drow_o, ad_o, dsb1_o, inv_s, coef_s,
):
    ss = sums[0:8, :]
    sg = sums[8:16, :]
    inv = lax.rsqrt(ss / INNER + EPS)
    coef = inv * inv * inv * sg / INNER
    for c in range(2):
        sl = slice(c * B, (c + 1) * B)
        tr = jnp.concatenate([inv[:, sl], coef[:, sl], jnp.zeros((112, B), F32)], axis=0).T
        inv_s[sl, :] = jnp.broadcast_to(tr[:, 0:1], (B, 128))
        coef_s[sl, :] = jnp.broadcast_to(tr[:, 8:9], (B, 128))
    rho_o[...] = jnp.zeros_like(rho_o)
    drow_o[...] = jnp.zeros_like(drow_o)
    for g in range(NG):
        ct = [
            bcc[c * B : (c + 1) * B, 256 + g * 128 : 256 + (g + 1) * 128].astype(F32).T.astype(BF16)
            for c in range(2)
        ]

        def tile(jj, carry, g=g, ct=ct):
            j = g * TPG + jj
            ln = lanes(j)
            e2 = spread_two(j)
            m = mixed[:, ln].astype(F32)
            zf = z[:, ln].astype(F32)
            go = g_in[:, ln].astype(F32)
            sig = sigmoid(zf)
            sl = zf * sig
            gated = m * sl
            iv = inv_s[...]
            dg = go * gain[0:1, ln] * iv - gated * coef_s[...]
            drow_o[0:1, ln] = jnp.sum(go * gated * iv, axis=0, keepdims=True)
            dz_o[:, ln] = (dg * m * (sig * (1.0 + zf * (1.0 - sig)))).astype(BF16)
            dm = (dg * sl).astype(BF16)
            dy_o[:, ln] = dm
            dy = dm.astype(F32)
            drow_o[1:2, ln] = jnp.sum(dy * xc[:, ln].astype(F32), axis=0, keepdims=True)
            rho_o[...] += head_sums(j, dy * y[:, ln])
            fs = dnn(mt[:, 2 * H : 4 * H], e2)
            fd = (fs * dy).astype(BF16)
            d0 = dnn(ct[0], fd[0:B]).astype(BF16)
            d1 = dnn(ct[1], fd[B:T]).astype(BF16)
            dsb1_o[:, ln] = d1
            put_state(ad_o, j, n, (fs[B - 1 : B] * d1.astype(F32) + d0.astype(F32)).astype(BF16))
            return carry

        lax.fori_loop(0, TPG, tile, 0)


def conv_backward(ext, vk, live, w, bias, dxc):
    u = conv_input(ext, live, w, bias)
    s = sigmoid(u)
    du = dxc.astype(BF16).astype(F32) * (s * (1.0 + u * (1.0 - s)))
    rows = [jnp.sum(du * ext[8 : 8 + T, :], axis=0, keepdims=True)]
    vk[0, 8 : 8 + T, :] = du
    for k in range(1, CONV):
        v = du * live[k - 1]
        rows.append(jnp.sum(v * ext[8 - k : 8 - k + T, :], axis=0, keepdims=True))
        vk[k, 8 : 8 + T, :] = v
    rows.append(jnp.sum(du, axis=0, keepdims=True))
    own = w[0] * du
    before = jnp.zeros((8, 128), F32)
    for k in range(1, CONV):
        own = own + w[k] * vk[k, 8 + k : 8 + k + T, :]
        before = before + w[k] * vk[k, k : k + 8, :]
    return own, before, rows


def k4_body(
    n, x, bc, halo, dtr, hp, cxw, cxb, cbw, cbb, xc, bcc, dt, r, rt, rs, mt, q, dy, rho, dsb1,
    sin, sb1, later, drow, skip,
    gx_o, gbc_o, gdt_o, tail_o, hb_o, pk_o, ph_o,
    ext, cnt, live, vk, acc, kap, tl, dbc,
):
    half = iota((B, 128), 1) < HEAD_DIM
    cnt[0:8, :] = jnp.zeros((8, 128), F32)
    cnt[8 : 8 + T, :] = jnp.broadcast_to(rt[:, H + 8 : H + 9], (T, 128))
    live_masks(cnt, live)
    vk[:, 0:8, :] = jnp.zeros((CONV, 8, 128), F32)
    vk[:, 8 + T :, :] = jnp.zeros((CONV, 8, 128), F32)
    kap[...] = jnp.zeros_like(kap)
    tl[...] = jnp.zeros_like(tl)
    masks = [block_mask(rt, q, c) for c in range(2)]
    for g in range(NG):
        acc[...] = jnp.zeros_like(acc)
        bbs = [bcc[c * B : (c + 1) * B, g * 128 : (g + 1) * 128] for c in range(2)]
        ccs = [bcc[c * B : (c + 1) * B, 256 + g * 128 : 256 + (g + 1) * 128] for c in range(2)]
        gms = [dnt(ccs[c], bbs[c]) for c in range(2)]

        def tile(jj, carry, g=g, bbs=bbs, ccs=ccs, gms=gms):
            j = g * TPG + jj
            ln = lanes(j)
            e2 = spread_two(j)
            dtte = dnn(mt[:, 0 : 2 * H], e2)
            fs = dnn(mt[:, 2 * H : 4 * H], e2)
            a1 = row_state(later, j, n, 0).astype(F32)
            s0 = row_state(sin, j, n, 0)
            lane = iota((1, 128), 1)
            sk = jnp.where(lane < HEAD_DIM, skip[2 * j], skip[2 * j + 1])
            parts = []
            for c in range(2):
                sl = slice(c * B, (c + 1) * B)
                rb2 = dnn(rs[sl, :], spread_pair(j))
                ls = []
                for i in range(2):
                    h = 2 * j + i
                    lm = jnp.exp(rb2[:, i * B : (i + 1) * B] - r[c, pl.ds(h, 1), :] + masks[c])
                    ls.append(lm * dt[c, pl.ds(h, 1), :])
                xt = xc[sl, ln]
                dyt = dy[sl, ln]
                zero = jnp.zeros_like(dyt)
                dybd = jnp.concatenate(
                    [jnp.where(half, dyt, zero), jnp.where(half, zero, dyt)], axis=0
                )
                dw = dnt(dybd, xt)
                acc[0, c] += dw[0:B] * ls[0] + dw[B : 2 * B] * ls[1]
                wst = jnp.concatenate([(gms[c] * lv).astype(BF16) for lv in ls], axis=0)
                dxw = dtn(wst, dybd)
                if c == 1:
                    ds = a1
                    sp = sb1[:, ln]
                    kk = fs[T - 1 : T]
                else:
                    ds = fs[T - 1 : T] * a1 + dsb1[:, ln].astype(F32)
                    sp = s0
                    kk = fs[B - 1 : B]
                dsh = ds.astype(BF16)
                xf = xt.astype(F32)
                dyf = dyt.astype(F32)
                dtc = dtte[sl]
                dxu = dnn(bbs[c], dsh) * dtc
                uu = (xf * dtc).astype(BF16)
                fd = (fs[sl] * dyf).astype(BF16)
                acc[1, c] += dnt(uu, dsh)
                acc[2, c] += dnt(fd, sp)
                ku = jnp.sum(xf * dxu, axis=0, keepdims=True)
                kd = jnp.sum(ds * sp.astype(F32), axis=0, keepdims=True) * kk
                both = jnp.concatenate(
                    [xf * (dxw + dxu), jnp.broadcast_to(ku + kd, (8, 128))], axis=0
                )
                hs = head_sums(j, both)
                kap[:, sl] += hs[:, 0:B]
                tl[:, c * 8 : (c + 1) * 8] += hs[:, B : B + 8]
                parts.append(dxw + dxu + sk * dyf)
            dxc = jnp.concatenate(parts, axis=0)
            shift_extend(ext, x[:, ln].astype(F32), halo[:, ln].astype(F32))
            own, before, rows = conv_backward(
                ext, vk, live, [cxw[k : k + 1, ln] for k in range(CONV)], cxb[0:1, ln], dxc
            )
            gx_o[:, ln] = own.astype(BF16)
            tail_o[:, ln] = own[T - 16 : T]
            hb_o[:, ln] = before
            for k in range(CONV + 1):
                pk_o[k : k + 1, ln] = rows[k]
            return carry

        lax.fori_loop(0, TPG, tile, 0)
        for c in range(2):
            sl = slice(c * B, (c + 1) * B)
            dg = acc[0, c].astype(BF16)
            dbc[sl, g * 128 : (g + 1) * 128] = acc[1, c] + dtn(dg, ccs[c])
            dbc[sl, 256 + g * 128 : 256 + (g + 1) * 128] = acc[2, c] + dnn(dg, bbs[c])

    for j in range(4):
        sl = slice(j * 128, (j + 1) * 128)
        sd = slice(D + j * 128, D + (j + 1) * 128)
        shift_extend(ext, bc[:, sl].astype(F32), halo[:, sd].astype(F32))
        own, before, rows = conv_backward(
            ext, vk, live, [cbw[k : k + 1, sl] for k in range(CONV)], cbb[0:1, sl], dbc[:, sl]
        )
        gbc_o[:, sl] = own.astype(BF16)
        tail_o[:, sd] = own[T - 16 : T]
        hb_o[:, sd] = before
        for k in range(CONV + 1):
            pk_o[k : k + 1, sd] = rows[k]
    pk_o[5:7, 0:D] = drow[0:2, :]
    pk_o[5:8, D:] = jnp.zeros((3, DB), F32)
    pk_o[7:8, 0:D] = jnp.zeros((1, D), F32)

    rate = jnp.exp(hp[:, 0:1])
    bias = hp[:, 1:2]
    rev = (iota((B, B), 0) >= iota((B, B), 1)).astype(F32)
    rate_sum = jnp.zeros((H, B), F32)
    bias_sum = jnp.zeros((H, B), F32)
    for c in range(2):
        sl = slice(c * B, (c + 1) * B)
        dtv = dt[c]
        kp = kap[:, sl]
        rr = dnn_full(rho[:, sl] - kp, rev) + tl[:, c * 8 : c * 8 + 1]
        ddt = kp / dtv - rate * rr
        gd = ddt * sigmoid(dtr[:, sl].astype(F32) + bias)
        gdt_o[:, sl] = gd
        rate_sum = rate_sum - rate * dtv * rr
        bias_sum = bias_sum + gd
    ones = jnp.ones((8, B), F32)
    zer = jnp.zeros((96, B), F32)
    ph_o[...] = dnt_full(ones, jnp.concatenate([rate_sum, bias_sum, zer[:64]], axis=0))


def param_body(n, pk, ph, hb, red_o, rh_o, own, got, rb, sb, ob, hbuf,
               sd, rd, s1, r1, s2, r2, sh, rh):
    nt = got.shape[0]
    me = lax.axis_index("ctx")
    dp = lax.axis_index("dp")
    ndp = lax.axis_size("dp")
    hbuf[...] = jnp.zeros_like(hbuf)
    barrier = pltpu.get_barrier_semaphore()

    def greet(k, carry):
        pl.semaphore_signal(
            barrier, inc=1, device_id={"ctx": lax.rem(me + k, n)}, device_id_type=MESH
        )
        return carry

    lax.fori_loop(1, n, greet, 0)
    if ndp == 2:
        pl.semaphore_signal(barrier, inc=1, device_id={"dp": 1 - dp}, device_id_type=MESH)
    for j in range(nt - 1):
        own[j] = pk[:, j * 128 : (j + 1) * 128]
    own[nt - 1] = ph[...]
    pl.semaphore_wait(barrier, n - 1 + (ndp - 1))

    def rcopy(src, dst, sem_s, sem_r, dev):
        return pltpu.make_async_remote_copy(
            src_ref=src, dst_ref=dst, send_sem=sem_s, recv_sem=sem_r,
            device_id=dev, device_id_type=MESH,
        )

    back = rcopy(hb, hbuf, sh, rh, {"ctx": lax.rem(me + n - 1, n)})

    @pl.when(me > 0)
    def _():
        back.start()

    if ndp == 2:
        swap = rcopy(own, got, sd, rd, {"dp": 1 - dp})
        swap.start()
        swap.wait()
        sb[...] = own[...] + got[...]
    else:
        sb[...] = own[...]

    def send(k, carry):
        to = lax.rem(me + k, n)

        @pl.when(to < nt)
        def _():
            rcopy(sb.at[to], rb.at[me], s1.at[to], r1.at[me], {"ctx": to}).start()

        return carry

    lax.fori_loop(1, n, send, 0)

    @pl.when(me < nt)
    def _():
        rb[me] = sb[me]

        def collect(d, total):
            @pl.when(d != me)
            def _():
                rcopy(sb.at[0], rb.at[d], s1.at[0], r1.at[d], {"ctx": d}).wait_recv()

            return total + rb[d]

        ob[me] = lax.fori_loop(0, n, collect, jnp.zeros((8, 128), F32))

        def give(k, carry):
            to = lax.rem(me + k, n)
            rcopy(ob.at[me], ob.at[me], s2.at[to], r2.at[me], {"ctx": to}).start()
            return carry

        lax.fori_loop(1, n, give, 0)

    def finish(k, carry):
        d = lax.rem(me + k, n)

        @pl.when(d < nt)
        def _():
            rcopy(sb.at[d], rb.at[0], s1.at[d], r1.at[0], {"ctx": d}).wait_send()
            rcopy(ob.at[0], ob.at[d], s2.at[d], r2.at[d], {"ctx": d}).wait_recv()

        @pl.when(me < nt)
        def _():
            rcopy(ob.at[0], ob.at[0], s2.at[d], r2.at[0], {"ctx": d}).wait_send()

        return carry

    lax.fori_loop(1, n, finish, 0)

    @pl.when(me > 0)
    def _():
        back.wait_send()

    @pl.when(me < n - 1)
    def _():
        back.wait_recv()

    rh_o[...] = hbuf[...]
    red_o[...] = ob[...]


def k5_body(scale, red, rh, tail, flg, gx_in, gbc_in,
            gx_o, gbc_o, cw_o, cb_o, bw_o, bb_o, al_o, db_o, sk_o, ga_o):
    f = flg[:, B:T].astype(F32)
    lane = iota((1, B), 1)
    last = jnp.sum(jnp.where(lane == B - 1, f, 0.0))
    two = jnp.sum(jnp.where(lane >= B - 2, f, 0.0))
    row = iota((16, 128), 0)
    keep = jnp.where(row == 15, 1.0, 0.0)
    keep = keep + jnp.where((row == 14) & (last == 0.0), 1.0, 0.0)
    keep = keep + jnp.where((row == 13) & (two == 0.0), 1.0, 0.0)
    for j in range(NT + 4):
        sl = slice(j * 128, (j + 1) * 128)
        add = jnp.concatenate([jnp.zeros((8, 128), F32), rh[:, sl]], axis=0)
        v = (tail[:, sl] + add * keep).astype(BF16)
        t = red[j] * scale
        if j < NT:
            gx_o[:, sl] = v
            cw_o[:, sl] = t[0:4]
            cb_o[:, sl] = t[4:5]
            ga_o[:, sl] = t[5:6]
            hs = dnt_full(t[0:8], collect_two(j).astype(F32))
            if j == 0:
                skip = hs
            else:
                skip = skip + hs
        else:
            so = slice(j * 128 - D, (j + 1) * 128 - D)
            gbc_o[:, so] = v
            bw_o[:, so] = t[0:4]
            bb_o[:, so] = t[4:5]
    sk_o[...] = skip[6:7]
    last_tile = red[NT + 4] * scale
    al_o[...] = last_tile[0:1, 0:H]
    db_o[...] = last_tile[0:1, H : 2 * H]


def sds(*shape, dtype=F32):
    return jax.ShapeDtypeStruct(shape, dtype)


def call(body, outs, ins, scratch=(), specs=None, out_specs=None, cid=None, **kw):
    extra = {} if cid is None else {"collective_id": cid, "has_side_effects": True}
    return pl.pallas_call(
        body,
        out_shape=outs,
        in_specs=specs or [VM] * len(ins),
        out_specs=out_specs or [VM] * len(outs),
        scratch_shapes=list(scratch),
        compiler_params=pltpu.CompilerParams(vmem_limit_bytes=VLIM, **extra),
        **kw,
    )(*ins)


def per_device(
    x_raw, bc_raw, z_gate, dt_raw, resets, conv_x_weight, conv_x_bias, conv_bc_weight,
    conv_bc_bias, a_log, dt_bias, skip_weight, norm_gain, grad_out,
):
    n = lax.axis_size("ctx")
    nh = lax.axis_size("head")
    ndp = lax.axis_size("dp")
    ncq = n // 8
    w = D // ncq
    x = x_raw[0]
    bc = bc_raw[0].reshape(T, DB)
    z = z_gate[0]
    go = grad_out[0]
    dtr = dt_raw[0]
    gain = norm_gain.reshape(1, D)
    cxb = conv_x_bias.reshape(1, D)
    cbw = conv_bc_weight.reshape(CONV, DB)
    cbb = conv_bc_bias.reshape(1, DB)
    hp = jnp.stack([a_log, dt_bias], axis=1)

    f = resets[0, T - 8 :]
    keep = jnp.concatenate([jnp.cumsum(f[::-1])[::-1][1:] == 0, jnp.ones((1,), bool)])
    tail = jnp.concatenate([x[T - 8 :], bc[T - 8 :]], axis=1)
    tail = jnp.where(keep[:, None], tail, jnp.zeros_like(tail))
    halo = lax.ppermute(tail, "ctx", [(i, i + 1) for i in range(n - 1)])

    conv_scratch = [
        pltpu.VMEM((T + 8, 128), F32),
        pltpu.VMEM((T + 8, 128), F32),
        pltpu.VMEM((CONV - 1, T, 128), F32),
    ]
    xc, bcc, dt, r, mt, rt, rs, q, st, kr, fr = call(
        functools.partial(k1_body, n),
        (
            sds(T, D, dtype=BF16), sds(T, DB, dtype=BF16), sds(2, H, B), sds(2, H, B),
            sds(T, 128, dtype=BF16), sds(T, 128), sds(T, 128, dtype=BF16), sds(8, T),
            sds(n, ROWS, w, dtype=BF16), sds(ncq, 1, w), sds(NSTATE, D),
        ),
        (x, bc, halo, dtr, resets, hp, conv_x_weight, cxb, cbw, cbb),
        conv_scratch,
    )
    state = pltpu.VMEM((n, ROWS, w), BF16)
    dma = pltpu.SemaphoreType.DMA((n,))
    sin, kall = call(
        functools.partial(scan_body, n, True),
        (sds(n, ROWS, w, dtype=BF16), sds(n, 1, w)),
        (st, kr),
        [state, state, state, pltpu.VMEM((n, 1, w), F32)] + [dma] * 6,
        cid=0,
    )
    y, mixed, sums, sb1 = call(
        functools.partial(k2_body, n),
        (sds(T, D), sds(T, D, dtype=BF16), sds(16, T), sds(NSTATE, D, dtype=BF16)),
        (xc, bcc, dt, r, rt, rs, mt, q, sin, fr, z, go, gain, skip_weight),
        [pltpu.VMEM((2, T, 128), F32)],
        specs=[VM] * 13 + [SM],
    )
    if nh > 1:
        (sums,) = call(
            functools.partial(norm_body, nh),
            (sds(16, T),),
            (sums,),
            [pltpu.VMEM((nh, 16, T), F32)] + [pltpu.SemaphoreType.DMA((nh,))] * 2,
            cid=1,
        )
    dz, dy, rho, drow, ad, dsb1 = call(
        functools.partial(k3_body, n),
        (
            sds(T, D, dtype=BF16), sds(T, D, dtype=BF16), sds(H, T), sds(8, D),
            sds(n, ROWS, w, dtype=BF16), sds(NSTATE, D, dtype=BF16),
        ),
        (sums, mixed, z, go, gain, y, xc, mt, bcc),
        [pltpu.VMEM((T, 128), F32)] * 2,
    )
    (later,) = call(
        functools.partial(scan_body, n, False),
        (sds(n, ROWS, w, dtype=BF16),),
        (ad, kall),
        [state, state, state] + [dma] * 4,
        cid=2,
    )
    gx, gbc, gdt, tails, hb, pk, ph = call(
        functools.partial(k4_body, n),
        (
            sds(T, D, dtype=BF16), sds(T, DB, dtype=BF16), sds(H, T), sds(16, D + DB),
            sds(8, D + DB), sds(8, D + DB), sds(8, 128),
        ),
        (
            x, bc, halo, dtr, hp, conv_x_weight, cxb, cbw, cbb, xc, bcc, dt, r, rt, rs, mt, q,
            dy, rho, dsb1, sin, sb1, later, drow, skip_weight,
        ),
        conv_scratch
        + [
            pltpu.VMEM((CONV, T + 16, 128), F32),
            pltpu.VMEM((3, 2, B, 128), F32),
            pltpu.VMEM((H, T), F32),
            pltpu.VMEM((H, 16), F32),
            pltpu.VMEM((T, DB), F32),
        ],
        specs=[VM] * 24 + [SM],
    )
    nt = NT + 5
    owners = pltpu.SemaphoreType.DMA((max(n, nt),))
    one = pltpu.SemaphoreType.DMA
    tiles = pltpu.VMEM((nt, 8, 128), F32)
    red, rh = call(
        functools.partial(param_body, n),
        (sds(nt, 8, 128), sds(8, D + DB)),
        (pk, ph, hb),
        [tiles, tiles, pltpu.VMEM((n, 8, 128), F32), tiles, tiles, pltpu.VMEM((8, D + DB), F32)]
        + [one, one] + [owners] * 4 + [one, one],
        cid=3,
    )
    scale = float(ndp * n * T) ** (-0.5)
    whole = lambda *s: pl.BlockSpec(s, lambda i: (0,) * len(s))
    outs = pl.pallas_call(
        functools.partial(k5_body, scale),
        grid=(1,),
        out_shape=(
            sds(T, D, dtype=BF16), sds(T, DB, dtype=BF16), sds(CONV, D), sds(1, D), sds(CONV, DB),
            sds(1, DB), sds(1, H), sds(1, H), sds(1, H), sds(1, D),
        ),
        in_specs=[
            whole(nt, 8, 128), whole(8, D + DB), whole(16, D + DB), whole(1, T),
            pl.BlockSpec(memory_space=pl.ANY), pl.BlockSpec(memory_space=pl.ANY),
        ],
        out_specs=[
            pl.BlockSpec((16, D), lambda i: (T // 16 - 1, 0)),
            pl.BlockSpec((16, DB), lambda i: (T // 16 - 1, 0)),
            whole(CONV, D), whole(1, D), whole(CONV, DB), whole(1, DB), whole(1, H), whole(1, H),
            whole(1, H), whole(1, D),
        ],
        input_output_aliases={4: 0, 5: 1},
    )(red, rh, tails, resets, gx, gbc)
    gx, gbc, cw, cb, bw, bb, al, db, sk, ga = outs
    return (
        gx[None], gbc.reshape(1, T, 2, DB // 2), dz[None], gdt[None], cw, cb.reshape(D),
        bw.reshape(CONV, 2, DB // 2), bb.reshape(2, DB // 2), al.reshape(H), db.reshape(H),
        sk.reshape(H), ga.reshape(D),
    )


def solution(mesh):
    return jax.shard_map(
        per_device,
        mesh=mesh,
        in_specs=(
            P("dp", "ctx", "head"),
            P("dp", "ctx", None, "head"),
            P("dp", "ctx", "head"),
            P("dp", "head", "ctx"),
            P("dp", "ctx"),
            P(None, "head"),
            P("head"),
            P(None, None, "head"),
            P(None, "head"),
            P("head"),
            P("head"),
            P("head"),
            P("head"),
            P("dp", "ctx", "head"),
        ),
        out_specs=(
            P("dp", "ctx", "head"),
            P("dp", "ctx", None, "head"),
            P("dp", "ctx", "head"),
            P("dp", "head", "ctx"),
            P(None, "head"),
            P("head"),
            P(None, None, "head"),
            P(None, "head"),
            P("head"),
            P("head"),
            P("head"),
            P("head"),
        ),
        check_vma=False,
    )
```

```python
import functools

import types

import jax
import jax.numpy as jnp
from jax import lax
from jax.experimental import pallas as pl
from jax.experimental.pallas import tpu as pltpu
from jax.sharding import PartitionSpec as P

F32 = jnp.float32
BF16 = jnp.bfloat16
HIGHEST = lax.Precision.HIGHEST
MESH = pl.DeviceIdType.MESH

HEAD_DIM = 64
NSTATE = 128
CONV = 4
INNER = 8192
EPS = 1e-05

T = 256
B = 128
H = 32
D = 2048
DB = 512
NT = D // 128
NG = 2
TPG = NT // NG
ROWS = 16
VM = pl.BlockSpec(memory_space=pltpu.VMEM)
SM = pl.BlockSpec(memory_space=pltpu.SMEM)
VLIM = 60 * 1024 * 1024


def dnn(a, b):
    return lax.dot_general(a, b, (((1,), (0,)), ((), ())), preferred_element_type=F32)


def dnt(a, b):
    return lax.dot_general(a, b, (((1,), (1,)), ((), ())), preferred_element_type=F32)


def dtn(a, b):
    return lax.dot_general(a, b, (((0,), (0,)), ((), ())), preferred_element_type=F32)


def dnn_full(a, b):
    return lax.dot_general(
        a, b, (((1,), (0,)), ((), ())), precision=HIGHEST, preferred_element_type=F32
    )


def dnt_full(a, b):
    return lax.dot_general(
        a, b, (((1,), (1,)), ((), ())), precision=HIGHEST, preferred_element_type=F32
    )


def iota(shape, dim):
    return lax.broadcasted_iota(jnp.int32, shape, dim)


def high_low(v):
    high = v.astype(BF16).astype(F32)
    return high, v - high


def sigmoid(v):
    return 1.0 / (1.0 + jnp.exp(-v))


def softplus(v):
    y = jnp.exp(-jnp.abs(v))
    series = y * (1.0 - y * (0.5 - y * (1.0 / 3.0 - y * (0.25 - 0.2 * y))))
    return jnp.maximum(v, 0.0) + jnp.where(y < 0.02, series, jnp.log(1.0 + y))


def lanes(j):
    return pl.ds(pl.multiple_of(j * 128, 128), 128)


def spread_two(j):
    row = iota((2 * H, 128), 0) % H
    lane = iota((2 * H, 128), 1)
    return (row == 2 * j + lane // HEAD_DIM).astype(BF16)


def spread_pair(j):
    row = iota((128, 256), 0)
    lane = iota((128, 256), 1)
    return ((row % H == 2 * j + lane // 128) & (row < 3 * H)).astype(BF16)


def collect_two(j):
    row = iota((H, 128), 0)
    lane = iota((H, 128), 1)
    return (row == 2 * j + lane // HEAD_DIM).astype(BF16)


def head_sums(j, v):
    high = v.astype(BF16)
    low = (v - high.astype(F32)).astype(BF16)
    e = collect_two(j)
    return dnt(e, high) + dnt(e, low)


def conv_input(ext, live, w, bias, lo, rows):
    u = bias + w[0] * ext[8 + lo : 8 + lo + rows, :]
    for k in range(1, CONV):
        u = u + w[k] * ext[8 - k + lo : 8 - k + lo + rows, :] * live[k - 1, lo : lo + rows, :]
    return u


def live_masks(cnt, live):
    now = cnt[8 : 8 + T, :]
    for k in range(1, CONV):
        live[k - 1] = (now == cnt[8 - k : 8 - k + T, :]).astype(F32)


def block_mask(rt, q, c):
    qc = rt[c * B : (c + 1) * B, H : H + 1]
    qr = q[0:1, c * B : (c + 1) * B]
    ok = (qc == qr) & (iota((B, B), 0) >= iota((B, B), 1))
    return jnp.where(ok, 0.0, -1e30)


def row_state(ref, j, n, lead):
    ncq = n // 8
    tpc = NT // ncq
    cq = j // tpc
    lane = lanes(j % tpc)
    return jnp.concatenate([ref[rz * ncq + cq, :, lane] for rz in range(8)], axis=0)


def put_state(ref, j, n, v):
    ncq = n // 8
    tpc = NT // ncq
    cq = j // tpc
    lane = lanes(j % tpc)
    for rz in range(8):
        ref[rz * ncq + cq, :, lane] = v[rz * ROWS : (rz + 1) * ROWS]


def column(row):
    return jnp.concatenate(
        [jnp.broadcast_to(row, (128, H)), jnp.zeros((128, 128 - H), F32)], axis=1
    ).T[0:H, 0:1]


def rcopy(src, dst, sem_s, sem_r, dev):
    return pltpu.make_async_remote_copy(
        src_ref=src, dst_ref=dst, send_sem=sem_s, recv_sem=sem_r,
        device_id=dev, device_id_type=MESH,
    )


def send_pieces(n, st, rb, s1, r1, cq, me):
    ncq = n // 8

    def send(rz, carry):
        to = rz * ncq + cq

        @pl.when(to != me)
        def _():
            rcopy(st.at[to], rb.at[me], s1.at[to], r1.at[me], {"ctx": to}).start()

        return carry

    lax.fori_loop(0, 8, send, 0)


def owner_scan(n, st, rb, pb, ob, kb, s1, r1, s2, r2, me, backward):
    rb[me] = st[me]

    def step(i, acc):
        d = n - 1 - i if backward else i

        @pl.when(d != me)
        def _():
            rcopy(st.at[0], rb.at[d], s1.at[d], r1.at[d], {"ctx": d}).wait_recv()

        pb[d] = acc.astype(BF16)

        @pl.when(d != me)
        def _():
            rcopy(pb.at[d], ob.at[me], s2.at[d], r2.at[me], {"ctx": d}).start()

        return kb[d] * acc + rb[d].astype(F32)

    lax.fori_loop(0, n, step, jnp.zeros(rb.shape[1:], F32))
    ob[me] = pb[me]


def take_pieces(n, pb, ob, s2, r2, me):
    def step(k, carry):
        d = lax.rem(me + k, n)
        rcopy(pb.at[d], ob.at[d], s2.at[d], r2.at[d], {"ctx": d}).wait_recv()
        return carry

    lax.fori_loop(1, n, step, 0)


def main_body(n, nh, ndp, nt, names, *refs):
    r = types.SimpleNamespace(**dict(zip(names, refs)))
    ncq = n // 8
    tpc = NT // ncq
    me = lax.axis_index("ctx")
    dp = lax.axis_index("dp")
    hd = lax.axis_index("head")
    ne = n * ndp
    mine = dp * n + me
    half = iota((B, 128), 1) < HEAD_DIM
    lane1 = iota((1, 128), 1)
    blocks = [slice(0, B), slice(B, T)]

    r.hbuf[...] = jnp.zeros_like(r.hbuf)
    r.bbuf[...] = jnp.zeros_like(r.bbuf)
    barrier = pltpu.get_barrier_semaphore()

    def greet(k, carry):
        e = lax.rem(mine + k, ne)
        pl.semaphore_signal(
            barrier, inc=1, device_id={"dp": e // n, "ctx": lax.rem(e, n)}, device_id_type=MESH
        )
        return carry

    lax.fori_loop(1, ne, greet, 0)
    for k in range(1, nh):
        pl.semaphore_signal(
            barrier, inc=1, device_id={"head": lax.rem(hd + k, nh)}, device_id_type=MESH
        )
    zcopy = pltpu.make_async_copy(r.z_hbm.at[0], r.z, r.zs)
    gcopy = pltpu.make_async_copy(r.go_hbm.at[0], r.go, r.gs)
    zcopy.start()
    gcopy.start()

    rate = jnp.exp(column(r.alog[...]))
    bias = column(r.dtb[...])
    tri = (iota((B, B), 0) <= iota((B, B), 1)).astype(F32)
    before = jnp.zeros((8, 1), F32)
    r.cnt[0:8, :] = jnp.zeros((8, 128), F32)
    masks = []
    for c in range(2):
        sl = blocks[c]
        dtv = softplus(r.dtr[0, :, sl].astype(F32) + bias)
        run = dnn_full(-rate * dtv, tri)
        q = dnn(jnp.broadcast_to(r.flg[:, sl].astype(F32), (8, B)), tri)
        rl = run[:, B - 1 : B]
        ql = q[:, B - 1 : B]
        dtte = dtv * jnp.where(q[0:1] == ql[0:1], jnp.exp(rl - run), 0.0)
        fs = jnp.where(q[0:1] == 0.0, jnp.exp(run), 0.0)
        r.dt[c] = dtv
        r.run[c] = run
        a1, a2 = high_low(dtte)
        b1, b2 = high_low(fs)
        r.mt[sl, :] = jnp.concatenate([a1, a2, b1, b2], axis=0).T.astype(BF16)
        dev = q + before
        before = dev[:, B - 1 : B]
        rt = jnp.concatenate([q, dev, jnp.zeros((112, B), F32)], axis=0).T
        r1, r2 = high_low(run)
        r2, r3 = high_low(r2)
        r.rs[sl, :] = jnp.concatenate(
            [r1, r2, r3, jnp.zeros((H, B), F32)], axis=0
        ).T.astype(BF16)
        r.cnt[8 + c * B : 8 + (c + 1) * B, :] = jnp.broadcast_to(rt[:, 8:9], (B, 128))
        ok = (rt[:, 0:1] == q[0:1, :]) & (iota((B, B), 0) >= iota((B, B), 1))
        r.mask[c] = jnp.where(ok, 0.0, -1e30)
    live_masks(r.cnt, r.live)

    row16 = iota((16, 128), 0)
    same = (r.cnt[8 + T - 16 : 8 + T, :] == r.cnt[8 + T - 1 : 8 + T, :])
    for j in range(NT + 4):
        v = r.x[0, T - 16 : T, j * 128 : (j + 1) * 128] if j < NT else r.bc[
            T - 16 : T, j * 128 - D : (j + 1) * 128 - D
        ]
        r.tail[:, j * 128 : (j + 1) * 128] = jnp.where(same, v.astype(F32), 0.0).astype(BF16)

    def bc_weights(j):
        i, sl = j // 2, slice((j % 2) * 128, (j % 2) * 128 + 128)
        return [r.cbw[k, i : i + 1, sl] for k in range(CONV)], r.cbb[i : i + 1, sl]

    def x_weights(ln):
        return [r.cxw[k : k + 1, ln] for k in range(CONV)], r.cxb[0:1, ln]

    def bc_conv(c):
        for j in range(4):
            sl = slice(j * 128, (j + 1) * 128)
            ext = r.ext.at[j]
            if c == 1:
                ext[8 : 8 + T, :] = r.bc[:, sl].astype(F32)
            else:
                ext[8 : 8 + B, :] = r.bc[0:B, sl].astype(F32)
                ext[0:8, :] = r.hbuf[8:16, D + j * 128 : D + (j + 1) * 128].astype(F32)
            u = conv_input(ext, r.live, *bc_weights(j), c * B, B)
            sg = sigmoid(u)
            r.bcc[blocks[c], sl] = (u * sg).astype(BF16)
            r.cdb[blocks[c], sl] = sg * (1.0 + u * (1.0 - sg))

    def x_conv(j, c):
        ln = lanes(j)
        ext = r.ext.at[j % 4]
        if c == 1:
            ext[8 : 8 + T, :] = r.x[0, :, ln].astype(F32)
        else:
            ext[8 : 8 + B, :] = r.x[0, 0:B, ln].astype(F32)
            ext[0:8, :] = r.hbuf[8:16, ln].astype(F32)
        u = conv_input(ext, r.live, *x_weights(ln), c * B, B)
        xc = (u * sigmoid(u)).astype(BF16)
        r.xc[blocks[c], ln] = xc
        dtte = dnn(r.mt[blocks[c], 0 : 2 * H], spread_two(j))
        return (xc.astype(F32) * dtte).astype(BF16)

    def b_turned(g, c):
        return r.bcc[blocks[c], g * 128 : (g + 1) * 128].astype(F32).T.astype(BF16)

    def keep_row(j, c):
        return dnn(r.mt[(c + 1) * B - 16 : (c + 1) * B, 2 * H : 4 * H], spread_two(j))[15:16]

    bc_conv(1)
    for g in range(NG):
        bt = b_turned(g, 1)

        def second(jj, carry, g=g, bt=bt):
            j = g * TPG + jj
            r.fr[1, :, lanes(j)] = dnn(bt, x_conv(j, 1))
            return carry

        lax.fori_loop(0, TPG, second, 0, unroll=2)
        if g == 0:
            pl.semaphore_wait(barrier, ne - 1 + nh - 1)
            halo = rcopy(r.tail, r.hbuf, r.sh, r.rh, {"ctx": lax.rem(me + 1, n)})

            @pl.when(me < n - 1)
            def _():
                halo.start()

    @pl.when(me > 0)
    def _():
        halo.wait_recv()

    bc_conv(0)
    bts = [b_turned(g, 0) for g in range(NG)]
    for cq in range(ncq):
        bt = bts[cq * tpc // TPG]

        def first(jj, carry, cq=cq, bt=bt):
            j = cq * tpc + jj
            ln = lanes(j)
            fresh = dnn(bt, x_conv(j, 0))
            r.fr[0, :, ln] = fresh
            k1 = keep_row(j, 1)
            put_state(r.st, j, n, (k1 * fresh + r.fr[1, :, ln]).astype(BF16))
            r.kr[cq, :, lanes(jj)] = keep_row(j, 0) * k1
            return carry

        lax.fori_loop(0, tpc, first, 0, unroll=2)
        send_pieces(n, r.st, r.rb, r.s1, r.r1, cq, me)

        def send_row(rz, carry, cq=cq):
            to = rz * ncq + cq

            @pl.when(to != me)
            def _():
                rcopy(r.kr.at[cq], r.kb.at[me], r.sk.at[to], r.rk.at[me], {"ctx": to}).start()

            return carry

        lax.fori_loop(0, 8, send_row, 0)

    def group_parts(g, c):
        return (
            r.bcc[blocks[c], g * 128 : (g + 1) * 128],
            r.bcc[blocks[c], 256 + g * 128 : 256 + (g + 1) * 128],
        )

    for g in range(NG):
        for c in range(2):
            bb, cc = group_parts(g, c)
            r.gm[...] = dnt(cc, bb)

            def inside(jj, carry, g=g, c=c):
                j = g * TPG + jj
                ln = lanes(j)
                rb2 = dnn(r.rs[blocks[c], :], spread_pair(j))
                ws = []
                for i in range(2):
                    h = 2 * j + i
                    lm = jnp.exp(
                        rb2[:, i * B : (i + 1) * B] - r.run[c, pl.ds(h, 1), :] + r.mask[c]
                    ) * r.dt[c, pl.ds(h, 1), :]
                    r.lm[2 * j + c, i * B : (i + 1) * B, :] = lm
                    wv = (r.gm[...] * lm).astype(BF16)
                    r.wm[2 * j + c, i * B : (i + 1) * B, :] = wv
                    ws.append(wv)
                xt = r.xc[blocks[c], ln]
                zero = jnp.zeros_like(xt)
                xbd = jnp.concatenate(
                    [jnp.where(half, xt, zero), jnp.where(half, zero, xt)], axis=0
                )
                r.y[blocks[c], ln] = dnn(jnp.concatenate(ws, axis=1), xbd)
                return carry

            lax.fori_loop(0, TPG, inside, 0, unroll=2)

    r.kb[me] = r.kr[lax.rem(me, ncq)]

    def rows_in(k, carry):
        d = lax.rem(me + k, n)
        rcopy(r.kr.at[0], r.kb.at[d], r.sk.at[d], r.rk.at[d], {"ctx": d}).wait_recv()
        return carry

    lax.fori_loop(1, n, rows_in, 0)
    owner_scan(n, r.st, r.rb, r.pb, r.ob, r.kb, r.s1, r.r1, r.s2, r.r2, me, False)

    zcopy.wait()
    gcopy.wait()

    def prepare(j, carry):
        ln = lanes(j)
        zf = r.z[:, ln].astype(F32)
        sg = sigmoid(zf)
        r.gate[:, ln] = zf * sg
        r.dgate[:, ln] = sg * (1.0 + zf * (1.0 - sg))
        ext = r.ext.at[j % 4]
        ext[8 : 8 + T, :] = r.x[0, :, ln].astype(F32)
        ext[0:8, :] = r.hbuf[8:16, ln].astype(F32)
        for c in range(2):
            u = conv_input(ext, r.live, *x_weights(ln), c * B, B)
            sg = sigmoid(u)
            r.cdx[blocks[c], ln] = sg * (1.0 + u * (1.0 - sg))
        return carry

    lax.fori_loop(0, NT, prepare, 0)
    take_pieces(n, r.pb, r.ob, r.s2, r.r2, me)

    r.sums_acc[...] = jnp.zeros_like(r.sums_acc)

    def skip_row(j):
        return jnp.where(lane1 < HEAD_DIM, r.skip[2 * j], r.skip[2 * j + 1])

    for g in range(NG):
        ccs = [group_parts(g, c)[1] for c in range(2)]

        def outputs(jj, carry, g=g, ccs=ccs):
            j = g * TPG + jj
            ln = lanes(j)
            fs = dnn(r.mt[:, 2 * H : 4 * H], spread_two(j))
            sb0 = row_state(r.ob, j, n, 0)
            sb1 = (fs[B - 1 : B] * sb0.astype(F32) + r.fr[0, :, ln]).astype(BF16)
            r.sb1[:, ln] = sb1
            for c in range(2):
                sl = blocks[c]
                y = r.y[sl, ln] + dnn(ccs[c], sb0 if c == 0 else sb1) * fs[sl]
                r.y[sl, ln] = y
                mixed = (y + skip_row(j) * r.xc[sl, ln].astype(F32)).astype(BF16)
                r.mixed[sl, ln] = mixed
                gated = mixed.astype(F32) * r.gate[sl, ln]
                gained = r.go[sl, ln].astype(F32) * r.gain[0:1, ln]
                r.sums_acc[0, sl, :] += gated * gated
                r.sums_acc[1, sl, :] += gated * gained
            return carry

        lax.fori_loop(0, TPG, outputs, 0, unroll=2)
    ones = jnp.ones((8, 128), F32)
    r.sums[0:8, :] = dnt_full(ones, r.sums_acc[0])
    r.sums[8:16, :] = dnt_full(ones, r.sums_acc[1])
    copies = []
    for k in range(1, nh):
        copies.append(
            rcopy(r.sums, r.sbuf.at[k], r.hs.at[k], r.hr.at[k], {"head": lax.rem(hd + k, nh)})
        )
        copies[-1].start()
    for cp in copies:
        cp.wait()
    parts = [r.sums[...]] + [r.sbuf[k] for k in range(1, nh)]
    total = jnp.zeros_like(parts[0])
    for d in range(nh):
        for k in range(nh):
            total = total + jnp.where(lax.rem(hd - k + nh, nh) == d, parts[k], 0.0)
    inv = lax.rsqrt(total[0:8] / INNER + EPS)
    coef = inv * inv * inv * total[8:16] / INNER
    for c in range(2):
        sl = blocks[c]
        tr = jnp.concatenate([inv[:, sl], coef[:, sl], jnp.zeros((112, B), F32)], axis=0).T
        r.inv[sl, :] = jnp.broadcast_to(tr[:, 0:1], (B, 128))
        r.coef[sl, :] = jnp.broadcast_to(tr[:, 8:9], (B, 128))

    r.rho[...] = jnp.zeros_like(r.rho)
    r.skc[...] = jnp.zeros_like(r.skc)
    cts = [[group_parts(g, c)[1].astype(F32).T.astype(BF16) for c in range(2)] for g in range(NG)]
    for cq in range(ncq):
        ct = cts[cq * tpc // TPG]

        def gates(jj, carry, cq=cq, ct=ct):
            j = cq * tpc + jj
            ln = lanes(j)
            e2 = spread_two(j)
            grow = jnp.zeros((1, 128), F32)
            srow = jnp.zeros((1, 128), F32)
            ds = []
            for c in range(2):
                sl = blocks[c]
                m = r.mixed[sl, ln].astype(F32)
                gt = r.gate[sl, ln]
                go = r.go[sl, ln].astype(F32)
                gated = m * gt
                iv = r.inv[sl, :]
                dg = go * r.gain[0:1, ln] * iv - gated * r.coef[sl, :]
                grow = grow + jnp.sum(go * gated * iv, axis=0, keepdims=True)
                r.dz[sl, ln] = (dg * m * r.dgate[sl, ln]).astype(BF16)
                dm = (dg * gt).astype(BF16)
                r.dy[sl, ln] = dm
                dy = dm.astype(F32)
                srow = srow + jnp.sum(dy * r.xc[sl, ln].astype(F32), axis=0, keepdims=True)
                r.rho[:, sl] += head_sums(j, dy * r.y[sl, ln])
                fs = dnn(r.mt[sl, 2 * H : 4 * H], e2)
                if c == 1:
                    k0 = keep_row(j, 0)
                fd = (fs * dy).astype(BF16)
                r.fd[sl, ln] = fd
                ds.append(dnn(ct[c], fd).astype(BF16))
            r.dsb1[:, ln] = ds[1]
            put_state(
                r.ad, j, n, (k0 * ds[1].astype(F32) + ds[0].astype(F32)).astype(BF16)
            )
            r.pk[j, 5:6, :] = grow
            r.pk[j, 6:8, :] = jnp.zeros((2, 128), F32)
            r.skc[...] += head_sums(j, jnp.broadcast_to(srow, (8, 128)))
            return carry

        lax.fori_loop(0, tpc, gates, 0, unroll=2)
        send_pieces(n, r.ad, r.rb2, r.s3, r.r3, cq, me)

    for g in range(NG):
        r.acc[...] = jnp.zeros_like(r.acc)

        def inner(jj, carry, g=g):
            j = g * TPG + jj
            ln = lanes(j)
            for c in range(2):
                sl = blocks[c]
                dyt = r.dy[sl, ln]
                zero = jnp.zeros_like(dyt)
                dybd = jnp.concatenate(
                    [jnp.where(half, dyt, zero), jnp.where(half, zero, dyt)], axis=0
                )
                dw = dnt(dybd, r.xc[sl, ln])
                i = 2 * j + c
                r.acc[0, c] += dw[0:B] * r.lm[i, 0:B, :] + dw[B : 2 * B] * r.lm[i, B : 2 * B, :]
                r.y[sl, ln] = dtn(r.wm[i], dybd)
                sp = row_state(r.ob, j, n, 0) if c == 0 else r.sb1[:, ln]
                r.acc[1, c] += dnt(r.fd[sl, ln], sp)
            return carry

        lax.fori_loop(0, TPG, inner, 0, unroll=2)
        for c in range(2):
            bb, cc = group_parts(g, c)
            dg = r.acc[0, c].astype(BF16)
            r.dbc[blocks[c], g * 128 : (g + 1) * 128] = dtn(dg, cc)
            r.dbc[blocks[c], 256 + g * 128 : 256 + (g + 1) * 128] = r.acc[1, c] + dnn(dg, bb)
        if g == 0:
            owner_scan(n, r.ad, r.rb2, r.pb2, r.ob2, r.kb, r.s3, r.r3, r.s4, r.r4, me, True)
    take_pieces(n, r.pb2, r.ob2, r.s4, r.r4, me)

    r.kap[...] = jnp.zeros_like(r.kap)
    r.tl[...] = jnp.zeros_like(r.tl)
    r.vk[:, :, 0:8, :] = jnp.zeros((2, CONV, 8, 128), F32)
    r.vk[:, :, 8 + T :, :] = jnp.zeros((2, CONV, 8, 128), F32)

    def is_owner(j):
        return (me == j) & (dp == lax.rem(j, ndp))

    def give_tile(j):
        @pl.when(jnp.logical_not(is_owner(j)))
        def _():
            rcopy(
                r.pk.at[j], r.prb.at[mine], r.ps.at[j], r.pr.at[mine],
                {"dp": lax.rem(j, ndp), "ctx": j},
            ).start()

    def conv_back(ext, vk, w, deriv, dxc, j):
        du = dxc.astype(BF16).astype(F32) * deriv
        rows = [jnp.sum(du * ext[8 : 8 + T, :], axis=0, keepdims=True)]
        for k in range(1, CONV):
            v = du * r.live[k - 1]
            rows.append(jnp.sum(v * ext[8 - k : 8 - k + T, :], axis=0, keepdims=True))
            vk[k, 8 : 8 + T, :] = v
        rows.append(jnp.sum(du, axis=0, keepdims=True))
        own = w[0] * du
        prior = jnp.zeros((8, 128), F32)
        for k in range(1, CONV):
            own = own + w[k] * vk[k, 8 + k : 8 + k + T, :]
            prior = prior + w[k] * vk[k, k : k + 8, :]
        r.pk[j, 0 : CONV + 1, :] = jnp.concatenate(rows, axis=0)
        return own, prior

    for g in range(NG):
        r.acc[1] = jnp.zeros((2, B, 128), F32)

        def outer(jj, carry, g=g):
            j = g * TPG + jj
            ln = lanes(j)
            e2 = spread_two(j)
            a1 = row_state(r.ob2, j, n, 0).astype(F32)
            sk = skip_row(j)
            outs = []
            for c in range(2):
                sl = blocks[c]
                if c == 1:
                    ds = a1
                    sp = r.sb1[:, ln]
                else:
                    ds = keep_row(j, 1) * a1 + r.dsb1[:, ln].astype(F32)
                    sp = row_state(r.ob, j, n, 0)
                dsh = ds.astype(BF16)
                xf = r.xc[sl, ln].astype(F32)
                dtte = dnn(r.mt[sl, 0 : 2 * H], e2)
                dxu = dnn(r.bcc[sl, g * 128 : (g + 1) * 128], dsh) * dtte
                r.acc[1, c] += dnt((xf * dtte).astype(BF16), dsh)
                dxs = r.y[sl, ln] + dxu
                ku = jnp.sum(xf * dxu, axis=0, keepdims=True)
                kd = jnp.sum(ds * sp.astype(F32), axis=0, keepdims=True) * keep_row(j, c)
                hs = head_sums(
                    j, jnp.concatenate([xf * dxs, jnp.broadcast_to(ku + kd, (8, 128))], axis=0)
                )
                r.kap[:, sl] += hs[:, 0:B]
                r.tl[:, c * 8 : (c + 1) * 8] += hs[:, B : B + 8]
                outs.append(dxs + sk * r.dy[sl, ln].astype(F32))
            ext = r.ext.at[j % 4]
            ext[8 : 8 + T, :] = r.x[0, :, ln].astype(F32)
            ext[0:8, :] = r.hbuf[8:16, ln].astype(F32)
            own, prior = conv_back(
                ext, r.vk.at[j % 2], x_weights(ln)[0], r.cdx[:, ln],
                jnp.concatenate(outs, axis=0), j,
            )
            r.gx[:, ln] = own.astype(BF16)
            r.tails[:, ln] = own[T - 16 : T]
            r.hb[:, ln] = prior
            give_tile(j)
            return carry

        lax.fori_loop(0, TPG, outer, 0, unroll=2)
        for c in range(2):
            r.dbc[blocks[c], g * 128 : (g + 1) * 128] += r.acc[1, c]

    for j in range(4):
        sl = slice(j * 128, (j + 1) * 128)
        sd = slice(D + j * 128, D + (j + 1) * 128)
        ext = r.ext.at[j]
        ext[8 : 8 + T, :] = r.bc[:, sl].astype(F32)
        ext[0:8, :] = r.hbuf[8:16, sd].astype(F32)
        own, prior = conv_back(
            ext, r.vk.at[j % 2], bc_weights(j)[0], r.cdb[:, sl], r.dbc[:, sl], NT + j
        )
        r.pk[NT + j, 5:8, :] = jnp.zeros((3, 128), F32)
        r.gbc[:, sl] = own.astype(BF16)
        r.tails[:, sd] = own[T - 16 : T]
        r.hb[:, sd] = prior
        give_tile(NT + j)
    back = rcopy(r.hb, r.bbuf, r.sb, r.rb_sem, {"ctx": lax.rem(me + n - 1, n)})

    @pl.when(me > 0)
    def _():
        back.start()

    rev = (iota((B, B), 0) >= iota((B, B), 1)).astype(F32)
    rate_sum = jnp.zeros((H, B), F32)
    bias_sum = jnp.zeros((H, B), F32)
    for c in range(2):
        sl = blocks[c]
        dtv = r.dt[c]
        kp = r.kap[:, sl]
        rr = dnn_full(r.rho[:, sl] - kp, rev) + r.tl[:, c * 8 : c * 8 + 1]
        gd = (kp / dtv - rate * rr) * sigmoid(r.dtr[0, :, sl].astype(F32) + bias)
        r.gdt[:, sl] = gd
        rate_sum = rate_sum - rate * dtv * rr
        bias_sum = bias_sum + gd
    skips = jnp.where(iota((H, B), 1) == 0, r.skc[:, 0:1], 0.0)
    r.pk[nt - 1] = dnt_full(
        ones, jnp.concatenate([rate_sum, bias_sum, skips, jnp.zeros((H, B), F32)], axis=0)
    )
    give_tile(nt - 1)

    @pl.when((me < nt) & (dp == lax.rem(me, ndp)))
    def _():
        r.prb[mine] = r.pk[me]

        def collect(e, total):
            @pl.when(e != mine)
            def _():
                rcopy(
                    r.pk.at[0], r.prb.at[e], r.ps.at[0], r.pr.at[e],
                    {"dp": e // n, "ctx": lax.rem(e, n)},
                ).wait_recv()

            return total + r.prb[e]

        r.pob[me] = lax.fori_loop(0, ne, collect, jnp.zeros((8, 128), F32))

        def give(k, carry):
            e = lax.rem(mine + k, ne)
            rcopy(
                r.pob.at[me], r.pob.at[me], r.as_.at[e], r.ar.at[me],
                {"dp": e // n, "ctx": lax.rem(e, n)},
            ).start()
            return carry

        lax.fori_loop(1, ne, give, 0)

    @pl.when(me < n - 1)
    def _():
        halo.wait_send()
        back.wait_recv()

    @pl.when(me > 0)
    def _():
        back.wait_send()

    def finish(k, carry):
        d = lax.rem(me + k, n)
        to = {"ctx": d}
        rcopy(r.st.at[d], r.rb.at[d], r.s1.at[d], r.r1.at[d], to).wait_send()
        rcopy(r.kr.at[0], r.kb.at[d], r.sk.at[d], r.rk.at[d], to).wait_send()
        rcopy(r.pb.at[d], r.ob.at[d], r.s2.at[d], r.r2.at[d], to).wait_send()
        rcopy(r.ad.at[d], r.rb2.at[d], r.s3.at[d], r.r3.at[d], to).wait_send()
        rcopy(r.pb2.at[d], r.ob2.at[d], r.s4.at[d], r.r4.at[d], to).wait_send()
        return carry

    lax.fori_loop(1, n, finish, 0)

    def tiles_in(j, carry):
        @pl.when(jnp.logical_not(is_owner(j)))
        def _():
            to = {"dp": lax.rem(j, ndp), "ctx": j}
            rcopy(r.pk.at[j], r.prb.at[0], r.ps.at[j], r.pr.at[0], to).wait_send()
            rcopy(r.pob.at[j], r.pob.at[j], r.as_.at[0], r.ar.at[j], to).wait_recv()

        return carry

    lax.fori_loop(0, nt, tiles_in, 0)

    @pl.when((me < nt) & (dp == lax.rem(me, ndp)))
    def _():
        def sent(k, carry):
            e = lax.rem(mine + k, ne)
            rcopy(
                r.pob.at[0], r.pob.at[0], r.as_.at[e], r.ar.at[0],
                {"dp": e // n, "ctx": lax.rem(e, n)},
            ).wait_send()
            return carry

        lax.fori_loop(1, ne, sent, 0)

    r.red[...] = r.pob[...]
    r.rh_o[...] = r.bbuf[...]


def k5_body(scale, red, rh, tail, flg, gx_in, gbc_in,
            gx_o, gbc_o, cw_o, cb_o, bw_o, bb_o, al_o, db_o, sk_o, ga_o):
    f = flg[:, B:T].astype(F32)
    lane = iota((1, B), 1)
    last = jnp.sum(jnp.where(lane == B - 1, f, 0.0))
    two = jnp.sum(jnp.where(lane >= B - 2, f, 0.0))
    row = iota((16, 128), 0)
    keep = jnp.where(row == 15, 1.0, 0.0)
    keep = keep + jnp.where((row == 14) & (last == 0.0), 1.0, 0.0)
    keep = keep + jnp.where((row == 13) & (two == 0.0), 1.0, 0.0)
    for j in range(NT + 4):
        sl = slice(j * 128, (j + 1) * 128)
        add = jnp.concatenate([jnp.zeros((8, 128), F32), rh[:, sl]], axis=0)
        v = (tail[:, sl] + add * keep).astype(BF16)
        t = red[j] * scale
        if j < NT:
            gx_o[:, sl] = v
            cw_o[:, sl] = t[0:4]
            cb_o[:, sl] = t[4:5]
            ga_o[:, sl] = t[5:6]
        else:
            so = slice(j * 128 - D, (j + 1) * 128 - D)
            gbc_o[:, so] = v
            i, sb = (j - NT) // 2, slice(((j - NT) % 2) * 128, ((j - NT) % 2) * 128 + 128)
            for k in range(CONV):
                bw_o[k, i : i + 1, sb] = t[k : k + 1]
            bb_o[i : i + 1, sb] = t[4:5]
    last_tile = red[NT + 4] * scale
    al_o[...] = last_tile[0:1, 0:H]
    db_o[...] = last_tile[0:1, H : 2 * H]
    sk_o[...] = last_tile[0:1, 2 * H : 3 * H]


def sds(*shape, dtype=F32):
    return jax.ShapeDtypeStruct(shape, dtype)


def per_device(
    x_raw, bc_raw, z_gate, dt_raw, resets, conv_x_weight, conv_x_bias, conv_bc_weight,
    conv_bc_bias, a_log, dt_bias, skip_weight, norm_gain, grad_out,
):
    n = lax.axis_size("ctx")
    nh = lax.axis_size("head")
    ndp = lax.axis_size("dp")
    ncq = n // 8
    w = D // ncq
    nt = NT + 5
    ne = n * ndp
    ANY = pl.BlockSpec(memory_space=pl.ANY)
    ins = [
        ("x", x_raw, VM), ("bc", bc_raw[0].reshape(T, DB), VM), ("z_hbm", z_gate, ANY),
        ("go_hbm", grad_out, ANY), ("dtr", dt_raw, VM), ("flg", resets, VM),
        ("alog", a_log.reshape(1, H), VM), ("dtb", dt_bias.reshape(1, H), VM),
        ("cxw", conv_x_weight, VM), ("cxb", conv_x_bias.reshape(1, D), VM),
        ("cbw", conv_bc_weight, VM), ("cbb", conv_bc_bias, VM),
        ("gain", norm_gain.reshape(1, D), VM), ("skip", skip_weight, SM),
    ]
    outs = [
        ("gx", sds(T, D, dtype=BF16)), ("gbc", sds(T, DB, dtype=BF16)),
        ("dz", sds(T, D, dtype=BF16)), ("gdt", sds(H, T)), ("tails", sds(16, D + DB)),
        ("red", sds(nt, 8, 128)), ("rh_o", sds(8, D + DB)),
    ]
    V = pltpu.VMEM
    dma = pltpu.SemaphoreType.DMA
    state = V((n, ROWS, w), BF16)
    scratch = [
        ("z", V((T, D), BF16)), ("go", V((T, D), BF16)), ("zs", dma), ("gs", dma),
        ("ext", V((4, T + 8, 128), F32)), ("cnt", V((T + 8, 128), F32)),
        ("live", V((CONV - 1, T, 128), F32)), ("mask", V((2, B, B), F32)),
        ("dt", V((2, H, B), F32)), ("run", V((2, H, B), F32)), ("mt", V((T, 128), BF16)),
        ("rs", V((T, 128), BF16)), ("tail", V((16, D + DB), BF16)),
        ("hbuf", V((16, D + DB), BF16)), ("xc", V((T, D), BF16)), ("bcc", V((T, DB), BF16)),
        ("cdb", V((T, DB), F32)), ("cdx", V((T, D), F32)), ("fr", V((2, NSTATE, D), F32)),
        ("kr", V((ncq, 1, w), F32)), ("kb", V((n, 1, w), F32)), ("gm", V((B, B), F32)),
        ("lm", V((2 * NT, 2 * B, B), F32)), ("wm", V((2 * NT, 2 * B, B), BF16)),
        ("y", V((T, D), F32)), ("gate", V((T, D), F32)), ("dgate", V((T, D), F32)),
        ("mixed", V((T, D), BF16)), ("sb1", V((NSTATE, D), BF16)),
        ("sums_acc", V((2, T, 128), F32)), ("sums", V((16, T), F32)),
        ("sbuf", V((nh, 16, T), F32)), ("inv", V((T, 128), F32)), ("coef", V((T, 128), F32)),
        ("rho", V((H, T), F32)), ("skc", V((H, 8), F32)), ("dy", V((T, D), BF16)),
        ("fd", V((T, D), BF16)), ("dsb1", V((NSTATE, D), BF16)), ("acc", V((2, 2, B, 128), F32)),
        ("dbc", V((T, DB), F32)), ("kap", V((H, T), F32)), ("tl", V((H, 16), F32)),
        ("vk", V((2, CONV, T + 16, 128), F32)), ("pk", V((nt, 8, 128), F32)),
        ("prb", V((ne, 8, 128), F32)), ("pob", V((nt, 8, 128), F32)),
        ("hb", V((8, D + DB), F32)), ("bbuf", V((8, D + DB), F32)),
        ("st", state), ("rb", state), ("pb", state), ("ob", state),
        ("ad", state), ("rb2", state), ("pb2", state), ("ob2", state),
        ("sh", dma), ("rh", dma), ("sb", dma), ("rb_sem", dma),
        ("hs", dma((nh,))), ("hr", dma((nh,))),
    ]
    scratch += [(k, dma((n,))) for k in ("s1", "r1", "s2", "r2", "s3", "r3", "s4", "r4", "sk", "rk")]
    scratch += [("ps", dma((nt,))), ("ar", dma((nt,))), ("pr", dma((ne,))), ("as_", dma((ne,)))]
    names = [v[0] for v in ins] + [v[0] for v in outs] + [v[0] for v in scratch]
    gx, gbc, dz, gdt, tails, red, rh = pl.pallas_call(
        functools.partial(main_body, n, nh, ndp, nt, names),
        out_shape=[v[1] for v in outs],
        in_specs=[v[2] for v in ins],
        out_specs=[VM] * len(outs),
        scratch_shapes=[v[1] for v in scratch],
        compiler_params=pltpu.CompilerParams(
            vmem_limit_bytes=VLIM, collective_id=0, has_side_effects=True
        ),
    )(*[v[1] for v in ins])
    scale = float(ndp * n * T) ** (-0.5)
    whole = lambda *s: pl.BlockSpec(s, lambda i: (0,) * len(s))
    outs = pl.pallas_call(
        functools.partial(k5_body, scale),
        grid=(1,),
        out_shape=(
            sds(T, D, dtype=BF16), sds(T, DB, dtype=BF16), sds(CONV, D), sds(1, D),
            sds(CONV, 2, DB // 2), sds(2, DB // 2), sds(1, H), sds(1, H), sds(1, H), sds(1, D),
        ),
        in_specs=[
            whole(nt, 8, 128), whole(8, D + DB), whole(16, D + DB), whole(1, T),
            pl.BlockSpec(memory_space=pl.ANY), pl.BlockSpec(memory_space=pl.ANY),
        ],
        out_specs=[
            pl.BlockSpec((16, D), lambda i: (T // 16 - 1, 0)),
            pl.BlockSpec((16, DB), lambda i: (T // 16 - 1, 0)),
            whole(CONV, D), whole(1, D), whole(CONV, 2, DB // 2), whole(2, DB // 2),
            whole(1, H), whole(1, H), whole(1, H), whole(1, D),
        ],
        input_output_aliases={4: 0, 5: 1},
    )(red, rh, tails, resets, gx, gbc)
    gx, gbc, cw, cb, bw, bb, al, db, sk, ga = outs
    return (
        gx[None], gbc.reshape(1, T, 2, DB // 2), dz[None], gdt[None], cw, cb.reshape(D),
        bw, bb, al.reshape(H), db.reshape(H), sk.reshape(H), ga.reshape(D),
    )


def solution(mesh):
    return jax.shard_map(
        per_device,
        mesh=mesh,
        in_specs=(
            P("dp", "ctx", "head"),
            P("dp", "ctx", None, "head"),
            P("dp", "ctx", "head"),
            P("dp", "head", "ctx"),
            P("dp", "ctx"),
            P(None, "head"),
            P("head"),
            P(None, None, "head"),
            P(None, "head"),
            P("head"),
            P("head"),
            P("head"),
            P("head"),
            P("dp", "ctx", "head"),
        ),
        out_specs=(
            P("dp", "ctx", "head"),
            P("dp", "ctx", None, "head"),
            P("dp", "ctx", "head"),
            P("dp", "head", "ctx"),
            P(None, "head"),
            P("head"),
            P(None, None, "head"),
            P(None, "head"),
            P("head"),
            P("head"),
            P("head"),
            P("head"),
        ),
        check_vma=False,
    )
```

```python
import functools

import types

import jax
import jax.numpy as jnp
from jax import lax
from jax.experimental import pallas as pl
from jax.experimental.pallas import tpu as pltpu
from jax.sharding import PartitionSpec as P

F32 = jnp.float32
BF16 = jnp.bfloat16
HIGHEST = lax.Precision.HIGHEST
MESH = pl.DeviceIdType.MESH

HEAD_DIM = 64
NSTATE = 128
CONV = 4
INNER = 8192
EPS = 1e-05

T = 256
B = 128
H = 32
D = 2048
DB = 512
NT = D // 128
NG = 2
TPG = NT // NG
ROWS = 16
VM = pl.BlockSpec(memory_space=pltpu.VMEM)
SM = pl.BlockSpec(memory_space=pltpu.SMEM)
VLIM = 60 * 1024 * 1024


def dnn(a, b):
    return lax.dot_general(a, b, (((1,), (0,)), ((), ())), preferred_element_type=F32)


def dnt(a, b):
    return lax.dot_general(a, b, (((1,), (1,)), ((), ())), preferred_element_type=F32)


def dtn(a, b):
    return lax.dot_general(a, b, (((0,), (0,)), ((), ())), preferred_element_type=F32)


def dnn_full(a, b):
    return lax.dot_general(
        a, b, (((1,), (0,)), ((), ())), precision=HIGHEST, preferred_element_type=F32
    )


def dnt_full(a, b):
    return lax.dot_general(
        a, b, (((1,), (1,)), ((), ())), precision=HIGHEST, preferred_element_type=F32
    )


def iota(shape, dim):
    return lax.broadcasted_iota(jnp.int32, shape, dim)


def high_low(v):
    high = v.astype(BF16).astype(F32)
    return high, v - high


def sigmoid(v):
    return 1.0 / (1.0 + jnp.exp(-v))


def softplus(v):
    y = jnp.exp(-jnp.abs(v))
    series = y * (1.0 - y * (0.5 - y * (1.0 / 3.0 - y * (0.25 - 0.2 * y))))
    return jnp.maximum(v, 0.0) + jnp.where(y < 0.02, series, jnp.log(1.0 + y))


def lanes(j):
    return pl.ds(pl.multiple_of(j * 128, 128), 128)


def spread_two(j):
    row = iota((2 * H, 128), 0) % H
    lane = iota((2 * H, 128), 1)
    return (row == 2 * j + lane // HEAD_DIM).astype(BF16)


def spread_pair(j):
    row = iota((128, 256), 0)
    lane = iota((128, 256), 1)
    return ((row % H == 2 * j + lane // 128) & (row < 3 * H)).astype(BF16)


def collect_two(j):
    row = iota((H, 128), 0)
    lane = iota((H, 128), 1)
    return (row == 2 * j + lane // HEAD_DIM).astype(BF16)


def head_sums(j, v):
    high = v.astype(BF16)
    low = (v - high.astype(F32)).astype(BF16)
    e = collect_two(j)
    return dnt(e, high) + dnt(e, low)


def conv_input(ext, live, w, bias, lo, rows):
    u = bias + w[0] * ext[8 + lo : 8 + lo + rows, :]
    for k in range(1, CONV):
        u = u + w[k] * ext[8 - k + lo : 8 - k + lo + rows, :] * live[k - 1, lo : lo + rows, :]
    return u


def live_masks(cnt, live):
    now = cnt[8 : 8 + T, :]
    for k in range(1, CONV):
        live[k - 1] = (now == cnt[8 - k : 8 - k + T, :]).astype(F32)


def block_mask(rt, q, c):
    qc = rt[c * B : (c + 1) * B, H : H + 1]
    qr = q[0:1, c * B : (c + 1) * B]
    ok = (qc == qr) & (iota((B, B), 0) >= iota((B, B), 1))
    return jnp.where(ok, 0.0, -1e30)


def row_state(ref, j, n, lead):
    ncq = n // 8
    tpc = NT // ncq
    cq = j // tpc
    lane = lanes(j % tpc)
    return jnp.concatenate([ref[rz * ncq + cq, :, lane] for rz in range(8)], axis=0)


def put_state(ref, j, n, v):
    ncq = n // 8
    tpc = NT // ncq
    cq = j // tpc
    lane = lanes(j % tpc)
    for rz in range(8):
        ref[rz * ncq + cq, :, lane] = v[rz * ROWS : (rz + 1) * ROWS]


def column(row):
    return jnp.concatenate(
        [jnp.broadcast_to(row, (128, H)), jnp.zeros((128, 128 - H), F32)], axis=1
    ).T[0:H, 0:1]


def rcopy(src, dst, sem_s, sem_r, dev):
    return pltpu.make_async_remote_copy(
        src_ref=src, dst_ref=dst, send_sem=sem_s, recv_sem=sem_r,
        device_id=dev, device_id_type=MESH,
    )


def send_pieces(n, st, rb, s1, r1, cq, me):
    ncq = n // 8

    def send(rz, carry):
        to = rz * ncq + cq

        @pl.when(to != me)
        def _():
            rcopy(st.at[to], rb.at[me], s1, r1, {"ctx": to}).start()

        return carry

    lax.fori_loop(0, 8, send, 0)


def owner_scan(n, st, rb, pb, ob, kb, s1, r1, s2, r2, me, backward):
    rb[me] = st[me]
    others = pl.ds(0, n - 1)
    rcopy(st.at[others], rb.at[others], s1, r1, {"ctx": me}).wait_recv()

    def step(i, acc):
        d = n - 1 - i if backward else i

        pb[d] = acc.astype(BF16)

        @pl.when(d != me)
        def _():
            rcopy(pb.at[d], ob.at[me], s2, r2, {"ctx": d}).start()

        return kb[d] * acc + rb[d].astype(F32)

    lax.fori_loop(0, n, step, jnp.zeros(rb.shape[1:], F32))
    ob[me] = pb[me]


def take_pieces(n, pb, ob, s2, r2, me):
    others = pl.ds(0, n - 1)
    rcopy(pb.at[others], ob.at[others], s2, r2, {"ctx": me}).wait_recv()


def main_body(n, nh, ndp, nt, names, *refs):
    r = types.SimpleNamespace(**dict(zip(names, refs)))
    ncq = n // 8
    tpc = NT // ncq
    me = lax.axis_index("ctx")
    dp = lax.axis_index("dp")
    hd = lax.axis_index("head")
    ne = n * ndp
    mine = dp * n + me
    half = iota((B, 128), 1) < HEAD_DIM
    lane1 = iota((1, 128), 1)
    blocks = [slice(0, B), slice(B, T)]

    r.hbuf[...] = jnp.zeros_like(r.hbuf)
    r.bbuf[...] = jnp.zeros_like(r.bbuf)
    barrier = pltpu.get_barrier_semaphore()

    def greet(k, carry):
        e = lax.rem(mine + k, ne)
        pl.semaphore_signal(
            barrier, inc=1, device_id={"dp": e // n, "ctx": lax.rem(e, n)}, device_id_type=MESH
        )
        return carry

    lax.fori_loop(1, ne, greet, 0)
    for k in range(1, nh):
        pl.semaphore_signal(
            barrier, inc=1, device_id={"head": lax.rem(hd + k, nh)}, device_id_type=MESH
        )
    zcopy = pltpu.make_async_copy(r.z_hbm.at[0], r.z, r.zs)
    gcopy = pltpu.make_async_copy(r.go_hbm.at[0], r.go, r.gs)
    zcopy.start()
    gcopy.start()

    rate = jnp.exp(column(r.alog[...]))
    bias = column(r.dtb[...])
    tri = (iota((B, B), 0) <= iota((B, B), 1)).astype(F32)
    before = jnp.zeros((8, 1), F32)
    r.cnt[0:8, :] = jnp.zeros((8, 128), F32)
    masks = []
    for c in range(2):
        sl = blocks[c]
        dtv = softplus(r.dtr[0, :, sl].astype(F32) + bias)
        run = dnn_full(-rate * dtv, tri)
        q = dnn(jnp.broadcast_to(r.flg[:, sl].astype(F32), (8, B)), tri)
        rl = run[:, B - 1 : B]
        ql = q[:, B - 1 : B]
        dtte = dtv * jnp.where(q[0:1] == ql[0:1], jnp.exp(rl - run), 0.0)
        fs = jnp.where(q[0:1] == 0.0, jnp.exp(run), 0.0)
        r.dt[c] = dtv
        r.run[c] = run
        a1, a2 = high_low(dtte)
        b1, b2 = high_low(fs)
        r.mt[sl, :] = jnp.concatenate([a1, a2, b1, b2], axis=0).T.astype(BF16)
        dev = q + before
        before = dev[:, B - 1 : B]
        rt = jnp.concatenate([q, dev, jnp.zeros((112, B), F32)], axis=0).T
        r1, r2 = high_low(run)
        r2, r3 = high_low(r2)
        r.rs[sl, :] = jnp.concatenate(
            [r1, r2, r3, jnp.zeros((H, B), F32)], axis=0
        ).T.astype(BF16)
        r.cnt[8 + c * B : 8 + (c + 1) * B, :] = jnp.broadcast_to(rt[:, 8:9], (B, 128))
        ok = (rt[:, 0:1] == q[0:1, :]) & (iota((B, B), 0) >= iota((B, B), 1))
        r.mask[c] = jnp.where(ok, 0.0, -1e30)
    live_masks(r.cnt, r.live)

    row16 = iota((16, 128), 0)
    same = (r.cnt[8 + T - 16 : 8 + T, :] == r.cnt[8 + T - 1 : 8 + T, :])
    for j in range(NT + 4):
        v = r.x[0, T - 16 : T, j * 128 : (j + 1) * 128] if j < NT else r.bc[
            T - 16 : T, j * 128 - D : (j + 1) * 128 - D
        ]
        r.tail[:, j * 128 : (j + 1) * 128] = jnp.where(same, v.astype(F32), 0.0).astype(BF16)

    def bc_weights(j):
        i, sl = j // 2, slice((j % 2) * 128, (j % 2) * 128 + 128)
        return [r.cbw[k, i : i + 1, sl] for k in range(CONV)], r.cbb[i : i + 1, sl]

    def x_weights(ln):
        return [r.cxw[k : k + 1, ln] for k in range(CONV)], r.cxb[0:1, ln]

    def bc_conv(c):
        for j in range(4):
            sl = slice(j * 128, (j + 1) * 128)
            ext = r.ext.at[j]
            if c == 1:
                ext[8 : 8 + T, :] = r.bc[:, sl].astype(F32)
            else:
                ext[8 : 8 + B, :] = r.bc[0:B, sl].astype(F32)
                ext[0:8, :] = r.hbuf[8:16, D + j * 128 : D + (j + 1) * 128].astype(F32)
            u = conv_input(ext, r.live, *bc_weights(j), c * B, B)
            sg = sigmoid(u)
            r.bcc[blocks[c], sl] = (u * sg).astype(BF16)
            r.cdb[blocks[c], sl] = sg * (1.0 + u * (1.0 - sg))

    def x_conv(j, c):
        ln = lanes(j)
        ext = r.ext.at[j % 4]
        if c == 1:
            ext[8 : 8 + T, :] = r.x[0, :, ln].astype(F32)
        else:
            ext[8 : 8 + B, :] = r.x[0, 0:B, ln].astype(F32)
            ext[0:8, :] = r.hbuf[8:16, ln].astype(F32)
        u = conv_input(ext, r.live, *x_weights(ln), c * B, B)
        xc = (u * sigmoid(u)).astype(BF16)
        r.xc[blocks[c], ln] = xc
        dtte = dnn(r.mt[blocks[c], 0 : 2 * H], spread_two(j))
        return (xc.astype(F32) * dtte).astype(BF16)

    def b_turned(g, c):
        return r.bcc[blocks[c], g * 128 : (g + 1) * 128].astype(F32).T.astype(BF16)

    def keep_row(j, c):
        return dnn(r.mt[(c + 1) * B - 16 : (c + 1) * B, 2 * H : 4 * H], spread_two(j))[15:16]

    bc_conv(1)
    for g in range(NG):
        bt = b_turned(g, 1)

        def second(jj, carry, g=g, bt=bt):
            j = g * TPG + jj
            r.fr[1, :, lanes(j)] = dnn(bt, x_conv(j, 1))
            return carry

        lax.fori_loop(0, TPG, second, 0, unroll=4)
        if g == 0:
            pl.semaphore_wait(barrier, ne - 1 + nh - 1)
            halo = rcopy(r.tail, r.hbuf, r.sh, r.rh, {"ctx": lax.rem(me + 1, n)})

            @pl.when(me < n - 1)
            def _():
                halo.start()

    @pl.when(me > 0)
    def _():
        halo.wait_recv()

    bc_conv(0)
    bts = [b_turned(g, 0) for g in range(NG)]
    for cq in range(ncq):
        bt = bts[cq * tpc // TPG]

        def first(jj, carry, cq=cq, bt=bt):
            j = cq * tpc + jj
            ln = lanes(j)
            fresh = dnn(bt, x_conv(j, 0))
            r.fr[0, :, ln] = fresh
            k1 = keep_row(j, 1)
            put_state(r.st, j, n, (k1 * fresh + r.fr[1, :, ln]).astype(BF16))
            r.kr[cq, :, lanes(jj)] = keep_row(j, 0) * k1
            return carry

        lax.fori_loop(0, tpc, first, 0, unroll=4)
        send_pieces(n, r.st, r.rb, r.s1, r.r1, cq, me)

        def send_row(rz, carry, cq=cq):
            to = rz * ncq + cq

            @pl.when(to != me)
            def _():
                rcopy(r.kr.at[cq], r.kb.at[me], r.sk, r.rk, {"ctx": to}).start()

            return carry

        lax.fori_loop(0, 8, send_row, 0)

    def group_parts(g, c):
        return (
            r.bcc[blocks[c], g * 128 : (g + 1) * 128],
            r.bcc[blocks[c], 256 + g * 128 : 256 + (g + 1) * 128],
        )

    for g in range(NG):
        for c in range(2):
            bb, cc = group_parts(g, c)
            r.gm[...] = dnt(cc, bb)

            def inside(jj, carry, g=g, c=c):
                j = g * TPG + jj
                ln = lanes(j)
                rb2 = dnn(r.rs[blocks[c], :], spread_pair(j))
                ws = []
                for i in range(2):
                    h = 2 * j + i
                    lm = jnp.exp(
                        rb2[:, i * B : (i + 1) * B] - r.run[c, pl.ds(h, 1), :] + r.mask[c]
                    ) * r.dt[c, pl.ds(h, 1), :]
                    r.lm[2 * j + c, i * B : (i + 1) * B, :] = lm
                    wv = (r.gm[...] * lm).astype(BF16)
                    r.wm[2 * j + c, i * B : (i + 1) * B, :] = wv
                    ws.append(wv)
                xt = r.xc[blocks[c], ln]
                zero = jnp.zeros_like(xt)
                xbd = jnp.concatenate(
                    [jnp.where(half, xt, zero), jnp.where(half, zero, xt)], axis=0
                )
                r.y[blocks[c], ln] = dnn(jnp.concatenate(ws, axis=1), xbd)
                return carry

            lax.fori_loop(0, TPG, inside, 0, unroll=4)

    r.kb[me] = r.kr[lax.rem(me, ncq)]

    others = pl.ds(0, n - 1)
    rcopy(r.kb.at[others], r.kb.at[others], r.sk, r.rk, {"ctx": me}).wait_recv()
    owner_scan(n, r.st, r.rb, r.pb, r.ob, r.kb, r.s1, r.r1, r.s2, r.r2, me, False)

    zcopy.wait()
    gcopy.wait()

    def prepare(j, carry):
        ln = lanes(j)
        zf = r.z[:, ln].astype(F32)
        sg = sigmoid(zf)
        r.gate[:, ln] = zf * sg
        r.dgate[:, ln] = sg * (1.0 + zf * (1.0 - sg))
        ext = r.ext.at[j % 4]
        ext[8 : 8 + T, :] = r.x[0, :, ln].astype(F32)
        ext[0:8, :] = r.hbuf[8:16, ln].astype(F32)
        for c in range(2):
            u = conv_input(ext, r.live, *x_weights(ln), c * B, B)
            sg = sigmoid(u)
            r.cdx[blocks[c], ln] = sg * (1.0 + u * (1.0 - sg))
        return carry

    lax.fori_loop(0, NT, prepare, 0, unroll=2)
    take_pieces(n, r.pb, r.ob, r.s2, r.r2, me)

    r.sums_acc[...] = jnp.zeros_like(r.sums_acc)

    def skip_row(j):
        return jnp.where(lane1 < HEAD_DIM, r.skip[2 * j], r.skip[2 * j + 1])

    for g in range(NG):
        ccs = [group_parts(g, c)[1] for c in range(2)]

        def outputs(jj, carry, g=g, ccs=ccs):
            j = g * TPG + jj
            ln = lanes(j)
            fs = dnn(r.mt[:, 2 * H : 4 * H], spread_two(j))
            sb0 = row_state(r.ob, j, n, 0)
            sb1 = (fs[B - 1 : B] * sb0.astype(F32) + r.fr[0, :, ln]).astype(BF16)
            r.sb1[:, ln] = sb1
            for c in range(2):
                sl = blocks[c]
                y = r.y[sl, ln] + dnn(ccs[c], sb0 if c == 0 else sb1) * fs[sl]
                r.y[sl, ln] = y
                mixed = (y + skip_row(j) * r.xc[sl, ln].astype(F32)).astype(BF16)
                r.mixed[sl, ln] = mixed
                gated = mixed.astype(F32) * r.gate[sl, ln]
                gained = r.go[sl, ln].astype(F32) * r.gain[0:1, ln]
                r.sums_acc[0, sl, :] += gated * gated
                r.sums_acc[1, sl, :] += gated * gained
            return carry

        lax.fori_loop(0, TPG, outputs, 0, unroll=4)
    ones = jnp.ones((8, 128), F32)
    r.sums[0:8, :] = dnt_full(ones, r.sums_acc[0])
    r.sums[8:16, :] = dnt_full(ones, r.sums_acc[1])
    copies = []
    for k in range(1, nh):
        copies.append(
            rcopy(r.sums, r.sbuf.at[k], r.hs.at[k], r.hr.at[k], {"head": lax.rem(hd + k, nh)})
        )
        copies[-1].start()
    for cp in copies:
        cp.wait()
    parts = [r.sums[...]] + [r.sbuf[k] for k in range(1, nh)]
    total = jnp.zeros_like(parts[0])
    for d in range(nh):
        for k in range(nh):
            total = total + jnp.where(lax.rem(hd - k + nh, nh) == d, parts[k], 0.0)
    inv = lax.rsqrt(total[0:8] / INNER + EPS)
    coef = inv * inv * inv * total[8:16] / INNER
    for c in range(2):
        sl = blocks[c]
        tr = jnp.concatenate([inv[:, sl], coef[:, sl], jnp.zeros((112, B), F32)], axis=0).T
        r.inv[sl, :] = jnp.broadcast_to(tr[:, 0:1], (B, 128))
        r.coef[sl, :] = jnp.broadcast_to(tr[:, 8:9], (B, 128))

    r.rho[...] = jnp.zeros_like(r.rho)
    r.skc[...] = jnp.zeros_like(r.skc)
    cts = [[group_parts(g, c)[1].astype(F32).T.astype(BF16) for c in range(2)] for g in range(NG)]
    for cq in range(ncq):
        ct = cts[cq * tpc // TPG]

        def gates(jj, carry, cq=cq, ct=ct):
            j = cq * tpc + jj
            ln = lanes(j)
            e2 = spread_two(j)
            grow = jnp.zeros((1, 128), F32)
            srow = jnp.zeros((1, 128), F32)
            ds = []
            for c in range(2):
                sl = blocks[c]
                m = r.mixed[sl, ln].astype(F32)
                gt = r.gate[sl, ln]
                go = r.go[sl, ln].astype(F32)
                gated = m * gt
                iv = r.inv[sl, :]
                dg = go * r.gain[0:1, ln] * iv - gated * r.coef[sl, :]
                grow = grow + jnp.sum(go * gated * iv, axis=0, keepdims=True)
                r.dz[sl, ln] = (dg * m * r.dgate[sl, ln]).astype(BF16)
                dm = (dg * gt).astype(BF16)
                r.dy[sl, ln] = dm
                dy = dm.astype(F32)
                srow = srow + jnp.sum(dy * r.xc[sl, ln].astype(F32), axis=0, keepdims=True)
                r.rho[:, sl] += head_sums(j, dy * r.y[sl, ln])
                fs = dnn(r.mt[sl, 2 * H : 4 * H], e2)
                if c == 1:
                    k0 = keep_row(j, 0)
                fd = (fs * dy).astype(BF16)
                r.fd[sl, ln] = fd
                ds.append(dnn(ct[c], fd).astype(BF16))
            r.dsb1[:, ln] = ds[1]
            put_state(
                r.ad, j, n, (k0 * ds[1].astype(F32) + ds[0].astype(F32)).astype(BF16)
            )
            r.pk[j, 5:6, :] = grow
            r.pk[j, 6:8, :] = jnp.zeros((2, 128), F32)
            r.skc[...] += head_sums(j, jnp.broadcast_to(srow, (8, 128)))
            return carry

        lax.fori_loop(0, tpc, gates, 0, unroll=4)
        send_pieces(n, r.ad, r.rb2, r.s3, r.r3, cq, me)

    for g in range(NG):
        r.acc[...] = jnp.zeros_like(r.acc)

        def inner(jj, carry, g=g):
            j = g * TPG + jj
            ln = lanes(j)
            for c in range(2):
                sl = blocks[c]
                dyt = r.dy[sl, ln]
                zero = jnp.zeros_like(dyt)
                dybd = jnp.concatenate(
                    [jnp.where(half, dyt, zero), jnp.where(half, zero, dyt)], axis=0
                )
                dw = dnt(dybd, r.xc[sl, ln])
                i = 2 * j + c
                r.acc[0, c] += dw[0:B] * r.lm[i, 0:B, :] + dw[B : 2 * B] * r.lm[i, B : 2 * B, :]
                r.y[sl, ln] = dtn(r.wm[i], dybd)
                sp = row_state(r.ob, j, n, 0) if c == 0 else r.sb1[:, ln]
                r.acc[1, c] += dnt(r.fd[sl, ln], sp)
            return carry

        lax.fori_loop(0, TPG, inner, 0, unroll=4)
        for c in range(2):
            bb, cc = group_parts(g, c)
            dg = r.acc[0, c].astype(BF16)
            r.dbc[blocks[c], g * 128 : (g + 1) * 128] = dtn(dg, cc)
            r.dbc[blocks[c], 256 + g * 128 : 256 + (g + 1) * 128] = r.acc[1, c] + dnn(dg, bb)
        if g == 0:
            owner_scan(n, r.ad, r.rb2, r.pb2, r.ob2, r.kb, r.s3, r.r3, r.s4, r.r4, me, True)
    take_pieces(n, r.pb2, r.ob2, r.s4, r.r4, me)

    r.kap[...] = jnp.zeros_like(r.kap)
    r.tl[...] = jnp.zeros_like(r.tl)
    r.vk[:, :, 0:8, :] = jnp.zeros((2, CONV, 8, 128), F32)
    r.vk[:, :, 8 + T :, :] = jnp.zeros((2, CONV, 8, 128), F32)

    def is_owner(j):
        return (me == j) & (dp == lax.rem(j, ndp))

    def give_tile(j):
        @pl.when(jnp.logical_not(is_owner(j)))
        def _():
            rcopy(
                r.pk.at[j], r.prb.at[mine], r.ps, r.pr,
                {"dp": lax.rem(j, ndp), "ctx": j},
            ).start()

    def conv_back(ext, vk, w, deriv, dxc, j):
        du = dxc.astype(BF16).astype(F32) * deriv
        rows = [jnp.sum(du * ext[8 : 8 + T, :], axis=0, keepdims=True)]
        for k in range(1, CONV):
            v = du * r.live[k - 1]
            rows.append(jnp.sum(v * ext[8 - k : 8 - k + T, :], axis=0, keepdims=True))
            vk[k, 8 : 8 + T, :] = v
        rows.append(jnp.sum(du, axis=0, keepdims=True))
        own = w[0] * du
        prior = jnp.zeros((8, 128), F32)
        for k in range(1, CONV):
            own = own + w[k] * vk[k, 8 + k : 8 + k + T, :]
            prior = prior + w[k] * vk[k, k : k + 8, :]
        r.pk[j, 0 : CONV + 1, :] = jnp.concatenate(rows, axis=0)
        return own, prior

    for g in range(NG):
        r.acc[1] = jnp.zeros((2, B, 128), F32)

        def outer(jj, carry, g=g):
            j = g * TPG + jj
            ln = lanes(j)
            e2 = spread_two(j)
            a1 = row_state(r.ob2, j, n, 0).astype(F32)
            sk = skip_row(j)
            outs = []
            for c in range(2):
                sl = blocks[c]
                if c == 1:
                    ds = a1
                    sp = r.sb1[:, ln]
                else:
                    ds = keep_row(j, 1) * a1 + r.dsb1[:, ln].astype(F32)
                    sp = row_state(r.ob, j, n, 0)
                dsh = ds.astype(BF16)
                xf = r.xc[sl, ln].astype(F32)
                dtte = dnn(r.mt[sl, 0 : 2 * H], e2)
                dxu = dnn(r.bcc[sl, g * 128 : (g + 1) * 128], dsh) * dtte
                r.acc[1, c] += dnt((xf * dtte).astype(BF16), dsh)
                dxs = r.y[sl, ln] + dxu
                ku = jnp.sum(xf * dxu, axis=0, keepdims=True)
                kd = jnp.sum(ds * sp.astype(F32), axis=0, keepdims=True) * keep_row(j, c)
                hs = head_sums(
                    j, jnp.concatenate([xf * dxs, jnp.broadcast_to(ku + kd, (8, 128))], axis=0)
                )
                r.kap[:, sl] += hs[:, 0:B]
                r.tl[:, c * 8 : (c + 1) * 8] += hs[:, B : B + 8]
                outs.append(dxs + sk * r.dy[sl, ln].astype(F32))
            ext = r.ext.at[j % 4]
            ext[8 : 8 + T, :] = r.x[0, :, ln].astype(F32)
            ext[0:8, :] = r.hbuf[8:16, ln].astype(F32)
            own, prior = conv_back(
                ext, r.vk.at[j % 2], x_weights(ln)[0], r.cdx[:, ln],
                jnp.concatenate(outs, axis=0), j,
            )
            r.gx[:, ln] = own.astype(BF16)
            r.tails[:, ln] = own[T - 16 : T]
            r.hb[:, ln] = prior
            give_tile(j)
            return carry

        lax.fori_loop(0, TPG, outer, 0, unroll=2)
        for c in range(2):
            r.dbc[blocks[c], g * 128 : (g + 1) * 128] += r.acc[1, c]

    for j in range(4):
        sl = slice(j * 128, (j + 1) * 128)
        sd = slice(D + j * 128, D + (j + 1) * 128)
        ext = r.ext.at[j]
        ext[8 : 8 + T, :] = r.bc[:, sl].astype(F32)
        ext[0:8, :] = r.hbuf[8:16, sd].astype(F32)
        own, prior = conv_back(
            ext, r.vk.at[j % 2], bc_weights(j)[0], r.cdb[:, sl], r.dbc[:, sl], NT + j
        )
        r.pk[NT + j, 5:8, :] = jnp.zeros((3, 128), F32)
        r.gbc[:, sl] = own.astype(BF16)
        r.tails[:, sd] = own[T - 16 : T]
        r.hb[:, sd] = prior
        give_tile(NT + j)
    back = rcopy(r.hb, r.bbuf, r.sb, r.rb_sem, {"ctx": lax.rem(me + n - 1, n)})

    @pl.when(me > 0)
    def _():
        back.start()

    rev = (iota((B, B), 0) >= iota((B, B), 1)).astype(F32)
    rate_sum = jnp.zeros((H, B), F32)
    bias_sum = jnp.zeros((H, B), F32)
    for c in range(2):
        sl = blocks[c]
        dtv = r.dt[c]
        kp = r.kap[:, sl]
        rr = dnn_full(r.rho[:, sl] - kp, rev) + r.tl[:, c * 8 : c * 8 + 1]
        gd = (kp / dtv - rate * rr) * sigmoid(r.dtr[0, :, sl].astype(F32) + bias)
        r.gdt[:, sl] = gd
        rate_sum = rate_sum - rate * dtv * rr
        bias_sum = bias_sum + gd
    skips = jnp.where(iota((H, B), 1) == 0, r.skc[:, 0:1], 0.0)
    r.pk[nt - 1] = dnt_full(
        ones, jnp.concatenate([rate_sum, bias_sum, skips, jnp.zeros((H, B), F32)], axis=0)
    )
    give_tile(nt - 1)

    @pl.when((me < nt) & (dp == lax.rem(me, ndp)))
    def _():
        r.prb[mine] = r.pk[me]

        alls = pl.ds(0, ne - 1)
        rcopy(r.prb.at[alls], r.prb.at[alls], r.ps, r.pr, {"ctx": me}).wait_recv()

        def collect(e, total):
            return total + r.prb[e]

        r.pob[me] = lax.fori_loop(0, ne, collect, jnp.zeros((8, 128), F32), unroll=8)

        def give(k, carry):
            e = lax.rem(mine + k, ne)
            rcopy(
                r.pob.at[me], r.pob.at[me], r.as_, r.ar,
                {"dp": e // n, "ctx": lax.rem(e, n)},
            ).start()
            return carry

        lax.fori_loop(1, ne, give, 0)

    @pl.when(me < n - 1)
    def _():
        halo.wait_send()
        back.wait_recv()

    @pl.when(me > 0)
    def _():
        back.wait_send()

    rcopy(r.kb.at[others], r.kb.at[others], r.sk, r.rk, {"ctx": me}).wait_send()
    for sent in (r.s1, r.s2, r.s3, r.s4):
        rcopy(r.st.at[others], r.rb.at[others], sent, sent, {"ctx": me}).wait_send()

    owns = (me < nt) & (dp == lax.rem(me, ndp))

    @pl.when(owns)
    def _():
        alls = pl.ds(0, ne - 1)
        most = pl.ds(0, nt - 1)
        rcopy(r.prb.at[alls], r.prb.at[alls], r.as_, r.ar, {"ctx": me}).wait_send()
        rcopy(r.pk.at[most], r.pob.at[most], r.ps, r.ar, {"ctx": me}).wait()

    @pl.when(jnp.logical_not(owns))
    def _():
        rcopy(r.pk, r.pob, r.ps, r.ar, {"ctx": me}).wait()

    r.red[...] = r.pob[...]
    r.rh_o[...] = r.bbuf[...]


def k5_body(scale, red, rh, tail, flg, gx_in, gbc_in,
            gx_o, gbc_o, cw_o, cb_o, bw_o, bb_o, al_o, db_o, sk_o, ga_o):
    f = flg[:, B:T].astype(F32)
    lane = iota((1, B), 1)
    last = jnp.sum(jnp.where(lane == B - 1, f, 0.0))
    two = jnp.sum(jnp.where(lane >= B - 2, f, 0.0))
    row = iota((16, 128), 0)
    keep = jnp.where(row == 15, 1.0, 0.0)
    keep = keep + jnp.where((row == 14) & (last == 0.0), 1.0, 0.0)
    keep = keep + jnp.where((row == 13) & (two == 0.0), 1.0, 0.0)
    for j in range(NT + 4):
        sl = slice(j * 128, (j + 1) * 128)
        add = jnp.concatenate([jnp.zeros((8, 128), F32), rh[:, sl]], axis=0)
        v = (tail[:, sl] + add * keep).astype(BF16)
        t = red[j] * scale
        if j < NT:
            gx_o[:, sl] = v
            cw_o[:, sl] = t[0:4]
            cb_o[:, sl] = t[4:5]
            ga_o[:, sl] = t[5:6]
        else:
            so = slice(j * 128 - D, (j + 1) * 128 - D)
            gbc_o[:, so] = v
            i, sb = (j - NT) // 2, slice(((j - NT) % 2) * 128, ((j - NT) % 2) * 128 + 128)
            for k in range(CONV):
                bw_o[k, i : i + 1, sb] = t[k : k + 1]
            bb_o[i : i + 1, sb] = t[4:5]
    last_tile = red[NT + 4] * scale
    al_o[...] = last_tile[0:1, 0:H]
    db_o[...] = last_tile[0:1, H : 2 * H]
    sk_o[...] = last_tile[0:1, 2 * H : 3 * H]


def sds(*shape, dtype=F32):
    return jax.ShapeDtypeStruct(shape, dtype)


def per_device(
    x_raw, bc_raw, z_gate, dt_raw, resets, conv_x_weight, conv_x_bias, conv_bc_weight,
    conv_bc_bias, a_log, dt_bias, skip_weight, norm_gain, grad_out,
):
    n = lax.axis_size("ctx")
    nh = lax.axis_size("head")
    ndp = lax.axis_size("dp")
    ncq = n // 8
    w = D // ncq
    nt = NT + 5
    ne = n * ndp
    ANY = pl.BlockSpec(memory_space=pl.ANY)
    ins = [
        ("x", x_raw, VM), ("bc", bc_raw[0].reshape(T, DB), VM), ("z_hbm", z_gate, ANY),
        ("go_hbm", grad_out, ANY), ("dtr", dt_raw, VM), ("flg", resets, VM),
        ("alog", a_log.reshape(1, H), VM), ("dtb", dt_bias.reshape(1, H), VM),
        ("cxw", conv_x_weight, VM), ("cxb", conv_x_bias.reshape(1, D), VM),
        ("cbw", conv_bc_weight, VM), ("cbb", conv_bc_bias, VM),
        ("gain", norm_gain.reshape(1, D), VM), ("skip", skip_weight, SM),
    ]
    outs = [
        ("gx", sds(T, D, dtype=BF16)), ("gbc", sds(T, DB, dtype=BF16)),
        ("dz", sds(T, D, dtype=BF16)), ("gdt", sds(H, T)), ("tails", sds(16, D + DB)),
        ("red", sds(nt, 8, 128)), ("rh_o", sds(8, D + DB)),
    ]
    V = pltpu.VMEM
    dma = pltpu.SemaphoreType.DMA
    state = V((n, ROWS, w), BF16)
    scratch = [
        ("z", V((T, D), BF16)), ("go", V((T, D), BF16)), ("zs", dma), ("gs", dma),
        ("ext", V((4, T + 8, 128), F32)), ("cnt", V((T + 8, 128), F32)),
        ("live", V((CONV - 1, T, 128), F32)), ("mask", V((2, B, B), F32)),
        ("dt", V((2, H, B), F32)), ("run", V((2, H, B), F32)), ("mt", V((T, 128), BF16)),
        ("rs", V((T, 128), BF16)), ("tail", V((16, D + DB), BF16)),
        ("hbuf", V((16, D + DB), BF16)), ("xc", V((T, D), BF16)), ("bcc", V((T, DB), BF16)),
        ("cdb", V((T, DB), F32)), ("cdx", V((T, D), F32)), ("fr", V((2, NSTATE, D), F32)),
        ("kr", V((ncq, 1, w), F32)), ("kb", V((n, 1, w), F32)), ("gm", V((B, B), F32)),
        ("lm", V((2 * NT, 2 * B, B), F32)), ("wm", V((2 * NT, 2 * B, B), BF16)),
        ("y", V((T, D), F32)), ("gate", V((T, D), F32)), ("dgate", V((T, D), F32)),
        ("mixed", V((T, D), BF16)), ("sb1", V((NSTATE, D), BF16)),
        ("sums_acc", V((2, T, 128), F32)), ("sums", V((16, T), F32)),
        ("sbuf", V((nh, 16, T), F32)), ("inv", V((T, 128), F32)), ("coef", V((T, 128), F32)),
        ("rho", V((H, T), F32)), ("skc", V((H, 8), F32)), ("dy", V((T, D), BF16)),
        ("fd", V((T, D), BF16)), ("dsb1", V((NSTATE, D), BF16)), ("acc", V((2, 2, B, 128), F32)),
        ("dbc", V((T, DB), F32)), ("kap", V((H, T), F32)), ("tl", V((H, 16), F32)),
        ("vk", V((2, CONV, T + 16, 128), F32)), ("pk", V((nt, 8, 128), F32)),
        ("prb", V((ne, 8, 128), F32)), ("pob", V((nt, 8, 128), F32)),
        ("hb", V((8, D + DB), F32)), ("bbuf", V((8, D + DB), F32)),
        ("st", state), ("rb", state), ("pb", state), ("ob", state),
        ("ad", state), ("rb2", state), ("pb2", state), ("ob2", state),
        ("sh", dma), ("rh", dma), ("sb", dma), ("rb_sem", dma),
        ("hs", dma((nh,))), ("hr", dma((nh,))),
    ]
    scratch += [
        (k, dma)
        for k in (
            "s1", "r1", "s2", "r2", "s3", "r3", "s4", "r4", "sk", "rk", "ps", "ar", "pr", "as_"
        )
    ]
    names = [v[0] for v in ins] + [v[0] for v in outs] + [v[0] for v in scratch]
    gx, gbc, dz, gdt, tails, red, rh = pl.pallas_call(
        functools.partial(main_body, n, nh, ndp, nt, names),
        out_shape=[v[1] for v in outs],
        in_specs=[v[2] for v in ins],
        out_specs=[VM] * len(outs),
        scratch_shapes=[v[1] for v in scratch],
        compiler_params=pltpu.CompilerParams(
            vmem_limit_bytes=VLIM, collective_id=0, has_side_effects=True
        ),
    )(*[v[1] for v in ins])
    scale = float(ndp * n * T) ** (-0.5)
    whole = lambda *s: pl.BlockSpec(s, lambda i: (0,) * len(s))
    outs = pl.pallas_call(
        functools.partial(k5_body, scale),
        grid=(1,),
        out_shape=(
            sds(T, D, dtype=BF16), sds(T, DB, dtype=BF16), sds(CONV, D), sds(1, D),
            sds(CONV, 2, DB // 2), sds(2, DB // 2), sds(1, H), sds(1, H), sds(1, H), sds(1, D),
        ),
        in_specs=[
            whole(nt, 8, 128), whole(8, D + DB), whole(16, D + DB), whole(1, T),
            pl.BlockSpec(memory_space=pl.ANY), pl.BlockSpec(memory_space=pl.ANY),
        ],
        out_specs=[
            pl.BlockSpec((16, D), lambda i: (T // 16 - 1, 0)),
            pl.BlockSpec((16, DB), lambda i: (T // 16 - 1, 0)),
            whole(CONV, D), whole(1, D), whole(CONV, 2, DB // 2), whole(2, DB // 2),
            whole(1, H), whole(1, H), whole(1, H), whole(1, D),
        ],
        input_output_aliases={4: 0, 5: 1},
    )(red, rh, tails, resets, gx, gbc)
    gx, gbc, cw, cb, bw, bb, al, db, sk, ga = outs
    return (
        gx[None], gbc.reshape(1, T, 2, DB // 2), dz[None], gdt[None], cw, cb.reshape(D),
        bw, bb, al.reshape(H), db.reshape(H), sk.reshape(H), ga.reshape(D),
    )


def solution(mesh):
    return jax.shard_map(
        per_device,
        mesh=mesh,
        in_specs=(
            P("dp", "ctx", "head"),
            P("dp", "ctx", None, "head"),
            P("dp", "ctx", "head"),
            P("dp", "head", "ctx"),
            P("dp", "ctx"),
            P(None, "head"),
            P("head"),
            P(None, None, "head"),
            P(None, "head"),
            P("head"),
            P("head"),
            P("head"),
            P("head"),
            P("dp", "ctx", "head"),
        ),
        out_specs=(
            P("dp", "ctx", "head"),
            P("dp", "ctx", None, "head"),
            P("dp", "ctx", "head"),
            P("dp", "head", "ctx"),
            P(None, "head"),
            P("head"),
            P(None, None, "head"),
            P(None, "head"),
            P("head"),
            P("head"),
            P("head"),
            P("head"),
        ),
        check_vma=False,
    )
```

```python
import functools

import types

import jax
import jax.numpy as jnp
from jax import lax
from jax.experimental import pallas as pl
from jax.experimental.pallas import tpu as pltpu
from jax.sharding import PartitionSpec as P

F32 = jnp.float32
BF16 = jnp.bfloat16
HIGHEST = lax.Precision.HIGHEST
MESH = pl.DeviceIdType.MESH

HEAD_DIM = 64
NSTATE = 128
CONV = 4
INNER = 8192
EPS = 1e-05

T = 256
B = 128
H = 32
D = 2048
DB = 512
NT = D // 128
NG = 2
TPG = NT // NG
ROWS = 16
VM = pl.BlockSpec(memory_space=pltpu.VMEM)
SM = pl.BlockSpec(memory_space=pltpu.SMEM)
VLIM = 60 * 1024 * 1024


def dnn(a, b):
    return lax.dot_general(a, b, (((1,), (0,)), ((), ())), preferred_element_type=F32)


def dnt(a, b):
    return lax.dot_general(a, b, (((1,), (1,)), ((), ())), preferred_element_type=F32)


def dtn(a, b):
    return lax.dot_general(a, b, (((0,), (0,)), ((), ())), preferred_element_type=F32)


def dnn_full(a, b):
    return lax.dot_general(
        a, b, (((1,), (0,)), ((), ())), precision=HIGHEST, preferred_element_type=F32
    )


def dnt_full(a, b):
    return lax.dot_general(
        a, b, (((1,), (1,)), ((), ())), precision=HIGHEST, preferred_element_type=F32
    )


def iota(shape, dim):
    return lax.broadcasted_iota(jnp.int32, shape, dim)


def high_low(v):
    high = v.astype(BF16).astype(F32)
    return high, v - high


def sigmoid(v):
    return 1.0 / (1.0 + jnp.exp(-v))


def softplus(v):
    y = jnp.exp(-jnp.abs(v))
    series = y * (1.0 - y * (0.5 - y * (1.0 / 3.0 - y * (0.25 - 0.2 * y))))
    return jnp.maximum(v, 0.0) + jnp.where(y < 0.02, series, jnp.log(1.0 + y))


def lanes(j):
    return pl.ds(pl.multiple_of(j * 128, 128), 128)


def spread_two(j):
    row = iota((2 * H, 128), 0) % H
    lane = iota((2 * H, 128), 1)
    return (row == 2 * j + lane // HEAD_DIM).astype(BF16)


def spread_pair(j):
    row = iota((128, 256), 0)
    lane = iota((128, 256), 1)
    return ((row % H == 2 * j + lane // 128) & (row < 3 * H)).astype(BF16)


def conv_input(ext, live, w, bias, lo, rows):
    u = bias + w[0] * ext[8 + lo : 8 + lo + rows, :]
    for k in range(1, CONV):
        u = u + w[k] * ext[8 - k + lo : 8 - k + lo + rows, :] * live[k - 1, lo : lo + rows, :]
    return u


def live_masks(cnt, live):
    now = cnt[8 : 8 + T, :]
    for k in range(1, CONV):
        live[k - 1] = (now == cnt[8 - k : 8 - k + T, :]).astype(F32)


def row_state(ref, jj, n):
    ncq = n // 8
    tpc = TPG // ncq
    cq = jj // tpc
    lane = lanes(jj % tpc)
    return jnp.concatenate([ref[rz * ncq + cq, :, lane] for rz in range(8)], axis=0)


def put_state(ref, jj, n, v):
    ncq = n // 8
    tpc = TPG // ncq
    cq = jj // tpc
    lane = lanes(jj % tpc)
    for rz in range(8):
        ref[rz * ncq + cq, :, lane] = v[rz * ROWS : (rz + 1) * ROWS]


def head_rows(v):
    t = v.T
    return (
        jnp.sum(t[0:HEAD_DIM], axis=0, keepdims=True),
        jnp.sum(t[HEAD_DIM:], axis=0, keepdims=True),
    )


def column(row):
    return jnp.concatenate(
        [jnp.broadcast_to(row, (128, H)), jnp.zeros((128, 128 - H), F32)], axis=1
    ).T[0:H, 0:1]


def rcopy(src, dst, sem_s, sem_r, dev):
    return pltpu.make_async_remote_copy(
        src_ref=src, dst_ref=dst, send_sem=sem_s, recv_sem=sem_r,
        device_id=dev, device_id_type=MESH,
    )


def send_pieces(n, cq, me, st, rb, pb, ob, s1, r1, s2, r2):
    ncq = n // 8

    def send(rz, carry):
        to = rz * ncq + cq

        @pl.when(to != me)
        def _():
            rcopy(st.at[to], rb.at[me], s1, r1, {"ctx": to}).start()

        return carry

    lax.fori_loop(0, 8, send, 0)


def owner_scan(n, half, kb, st, rb, pb, ob, s1, r1, s2, r2, me, backward):
    rb[me] = st[me]
    others = pl.ds(0, n - 1)
    rcopy(st.at[others], rb.at[others], s1, r1, {"ctx": me}).wait_recv()

    def step(i, acc):
        d = n - 1 - i if backward else i

        pb[d] = acc.astype(BF16)

        @pl.when(d != me)
        def _():
            rcopy(pb.at[d], ob.at[me], s2, r2, {"ctx": d}).start()

        return kb[d, :, half] * acc + rb[d].astype(F32)

    lax.fori_loop(0, n, step, jnp.zeros(rb.shape[1:], F32))
    ob[me] = pb[me]


def take_pieces(n, me, st, rb, pb, ob, s1, r1, s2, r2):
    others = pl.ds(0, n - 1)
    rcopy(pb.at[others], ob.at[others], s2, r2, {"ctx": me}).wait_recv()


def main_body(n, nh, ndp, nt, names, *refs):
    r = types.SimpleNamespace(**dict(zip(names, refs)))
    ncq = n // 8
    wh = TPG * 128 // ncq
    me = lax.axis_index("ctx")
    dp = lax.axis_index("dp")
    hd = lax.axis_index("head")
    ne = n * ndp
    mine = dp * n + me
    half = iota((B, 128), 1) < HEAD_DIM
    lane1 = iota((1, 128), 1)
    blocks = [slice(0, B), slice(B, T)]
    halves = [slice(g * wh, (g + 1) * wh) for g in range(NG)]
    parts = ("st", "rb", "pb", "ob", "s1", "r1", "s2", "r2")
    fwd = [[getattr(r, k + "f" + str(g)) for k in parts] for g in range(NG)]
    bwd = [[getattr(r, k + "b" + str(g)) for k in parts] for g in range(NG)]
    states = [f[3] for f in fwd]
    laters = [f[3] for f in bwd]

    r.hbuf[...] = jnp.zeros_like(r.hbuf)
    r.bbuf[...] = jnp.zeros_like(r.bbuf)
    barrier = pltpu.get_barrier_semaphore()

    def greet(k, carry):
        e = lax.rem(mine + k, ne)
        pl.semaphore_signal(
            barrier, inc=1, device_id={"dp": e // n, "ctx": lax.rem(e, n)}, device_id_type=MESH
        )
        return carry

    lax.fori_loop(1, ne, greet, 0)
    for k in range(1, nh):
        pl.semaphore_signal(
            barrier, inc=1, device_id={"head": lax.rem(hd + k, nh)}, device_id_type=MESH
        )
    zcopy = pltpu.make_async_copy(r.z_hbm.at[0], r.z, r.zs)
    gcopy = pltpu.make_async_copy(r.go_hbm.at[0], r.go, r.gs)
    zcopy.start()
    gcopy.start()
    r.bc[...] = r.bc_raw[0].reshape(T, DB)
    r.hsr[...] = jnp.zeros_like(r.hsr)

    rate = jnp.exp(column(r.alog[...]))
    bias = column(r.dtb[...])
    tri = (iota((B, B), 0) <= iota((B, B), 1)).astype(F32)
    before = jnp.zeros((8, 1), F32)
    r.cnt[0:8, :] = jnp.zeros((8, 128), F32)
    masks = []
    for c in range(2):
        sl = blocks[c]
        dtv = softplus(r.dtr[0, :, sl].astype(F32) + bias)
        run = dnn_full(-rate * dtv, tri)
        q = dnn(jnp.broadcast_to(r.flg[:, sl].astype(F32), (8, B)), tri)
        rl = run[:, B - 1 : B]
        ql = q[:, B - 1 : B]
        dtte = dtv * jnp.where(q[0:1] == ql[0:1], jnp.exp(rl - run), 0.0)
        fs = jnp.where(q[0:1] == 0.0, jnp.exp(run), 0.0)
        r.dt[c] = dtv
        r.run[c] = run
        a1, a2 = high_low(dtte)
        b1, b2 = high_low(fs)
        r.mt[sl, :] = jnp.concatenate([a1, a2, b1, b2], axis=0).T.astype(BF16)
        dev = q + before
        before = dev[:, B - 1 : B]
        rt = jnp.concatenate([q, dev, jnp.zeros((112, B), F32)], axis=0).T
        r1, r2 = high_low(run)
        r2, r3 = high_low(r2)
        r.rs[sl, :] = jnp.concatenate(
            [r1, r2, r3, jnp.zeros((H, B), F32)], axis=0
        ).T.astype(BF16)
        r.cnt[8 + c * B : 8 + (c + 1) * B, :] = jnp.broadcast_to(rt[:, 8:9], (B, 128))
        ok = (rt[:, 0:1] == q[0:1, :]) & (iota((B, B), 0) >= iota((B, B), 1))
        r.mask[c] = jnp.where(ok, 0.0, -1e30)
    live_masks(r.cnt, r.live)

    def keeps(j, carry):
        e2 = spread_two(j)
        k0, k1 = [
            dnn(r.mt[(c + 1) * B - 16 : (c + 1) * B, 2 * H : 4 * H], e2)[15:16] for c in range(2)
        ]
        r.krow[0, :, lanes(j)] = k0
        r.krow[1, :, lanes(j)] = k1
        tpc = TPG // ncq
        jj = j % TPG
        r.kr[jj // tpc, :, lanes((j // TPG) * tpc + jj % tpc)] = k0 * k1
        return carry

    lax.fori_loop(0, NT, keeps, 0, unroll=4)

    row16 = iota((16, 128), 0)
    same = (r.cnt[8 + T - 16 : 8 + T, :] == r.cnt[8 + T - 1 : 8 + T, :])
    for j in range(NT + 4):
        v = r.x[0, T - 16 : T, j * 128 : (j + 1) * 128] if j < NT else r.bc[
            T - 16 : T, j * 128 - D : (j + 1) * 128 - D
        ]
        r.tail[:, j * 128 : (j + 1) * 128] = jnp.where(same, v.astype(F32), 0.0).astype(BF16)

    def bc_weights(j):
        i, sl = j // 2, slice((j % 2) * 128, (j % 2) * 128 + 128)
        return [r.cbw[k, i : i + 1, sl] for k in range(CONV)], r.cbb[i : i + 1, sl]

    def x_weights(ln):
        return [r.cxw[k : k + 1, ln] for k in range(CONV)], r.cxb[0:1, ln]

    def bc_conv(c):
        for j in range(4):
            sl = slice(j * 128, (j + 1) * 128)
            ext = r.ext.at[j]
            if c == 1:
                ext[8 : 8 + T, :] = r.bc[:, sl].astype(F32)
            else:
                ext[8 : 8 + B, :] = r.bc[0:B, sl].astype(F32)
                ext[0:8, :] = r.hbuf[8:16, D + j * 128 : D + (j + 1) * 128].astype(F32)
            u = conv_input(ext, r.live, *bc_weights(j), c * B, B)
            sg = sigmoid(u)
            r.bcc[blocks[c], sl] = (u * sg).astype(BF16)
            r.cdb[blocks[c], sl] = sg * (1.0 + u * (1.0 - sg))

    def x_conv(j, c):
        ln = lanes(j)
        ext = r.ext.at[j % 4]
        if c == 1:
            ext[8 : 8 + T, :] = r.x[0, :, ln].astype(F32)
        else:
            ext[8 : 8 + B, :] = r.x[0, 0:B, ln].astype(F32)
            ext[0:8, :] = r.hbuf[8:16, ln].astype(F32)
        u = conv_input(ext, r.live, *x_weights(ln), c * B, B)
        xc = (u * sigmoid(u)).astype(BF16)
        r.xc[blocks[c], ln] = xc
        dtte = dnn(r.mt[blocks[c], 0 : 2 * H], spread_two(j))
        uu = (xc.astype(F32) * dtte).astype(BF16)
        r.uu[blocks[c], ln] = uu
        return uu

    def b_turned(g, c):
        return r.bcc[blocks[c], g * 128 : (g + 1) * 128].astype(F32).T.astype(BF16)

    bc_conv(1)
    for g in range(NG):
        bt = b_turned(g, 1)

        def second(jj, carry, g=g, bt=bt):
            j = g * TPG + jj
            r.fr[1, :, lanes(j)] = dnn(bt, x_conv(j, 1))
            return carry

        lax.fori_loop(0, TPG, second, 0, unroll=4)
        if g == 0:
            pl.semaphore_wait(barrier, ne - 1 + nh - 1)
            halo = rcopy(r.tail, r.hbuf, r.sh, r.rh, {"ctx": lax.rem(me + 1, n)})

            @pl.when(me < n - 1)
            def _():
                halo.start()

            def send_row(k, carry):
                to = lax.rem(me + k, n)
                rcopy(
                    r.kr.at[lax.rem(to, ncq)], r.kb.at[me], r.sk, r.rk, {"ctx": to}
                ).start()
                return carry

            lax.fori_loop(1, n, send_row, 0)

    @pl.when(me > 0)
    def _():
        halo.wait_recv()

    bc_conv(0)
    for g in range(NG):
        bt = b_turned(g, 0)
        for hf in range(2):

            def first(i, carry, g=g, hf=hf, bt=bt):
                jj = hf * 4 + i
                j = g * TPG + jj
                ln = lanes(j)
                fresh = dnn(bt, x_conv(j, 0))
                r.fr[0, :, ln] = fresh
                put_state(
                    fwd[g][0], jj, n, (r.krow[1, :, ln] * fresh + r.fr[1, :, ln]).astype(BF16)
                )
                return carry

            lax.fori_loop(0, 4, first, 0, unroll=4)
            for cq in range(hf * ncq // 2, (hf + 1) * ncq // 2):
                send_pieces(n, cq, me, *fwd[g])

    def group_parts(g, c):
        return (
            r.bcc[blocks[c], g * 128 : (g + 1) * 128],
            r.bcc[blocks[c], 256 + g * 128 : 256 + (g + 1) * 128],
        )

    for g in range(NG):
        for c in range(2):
            bb, cc = group_parts(g, c)
            r.gm[...] = dnt(cc, bb)

            def inside(jj, carry, g=g, c=c):
                j = g * TPG + jj
                ln = lanes(j)
                rb2 = dnn(r.rs[blocks[c], :], spread_pair(j))
                ws = []
                for i in range(2):
                    h = 2 * j + i
                    lm = jnp.exp(
                        rb2[:, i * B : (i + 1) * B] - r.run[c, pl.ds(h, 1), :] + r.mask[c]
                    ) * r.dt[c, pl.ds(h, 1), :]
                    r.lm[2 * j + c, i * B : (i + 1) * B, :] = lm
                    wv = (r.gm[...] * lm).astype(BF16)
                    r.wm[2 * j + c, i * B : (i + 1) * B, :] = wv
                    ws.append(wv)
                xt = r.xc[blocks[c], ln]
                zero = jnp.zeros_like(xt)
                xbd = jnp.concatenate(
                    [jnp.where(half, xt, zero), jnp.where(half, zero, xt)], axis=0
                )
                r.y[blocks[c], ln] = dnn(jnp.concatenate(ws, axis=1), xbd)
                return carry

            lax.fori_loop(0, TPG, inside, 0, unroll=4)

    r.kb[me] = r.kr[lax.rem(me, ncq)]

    others = pl.ds(0, n - 1)
    rcopy(r.kb.at[others], r.kb.at[others], r.sk, r.rk, {"ctx": me}).wait_recv()
    owner_scan(n, halves[0], r.kb, *fwd[0], me, False)

    zcopy.wait()
    gcopy.wait()

    def prepare(j, carry):
        ln = lanes(j)
        zf = r.z[:, ln].astype(F32)
        sg = sigmoid(zf)
        r.gate[:, ln] = zf * sg
        r.dgate[:, ln] = sg * (1.0 + zf * (1.0 - sg))
        ext = r.ext.at[j % 4]
        ext[8 : 8 + T, :] = r.x[0, :, ln].astype(F32)
        ext[0:8, :] = r.hbuf[8:16, ln].astype(F32)
        for c in range(2):
            u = conv_input(ext, r.live, *x_weights(ln), c * B, B)
            sg = sigmoid(u)
            r.cdx[blocks[c], ln] = sg * (1.0 + u * (1.0 - sg))
        return carry

    lax.fori_loop(0, TPG, prepare, 0, unroll=2)
    owner_scan(n, halves[1], r.kb, *fwd[1], me, False)
    lax.fori_loop(TPG, NT, prepare, 0, unroll=2)

    r.sums_acc[...] = jnp.zeros_like(r.sums_acc)

    def skip_row(j):
        return jnp.where(lane1 < HEAD_DIM, r.skip[2 * j], r.skip[2 * j + 1])

    for g in range(NG):
        ccs = [group_parts(g, c)[1] for c in range(2)]
        take_pieces(n, me, *fwd[g])

        def outputs(jj, carry, g=g, ccs=ccs):
            j = g * TPG + jj
            ln = lanes(j)
            fs = dnn(r.mt[:, 2 * H : 4 * H], spread_two(j))
            sb0 = row_state(states[g], jj, n)
            sb1 = (r.krow[0, :, ln] * sb0.astype(F32) + r.fr[0, :, ln]).astype(BF16)
            r.sb1[:, ln] = sb1
            for c in range(2):
                sl = blocks[c]
                y = r.y[sl, ln] + dnn(ccs[c], sb0 if c == 0 else sb1) * fs[sl]
                r.y[sl, ln] = y
                mixed = (y + skip_row(j) * r.xc[sl, ln].astype(F32)).astype(BF16)
                r.mixed[sl, ln] = mixed
                gated = mixed.astype(F32) * r.gate[sl, ln]
                gained = r.go[sl, ln].astype(F32) * r.gain[0:1, ln]
                r.sums_acc[0, sl, :] += gated * gated
                r.sums_acc[1, sl, :] += gated * gained
            return carry

        lax.fori_loop(0, TPG, outputs, 0, unroll=4)
    ones = jnp.ones((8, 128), F32)
    r.sums[0:8, :] = dnt_full(ones, r.sums_acc[0])
    r.sums[8:16, :] = dnt_full(ones, r.sums_acc[1])
    copies = []
    for k in range(1, nh):
        copies.append(
            rcopy(r.sums, r.sbuf.at[k], r.hs.at[k], r.hr.at[k], {"head": lax.rem(hd + k, nh)})
        )
        copies[-1].start()
    for cp in copies:
        cp.wait()
    shares = [r.sums[...]] + [r.sbuf[k] for k in range(1, nh)]
    total = jnp.zeros_like(shares[0])
    for d in range(nh):
        for k in range(nh):
            total = total + jnp.where(lax.rem(hd - k + nh, nh) == d, shares[k], 0.0)
    inv = lax.rsqrt(total[0:8] / INNER + EPS)
    coef = inv * inv * inv * total[8:16] / INNER
    for c in range(2):
        sl = blocks[c]
        tr = jnp.concatenate([inv[:, sl], coef[:, sl], jnp.zeros((112, B), F32)], axis=0).T
        r.inv[sl, :] = jnp.broadcast_to(tr[:, 0:1], (B, 128))
        r.coef[sl, :] = jnp.broadcast_to(tr[:, 8:9], (B, 128))

    for g in range(NG):
        ct = [group_parts(g, c)[1].astype(F32).T.astype(BF16) for c in range(2)]
        for hf in range(2):

            def gates(i, carry, g=g, hf=hf, ct=ct):
                jj = hf * 4 + i
                j = g * TPG + jj
                ln = lanes(j)
                e2 = spread_two(j)
                grow = jnp.zeros((1, 128), F32)
                srow = jnp.zeros((1, 128), F32)
                ds = []
                for c in range(2):
                    sl = blocks[c]
                    m = r.mixed[sl, ln].astype(F32)
                    gt = r.gate[sl, ln]
                    gated = m * gt
                    gi = r.go[sl, ln].astype(F32) * r.inv[sl, :]
                    dg = gi * r.gain[0:1, ln] - gated * r.coef[sl, :]
                    grow = grow + jnp.sum(gi * gated, axis=0, keepdims=True)
                    r.dzv[sl, ln] = (dg * m * r.dgate[sl, ln]).astype(BF16)
                    dm = (dg * gt).astype(BF16)
                    r.dy[sl, ln] = dm
                    dy = dm.astype(F32)
                    srow = srow + jnp.sum(dy * r.xc[sl, ln].astype(F32), axis=0, keepdims=True)
                    h0, h1 = head_rows(dy * r.y[sl, ln])
                    r.rho[c, pl.ds(2 * j, 1), :] = h0
                    r.rho[c, pl.ds(2 * j + 1, 1), :] = h1
                    fd = (dnn(r.mt[sl, 2 * H : 4 * H], e2) * dy).astype(BF16)
                    r.fd[sl, ln] = fd
                    ds.append(dnn(ct[c], fd).astype(BF16))
                r.dsb1[:, ln] = ds[1]
                put_state(
                    bwd[g][0], jj, n,
                    (r.krow[0, :, ln] * ds[1].astype(F32) + ds[0].astype(F32)).astype(BF16),
                )
                r.pk[j, 5:6, :] = grow
                r.pk[j, 6:8, :] = jnp.zeros((2, 128), F32)
                r.hsr[2:3, ln] = srow
                return carry

            lax.fori_loop(0, 4, gates, 0, unroll=4)
            for cq in range(hf * ncq // 2, (hf + 1) * ncq // 2):
                send_pieces(n, cq, me, *bwd[g])
    zout = pltpu.make_async_copy(r.dzv, r.dz, r.zo)
    zout.start()

    for g in range(NG):
        r.acc[...] = jnp.zeros_like(r.acc)

        def inner(jj, carry, g=g):
            j = g * TPG + jj
            ln = lanes(j)
            for c in range(2):
                sl = blocks[c]
                dyt = r.dy[sl, ln]
                zero = jnp.zeros_like(dyt)
                dybd = jnp.concatenate(
                    [jnp.where(half, dyt, zero), jnp.where(half, zero, dyt)], axis=0
                )
                dw = dnt(dybd, r.xc[sl, ln])
                i = 2 * j + c
                r.acc[0, c] += dw[0:B] * r.lm[i, 0:B, :] + dw[B : 2 * B] * r.lm[i, B : 2 * B, :]
                r.y[sl, ln] = dtn(r.wm[i], dybd)
                sp = row_state(states[g], jj, n) if c == 0 else r.sb1[:, ln]
                r.acc[1, c] += dnt(r.fd[sl, ln], sp)
            return carry

        lax.fori_loop(0, TPG, inner, 0, unroll=4)
        for c in range(2):
            bb, cc = group_parts(g, c)
            dg = r.acc[0, c].astype(BF16)
            r.dbc[blocks[c], g * 128 : (g + 1) * 128] = dtn(dg, cc)
            r.dbc[blocks[c], 256 + g * 128 : 256 + (g + 1) * 128] = r.acc[1, c] + dnn(dg, bb)
        owner_scan(n, halves[g], r.kb, *bwd[g], me, True)

    r.vk[:, :, 0:8, :] = jnp.zeros((2, CONV, 8, 128), F32)
    r.vk[:, :, 8 + T :, :] = jnp.zeros((2, CONV, 8, 128), F32)

    def is_owner(j):
        return (me == j) & (dp == lax.rem(j, ndp))

    def give_tile(j):
        @pl.when(jnp.logical_not(is_owner(j)))
        def _():
            rcopy(
                r.pk.at[j], r.prb.at[mine], r.ps, r.pr,
                {"dp": lax.rem(j, ndp), "ctx": j},
            ).start()

    def conv_back(c, ext, vk, w, deriv, dxc, rows):
        sl = blocks[c]
        lo = c * B
        du = dxc * deriv
        rows[0] = rows[0] + jnp.sum(du * ext[8 + lo : 8 + lo + B, :], axis=0, keepdims=True)
        rows[CONV] = rows[CONV] + jnp.sum(du, axis=0, keepdims=True)
        own = w[0] * du
        for k in range(1, CONV):
            v = du * r.live[k - 1, sl, :]
            rows[k] = rows[k] + jnp.sum(
                v * ext[8 - k + lo : 8 - k + lo + B, :], axis=0, keepdims=True
            )
            vk[k, 8 + lo : 8 + lo + B, :] = v
        for k in range(1, CONV):
            own = own + w[k] * vk[k, 8 + k + lo : 8 + k + lo + B, :]
        return own

    def before_rows(vk, w):
        prior = jnp.zeros((8, 128), F32)
        for k in range(1, CONV):
            prior = prior + w[k] * vk[k, k : k + 8, :]
        return prior

    gouts = []
    for g in range(NG):
        r.acc[1] = jnp.zeros((2, B, 128), F32)
        take_pieces(n, me, *bwd[g])

        def outer(jj, carry, g=g):
            j = g * TPG + jj
            ln = lanes(j)
            e2 = spread_two(j)
            a1 = row_state(laters[g], jj, n).astype(F32)
            sk = skip_row(j)
            ext = r.ext.at[j % 4]
            ext[8 : 8 + T, :] = r.x[0, :, ln].astype(F32)
            ext[0:8, :] = r.hbuf[8:16, ln].astype(F32)
            vk = r.vk.at[j % 2]
            w = x_weights(ln)[0]
            rows = [jnp.zeros((1, 128), F32)] * (CONV + 1)
            for c in (1, 0):
                sl = blocks[c]
                if c == 1:
                    ds = a1
                    sp = r.sb1[:, ln]
                else:
                    ds = r.krow[1, :, ln] * a1 + r.dsb1[:, ln].astype(F32)
                    sp = row_state(states[g], jj, n)
                dsh = ds.astype(BF16)
                xf = r.xc[sl, ln].astype(F32)
                dxu = dnn(r.bcc[sl, g * 128 : (g + 1) * 128], dsh) * dnn(
                    r.mt[sl, 0 : 2 * H], e2
                )
                r.acc[1, c] += dnt(r.uu[sl, ln], dsh)
                dxs = r.y[sl, ln] + dxu
                ku = jnp.sum(xf * dxu, axis=0, keepdims=True)
                kd = jnp.sum(ds * sp.astype(F32), axis=0, keepdims=True) * r.krow[c, :, ln]
                r.hsr[c : c + 1, ln] = ku + kd
                h0, h1 = head_rows(xf * dxs)
                r.kap[c, pl.ds(2 * j, 1), :] = h0
                r.kap[c, pl.ds(2 * j + 1, 1), :] = h1
                own = conv_back(
                    c, ext, vk, w, r.cdx[sl, ln], dxs + sk * r.dy[sl, ln].astype(F32), rows
                )
                r.gxv[g, sl, lanes(jj)] = own.astype(BF16)
                if c == 1:
                    r.tails[:, ln] = own[B - 16 : B]
            r.hb[:, ln] = before_rows(vk, w)
            r.pk[j, 0 : CONV + 1, :] = jnp.concatenate(rows, axis=0)
            give_tile(j)
            return carry

        lax.fori_loop(0, TPG, outer, 0, unroll=2)
        gouts.append(
            pltpu.make_async_copy(
                r.gxv.at[g], r.gx.at[:, pl.ds(g * TPG * 128, TPG * 128)], r.xo.at[g]
            )
        )
        gouts[-1].start()
        for c in range(2):
            r.dbc[blocks[c], g * 128 : (g + 1) * 128] += r.acc[1, c]

    for j in range(4):
        sl = slice(j * 128, (j + 1) * 128)
        sd = slice(D + j * 128, D + (j + 1) * 128)
        ext = r.ext.at[j]
        ext[8 : 8 + T, :] = r.bc[:, sl].astype(F32)
        ext[0:8, :] = r.hbuf[8:16, sd].astype(F32)
        vk = r.vk.at[j % 2]
        w = bc_weights(j)[0]
        rows = [jnp.zeros((1, 128), F32)] * (CONV + 1)
        for c in (1, 0):
            own = conv_back(
                c, ext, vk, w, r.cdb[blocks[c], sl], r.dbc[blocks[c], sl], rows
            )
            r.gbc[blocks[c], sl] = own.astype(BF16)
            if c == 1:
                r.tails[:, sd] = own[B - 16 : B]
        r.hb[:, sd] = before_rows(vk, w)
        r.pk[NT + j, 0 : CONV + 1, :] = jnp.concatenate(rows, axis=0)
        r.pk[NT + j, 5:8, :] = jnp.zeros((3, 128), F32)
        give_tile(NT + j)
    back = rcopy(r.hb, r.bbuf, r.sb, r.rb_sem, {"ctx": lax.rem(me + n - 1, n)})

    @pl.when(me > 0)
    def _():
        back.start()

    of_head = (iota((H, D), 1) // HEAD_DIM == iota((H, D), 0)).astype(BF16)
    high = r.hsr[...].astype(BF16)
    low = (r.hsr[...] - high.astype(F32)).astype(BF16)
    hs = dnt(of_head, high) + dnt(of_head, low)
    rev = (iota((B, B), 0) >= iota((B, B), 1)).astype(F32)
    rate_sum = jnp.zeros((H, B), F32)
    bias_sum = jnp.zeros((H, B), F32)
    for c in range(2):
        sl = blocks[c]
        dtv = r.dt[c]
        kp = r.kap[c]
        rr = dnn_full(r.rho[c] - kp, rev) + hs[:, c : c + 1]
        gd = (kp / dtv - rate * rr) * sigmoid(r.dtr[0, :, sl].astype(F32) + bias)
        r.gdt[:, sl] = gd
        rate_sum = rate_sum - rate * dtv * rr
        bias_sum = bias_sum + gd
    skips = jnp.where(iota((H, B), 1) == 0, hs[:, 2:3], 0.0)
    r.pk[nt - 1] = dnt_full(
        ones, jnp.concatenate([rate_sum, bias_sum, skips, jnp.zeros((H, B), F32)], axis=0)
    )
    give_tile(nt - 1)

    @pl.when((me < nt) & (dp == lax.rem(me, ndp)))
    def _():
        r.prb[mine] = r.pk[me]

        alls = pl.ds(0, ne - 1)
        rcopy(r.prb.at[alls], r.prb.at[alls], r.ps, r.pr, {"ctx": me}).wait_recv()

        def collect(e, total):
            return total + r.prb[e]

        r.pob[me] = lax.fori_loop(0, ne, collect, jnp.zeros((8, 128), F32), unroll=8)

        def give(k, carry):
            e = lax.rem(mine + k, ne)
            rcopy(
                r.pob.at[me], r.pob.at[me], r.as_, r.ar,
                {"dp": e // n, "ctx": lax.rem(e, n)},
            ).start()
            return carry

        lax.fori_loop(1, ne, give, 0)

    @pl.when(me < n - 1)
    def _():
        halo.wait_send()
        back.wait_recv()

    @pl.when(me > 0)
    def _():
        back.wait_send()

    rcopy(r.kb.at[others], r.kb.at[others], r.sk, r.rk, {"ctx": me}).wait_send()
    for st, rb, pb, ob, s1, r1, s2, r2 in fwd + bwd:
        rcopy(st.at[others], rb.at[others], s1, r1, {"ctx": me}).wait_send()
        rcopy(pb.at[others], ob.at[others], s2, r2, {"ctx": me}).wait_send()
    zout.wait()
    for out in gouts:
        out.wait()

    owns = (me < nt) & (dp == lax.rem(me, ndp))

    @pl.when(owns)
    def _():
        alls = pl.ds(0, ne - 1)
        most = pl.ds(0, nt - 1)
        rcopy(r.prb.at[alls], r.prb.at[alls], r.as_, r.ar, {"ctx": me}).wait_send()
        rcopy(r.pk.at[most], r.pob.at[most], r.ps, r.ar, {"ctx": me}).wait()

    @pl.when(jnp.logical_not(owns))
    def _():
        rcopy(r.pk, r.pob, r.ps, r.ar, {"ctx": me}).wait()

    r.red[...] = r.pob[...]
    r.rh_o[...] = r.bbuf[...]


def k5_body(scale, red, rh, tail, flg, gx_i, dz_i, gbc_i, gdt_i,
            gx_o, dz_o, gbc_o, gdt_o, cw_o, cb_o, bw_o, bb_o, al_o, db_o, sk_o, ga_o, gbs):
    i = pl.program_id(0)
    last_step = pl.num_programs(0) - 1
    rows = gx_o.shape[0]
    gx_o[...] = gx_i[...]
    dz_o[...] = dz_i[...]
    gbs[...] = gbc_i[...]

    @pl.when(i == 0)
    def _():
        gdt_o[...] = gdt_i[...]
        for j in range(NT + 4):
            sl = slice(j * 128, (j + 1) * 128)
            t = red[j] * scale
            if j < NT:
                cw_o[:, sl] = t[0:4]
                cb_o[:, sl] = t[4:5]
                ga_o[:, sl] = t[5:6]
            else:
                m = j - NT
                sb = slice((m % 2) * 128, (m % 2) * 128 + 128)
                for k in range(CONV):
                    bw_o[k, m // 2 : m // 2 + 1, sb] = t[k : k + 1]
                bb_o[m // 2 : m // 2 + 1, sb] = t[4:5]
        last_tile = red[NT + 4] * scale
        al_o[...] = last_tile[0:1, 0:H]
        db_o[...] = last_tile[0:1, H : 2 * H]
        sk_o[...] = last_tile[0:1, 2 * H : 3 * H]

    @pl.when(i == last_step)
    def _():
        f = flg[:, B:T].astype(F32)
        lane = iota((1, B), 1)
        last = jnp.sum(jnp.where(lane == B - 1, f, 0.0))
        two = jnp.sum(jnp.where(lane >= B - 2, f, 0.0))
        row = iota((16, 128), 0)
        keep = jnp.where(row == 15, 1.0, 0.0)
        keep = keep + jnp.where((row == 14) & (last == 0.0), 1.0, 0.0)
        keep = keep + jnp.where((row == 13) & (two == 0.0), 1.0, 0.0)
        for j in range(NT + 4):
            sl = slice(j * 128, (j + 1) * 128)
            add = jnp.concatenate([jnp.zeros((8, 128), F32), rh[:, sl]], axis=0)
            v = (tail[:, sl] + add * keep).astype(BF16)
            if j < NT:
                gx_o[rows - 16 : rows, sl] = v
            else:
                gbs[rows - 16 : rows, j * 128 - D : (j + 1) * 128 - D] = v

    gbc_o[...] = gbs[...].reshape(rows, 2, DB // 2)


def sds(*shape, dtype=F32):
    return jax.ShapeDtypeStruct(shape, dtype)


def per_device(
    x_raw, bc_raw, z_gate, dt_raw, resets, conv_x_weight, conv_x_bias, conv_bc_weight,
    conv_bc_bias, a_log, dt_bias, skip_weight, norm_gain, grad_out,
):
    n = lax.axis_size("ctx")
    nh = lax.axis_size("head")
    ndp = lax.axis_size("dp")
    ncq = n // 8
    w = D // ncq
    nt = NT + 5
    ne = n * ndp
    ANY = pl.BlockSpec(memory_space=pl.ANY)
    ins = [
        ("x", x_raw, VM), ("bc_raw", bc_raw, VM), ("z_hbm", z_gate, ANY),
        ("go_hbm", grad_out, ANY), ("dtr", dt_raw, VM), ("flg", resets, VM),
        ("alog", a_log.reshape(1, H), VM), ("dtb", dt_bias.reshape(1, H), VM),
        ("cxw", conv_x_weight, VM), ("cxb", conv_x_bias.reshape(1, D), VM),
        ("cbw", conv_bc_weight, VM), ("cbb", conv_bc_bias, VM),
        ("gain", norm_gain.reshape(1, D), VM), ("skip", skip_weight, SM),
    ]
    outs = [
        ("gx", sds(T, D, dtype=BF16)), ("dz", sds(T, D, dtype=BF16)),
        ("gbc", sds(T, DB, dtype=BF16)), ("gdt", sds(H, T)), ("tails", sds(16, D + DB)),
        ("red", sds(nt, 8, 128)), ("rh_o", sds(8, D + DB)),
    ]
    V = pltpu.VMEM
    dma = pltpu.SemaphoreType.DMA
    state = V((n, ROWS, w // NG), BF16)
    scratch = [
        ("z", V((T, D), BF16)), ("go", V((T, D), BF16)), ("zs", dma), ("gs", dma),
        ("ext", V((4, T + 8, 128), F32)), ("cnt", V((T + 8, 128), F32)),
        ("live", V((CONV - 1, T, 128), F32)), ("mask", V((2, B, B), F32)),
        ("dt", V((2, H, B), F32)), ("run", V((2, H, B), F32)), ("mt", V((T, 128), BF16)),
        ("rs", V((T, 128), BF16)), ("tail", V((16, D + DB), BF16)),
        ("hbuf", V((16, D + DB), BF16)), ("xc", V((T, D), BF16)), ("bcc", V((T, DB), BF16)),
        ("cdb", V((T, DB), F32)), ("cdx", V((T, D), F32)), ("fr", V((2, NSTATE, D), F32)),
        ("kr", V((ncq, 1, w), F32)), ("kb", V((n, 1, w), F32)), ("krow", V((2, 1, D), F32)),
        ("uu", V((T, D), BF16)), ("bc", V((T, DB), BF16)), ("hsr", V((8, D), F32)),
        ("dzv", V((T, D), BF16)), ("gxv", V((NG, T, D // NG), BF16)), ("zo", dma),
        ("xo", dma((NG,))), ("gm", V((B, B), F32)),
        ("lm", V((2 * NT, 2 * B, B), F32)), ("wm", V((2 * NT, 2 * B, B), BF16)),
        ("y", V((T, D), F32)), ("gate", V((T, D), F32)), ("dgate", V((T, D), F32)),
        ("mixed", V((T, D), BF16)), ("sb1", V((NSTATE, D), BF16)),
        ("sums_acc", V((2, T, 128), F32)), ("sums", V((16, T), F32)),
        ("sbuf", V((nh, 16, T), F32)), ("inv", V((T, 128), F32)), ("coef", V((T, 128), F32)),
        ("rho", V((2, H, B), F32)), ("dy", V((T, D), BF16)),
        ("fd", V((T, D), BF16)), ("dsb1", V((NSTATE, D), BF16)), ("acc", V((2, 2, B, 128), F32)),
        ("dbc", V((T, DB), F32)), ("kap", V((2, H, B), F32)),
        ("vk", V((2, CONV, T + 16, 128), F32)), ("pk", V((nt, 8, 128), F32)),
        ("prb", V((ne, 8, 128), F32)), ("pob", V((nt, 8, 128), F32)),
        ("hb", V((8, D + DB), F32)), ("bbuf", V((8, D + DB), F32)),
        ("sh", dma), ("rh", dma), ("sb", dma), ("rb_sem", dma),
        ("hs", dma((nh,))), ("hr", dma((nh,))),
    ]
    scratch += [
        (k, dma)
        for k in (
            "sk", "rk", "ps", "ar", "pr", "as_",
        )
    ]
    for way in ("f0", "f1", "b0", "b1"):
        scratch += [(k + way, state) for k in ("st", "rb", "pb", "ob")]
        scratch += [(k + way, dma) for k in ("s1", "r1", "s2", "r2")]
    names = [v[0] for v in ins] + [v[0] for v in outs] + [v[0] for v in scratch]
    gx, dz, gbc, gdt, tails, red, rh = pl.pallas_call(
        functools.partial(main_body, n, nh, ndp, nt, names),
        out_shape=[v[1] for v in outs],
        in_specs=[v[2] for v in ins],
        out_specs=[ANY] * 2 + [VM] * (len(outs) - 2),
        scratch_shapes=[v[1] for v in scratch],
        compiler_params=pltpu.CompilerParams(
            vmem_limit_bytes=VLIM, collective_id=0, has_side_effects=True
        ),
    )(*[v[1] for v in ins])
    scale = float(ndp * n * T) ** (-0.5)
    whole = lambda *s: pl.BlockSpec(s, lambda i: (0,) * len(s))
    step = T // 4
    block = lambda c: pl.BlockSpec((step, c), lambda i: (i, 0))
    outs = pl.pallas_call(
        functools.partial(k5_body, scale),
        grid=(4,),
        out_shape=(
            sds(T, D, dtype=BF16), sds(T, D, dtype=BF16), sds(T, 2, DB // 2, dtype=BF16),
            sds(H, T), sds(CONV, D), sds(1, D), sds(CONV, 2, DB // 2), sds(2, DB // 2),
            sds(1, H), sds(1, H), sds(1, H), sds(1, D),
        ),
        in_specs=[
            whole(nt, 8, 128), whole(8, D + DB), whole(16, D + DB), whole(1, T),
            block(D), block(D), block(DB), whole(H, T),
        ],
        out_specs=[
            block(D), block(D), pl.BlockSpec((step, 2, DB // 2), lambda i: (i, 0, 0)),
            whole(H, T), whole(CONV, D), whole(1, D), whole(CONV, 2, DB // 2), whole(2, DB // 2),
            whole(1, H), whole(1, H), whole(1, H), whole(1, D),
        ],
        scratch_shapes=[V((step, DB), BF16)],
    )(red, rh, tails, resets, gx, dz, gbc, gdt)
    gx, dz, gbc, gdt, cw, cb, bw, bb, al, db, sk, ga = outs
    return (
        gx[None], gbc[None], dz[None], gdt[None], cw, cb.reshape(D),
        bw, bb, al.reshape(H), db.reshape(H), sk.reshape(H), ga.reshape(D),
    )


def solution(mesh):
    return jax.shard_map(
        per_device,
        mesh=mesh,
        in_specs=(
            P("dp", "ctx", "head"),
            P("dp", "ctx", None, "head"),
            P("dp", "ctx", "head"),
            P("dp", "head", "ctx"),
            P("dp", "ctx"),
            P(None, "head"),
            P("head"),
            P(None, None, "head"),
            P(None, "head"),
            P("head"),
            P("head"),
            P("head"),
            P("head"),
            P("dp", "ctx", "head"),
        ),
        out_specs=(
            P("dp", "ctx", "head"),
            P("dp", "ctx", None, "head"),
            P("dp", "ctx", "head"),
            P("dp", "head", "ctx"),
            P(None, "head"),
            P("head"),
            P(None, None, "head"),
            P(None, "head"),
            P("head"),
            P("head"),
            P("head"),
            P("head"),
        ),
        check_vma=False,
    )
```

```python
import functools

import types

import jax
import jax.numpy as jnp
from jax import lax
from jax.experimental import pallas as pl
from jax.experimental.pallas import tpu as pltpu
from jax.sharding import PartitionSpec as P

F32 = jnp.float32
BF16 = jnp.bfloat16
HIGHEST = lax.Precision.HIGHEST
MESH = pl.DeviceIdType.MESH

HEAD_DIM = 64
NSTATE = 128
CONV = 4
INNER = 8192
EPS = 1e-05

T = 256
B = 128
H = 32
D = 2048
DB = 512
NT = D // 128
NG = 2
TPG = NT // NG
ROWS = 16
VM = pl.BlockSpec(memory_space=pltpu.VMEM)
SM = pl.BlockSpec(memory_space=pltpu.SMEM)
VMAIN = 46 * 1024 * 1024


def dnn(a, b):
    return lax.dot_general(a, b, (((1,), (0,)), ((), ())), preferred_element_type=F32)


def dnt(a, b):
    return lax.dot_general(a, b, (((1,), (1,)), ((), ())), preferred_element_type=F32)


def dtn(a, b):
    return lax.dot_general(a, b, (((0,), (0,)), ((), ())), preferred_element_type=F32)


def dnn_full(a, b):
    return lax.dot_general(
        a, b, (((1,), (0,)), ((), ())), precision=HIGHEST, preferred_element_type=F32
    )


def dnt_full(a, b):
    return lax.dot_general(
        a, b, (((1,), (1,)), ((), ())), precision=HIGHEST, preferred_element_type=F32
    )


def iota(shape, dim):
    return lax.broadcasted_iota(jnp.int32, shape, dim)


def high_low(v):
    high = v.astype(BF16).astype(F32)
    return high, v - high


def sigmoid(v):
    return 1.0 / (1.0 + jnp.exp(-v))


def softplus(v):
    y = jnp.exp(-jnp.abs(v))
    series = y * (1.0 - y * (0.5 - y * (1.0 / 3.0 - y * (0.25 - 0.2 * y))))
    return jnp.maximum(v, 0.0) + jnp.where(y < 0.02, series, jnp.log(1.0 + y))


def lanes(j):
    return pl.ds(pl.multiple_of(j * 128, 128), 128)


def spread_two(j):
    row = iota((2 * H, 128), 0) % H
    lane = iota((2 * H, 128), 1)
    return (row == 2 * j + lane // HEAD_DIM).astype(BF16)


def spread_pair(j):
    row = iota((128, 256), 0)
    lane = iota((128, 256), 1)
    return ((row % H == 2 * j + lane // 128) & (row < 3 * H)).astype(BF16)


def conv_input(ext, live, w, bias, lo, rows):
    u = bias + w[0] * ext[8 + lo : 8 + lo + rows, :]
    for k in range(1, CONV):
        u = u + w[k] * ext[8 - k + lo : 8 - k + lo + rows, :] * live[k - 1, lo : lo + rows, :]
    return u


def live_masks(cnt, live):
    now = cnt[8 : 8 + T, :]
    for k in range(1, CONV):
        live[k - 1] = (now == cnt[8 - k : 8 - k + T, :]).astype(F32)


def row_state(ref, jj, n):
    ncq = n // 8
    tpc = TPG // ncq
    cq = jj // tpc
    lane = lanes(jj % tpc)
    return jnp.concatenate([ref[rz * ncq + cq, :, lane] for rz in range(8)], axis=0)


def put_state(ref, jj, n, v):
    ncq = n // 8
    tpc = TPG // ncq
    cq = jj // tpc
    lane = lanes(jj % tpc)
    for rz in range(8):
        ref[rz * ncq + cq, :, lane] = v[rz * ROWS : (rz + 1) * ROWS]


def head_rows(v):
    t = v.T
    return (
        jnp.sum(t[0:HEAD_DIM], axis=0, keepdims=True),
        jnp.sum(t[HEAD_DIM:], axis=0, keepdims=True),
    )


def column(row):
    return jnp.concatenate(
        [jnp.broadcast_to(row, (128, H)), jnp.zeros((128, 128 - H), F32)], axis=1
    ).T[0:H, 0:1]


def rcopy(src, dst, sem_s, sem_r, dev):
    return pltpu.make_async_remote_copy(
        src_ref=src, dst_ref=dst, send_sem=sem_s, recv_sem=sem_r,
        device_id=dev, device_id_type=MESH,
    )


def send_pieces(n, cq, me, st, rb, pb, ob, s1, r1, s2, r2):
    ncq = n // 8

    def send(rz, carry):
        to = rz * ncq + cq

        @pl.when(to != me)
        def _():
            rcopy(st.at[to], rb.at[me], s1, r1, {"ctx": to}).start()

        return carry

    lax.fori_loop(0, 8, send, 0)


def owner_scan(n, half, kb, st, rb, pb, ob, s1, r1, s2, r2, me, backward):
    rb[me] = st[me]
    others = pl.ds(0, n - 1)
    rcopy(st.at[others], rb.at[others], s1, r1, {"ctx": me}).wait_recv()

    def step(i, acc):
        d = n - 1 - i if backward else i

        pb[d] = acc.astype(BF16)

        @pl.when(d != me)
        def _():
            rcopy(pb.at[d], ob.at[me], s2, r2, {"ctx": d}).start()

        return kb[d, :, half] * acc + rb[d].astype(F32)

    lax.fori_loop(0, n, step, jnp.zeros(rb.shape[1:], F32))
    ob[me] = pb[me]


def take_pieces(n, me, st, rb, pb, ob, s1, r1, s2, r2):
    others = pl.ds(0, n - 1)
    rcopy(pb.at[others], ob.at[others], s2, r2, {"ctx": me}).wait_recv()


def main_body(n, nh, ndp, nt, names, fed, *refs):
    r = types.SimpleNamespace(**dict(zip(names, refs)))
    ncq = n // 8
    wh = TPG * 128 // ncq
    me = lax.axis_index("ctx")
    dp = lax.axis_index("dp")
    hd = lax.axis_index("head")
    ne = n * ndp
    mine = dp * n + me
    half = iota((B, 128), 1) < HEAD_DIM
    lane1 = iota((1, 128), 1)
    blocks = [slice(0, B), slice(B, T)]
    halves = [slice(g * wh, (g + 1) * wh) for g in range(NG)]
    parts = ("st", "rb", "pb", "ob", "s1", "r1", "s2", "r2")
    fwd = [[getattr(r, k + "f" + str(g)) for k in parts] for g in range(NG)]
    bwd = [[getattr(r, k + "b" + str(g)) for k in parts] for g in range(NG)]
    states = [f[3] for f in fwd]
    laters = [f[3] for f in bwd]

    r.hbuf[...] = jnp.zeros_like(r.hbuf)
    r.bbuf[...] = jnp.zeros_like(r.bbuf)
    barrier = pltpu.get_barrier_semaphore()

    def greet(k, carry):
        e = lax.rem(mine + k, ne)
        pl.semaphore_signal(
            barrier, inc=1, device_id={"dp": e // n, "ctx": lax.rem(e, n)}, device_id_type=MESH
        )
        return carry

    lax.fori_loop(1, ne, greet, 0)
    for k in range(1, nh):
        pl.semaphore_signal(
            barrier, inc=1, device_id={"head": lax.rem(hd + k, nh)}, device_id_type=MESH
        )
    loads = [
        pltpu.make_async_copy(getattr(r, k + "_in"), getattr(r, k), r.ins.at[i])
        for i, k in enumerate(fed)
    ]
    for load in loads:
        load.start()
    zcopy = pltpu.make_async_copy(r.z_hbm.at[0], r.z, r.zs)
    gcopy = pltpu.make_async_copy(r.go_hbm.at[0], r.go, r.gs)
    zcopy.start()
    gcopy.start()
    r.hsr[...] = jnp.zeros_like(r.hsr)
    for load in loads:
        load.wait()
    r.bc[...] = r.bc_raw[0].reshape(T, DB)

    rate = jnp.exp(column(r.alog[...]))
    bias = column(r.dtb[...])
    tri = (iota((B, B), 0) <= iota((B, B), 1)).astype(F32)
    before = jnp.zeros((8, 1), F32)
    r.cnt[0:8, :] = jnp.zeros((8, 128), F32)
    masks = []
    for c in range(2):
        sl = blocks[c]
        dtv = softplus(r.dtr[0, :, sl].astype(F32) + bias)
        run = dnn_full(-rate * dtv, tri)
        q = dnn(jnp.broadcast_to(r.flg[:, sl].astype(F32), (8, B)), tri)
        rl = run[:, B - 1 : B]
        ql = q[:, B - 1 : B]
        dtte = dtv * jnp.where(q[0:1] == ql[0:1], jnp.exp(rl - run), 0.0)
        fs = jnp.where(q[0:1] == 0.0, jnp.exp(run), 0.0)
        r.dt[c] = dtv
        r.run[c] = run
        a1, a2 = high_low(dtte)
        b1, b2 = high_low(fs)
        r.mt[sl, :] = jnp.concatenate([a1, a2, b1, b2], axis=0).T.astype(BF16)
        dev = q + before
        before = dev[:, B - 1 : B]
        rt = jnp.concatenate([q, dev, jnp.zeros((112, B), F32)], axis=0).T
        r1, r2 = high_low(run)
        r2, r3 = high_low(r2)
        r.rs[sl, :] = jnp.concatenate(
            [r1, r2, r3, jnp.zeros((H, B), F32)], axis=0
        ).T.astype(BF16)
        r.cnt[8 + c * B : 8 + (c + 1) * B, :] = jnp.broadcast_to(rt[:, 8:9], (B, 128))
        ok = (rt[:, 0:1] == q[0:1, :]) & (iota((B, B), 0) >= iota((B, B), 1))
        r.mask[c] = jnp.where(ok, 0.0, -1e30)
    live_masks(r.cnt, r.live)

    def keeps(j, carry):
        e2 = spread_two(j)
        k0, k1 = [
            dnn(r.mt[(c + 1) * B - 16 : (c + 1) * B, 2 * H : 4 * H], e2)[15:16] for c in range(2)
        ]
        r.krow[0, :, lanes(j)] = k0
        r.krow[1, :, lanes(j)] = k1
        tpc = TPG // ncq
        jj = j % TPG
        r.kr[jj // tpc, :, lanes((j // TPG) * tpc + jj % tpc)] = k0 * k1
        return carry

    lax.fori_loop(0, NT, keeps, 0, unroll=4)

    row16 = iota((16, 128), 0)
    same = (r.cnt[8 + T - 16 : 8 + T, :] == r.cnt[8 + T - 1 : 8 + T, :])
    for j in range(NT + 4):
        v = r.x[0, T - 16 : T, j * 128 : (j + 1) * 128] if j < NT else r.bc[
            T - 16 : T, j * 128 - D : (j + 1) * 128 - D
        ]
        r.tail[:, j * 128 : (j + 1) * 128] = jnp.where(same, v.astype(F32), 0.0).astype(BF16)

    def bc_weights(j):
        i, sl = j // 2, slice((j % 2) * 128, (j % 2) * 128 + 128)
        return [r.cbw[k, i : i + 1, sl] for k in range(CONV)], r.cbb[i : i + 1, sl]

    def x_weights(ln):
        return [r.cxw[k : k + 1, ln] for k in range(CONV)], r.cxb[0:1, ln]

    def bc_conv(c):
        for j in range(4):
            sl = slice(j * 128, (j + 1) * 128)
            ext = r.ext.at[j]
            if c == 1:
                ext[8 : 8 + T, :] = r.bc[:, sl].astype(F32)
            else:
                ext[8 : 8 + B, :] = r.bc[0:B, sl].astype(F32)
                ext[0:8, :] = r.hbuf[8:16, D + j * 128 : D + (j + 1) * 128].astype(F32)
            u = conv_input(ext, r.live, *bc_weights(j), c * B, B)
            sg = sigmoid(u)
            r.bcc[blocks[c], sl] = (u * sg).astype(BF16)
            r.cdb[blocks[c], sl] = sg * (1.0 + u * (1.0 - sg))

    def x_conv(j, c):
        ln = lanes(j)
        ext = r.ext.at[j % 4]
        if c == 1:
            ext[8 : 8 + T, :] = r.x[0, :, ln].astype(F32)
        else:
            ext[8 : 8 + B, :] = r.x[0, 0:B, ln].astype(F32)
            ext[0:8, :] = r.hbuf[8:16, ln].astype(F32)
        u = conv_input(ext, r.live, *x_weights(ln), c * B, B)
        xc = (u * sigmoid(u)).astype(BF16)
        r.xc[blocks[c], ln] = xc
        dtte = dnn(r.mt[blocks[c], 0 : 2 * H], spread_two(j))
        uu = (xc.astype(F32) * dtte).astype(BF16)
        r.uu[blocks[c], ln] = uu
        return uu

    def b_turned(g, c):
        return r.bcc[blocks[c], g * 128 : (g + 1) * 128].astype(F32).T.astype(BF16)

    bc_conv(1)
    for g in range(NG):
        bt = b_turned(g, 1)

        def second(jj, carry, g=g, bt=bt):
            j = g * TPG + jj
            r.fr[1, :, lanes(j)] = dnn(bt, x_conv(j, 1))
            return carry

        lax.fori_loop(0, TPG, second, 0, unroll=4)
        if g == 0:
            pl.semaphore_wait(barrier, ne - 1 + nh - 1)
            halo = rcopy(r.tail, r.hbuf, r.sh, r.rh, {"ctx": lax.rem(me + 1, n)})

            @pl.when(me < n - 1)
            def _():
                halo.start()

            def send_row(k, carry):
                to = lax.rem(me + k, n)
                rcopy(
                    r.kr.at[lax.rem(to, ncq)], r.kb.at[me], r.sk, r.rk, {"ctx": to}
                ).start()
                return carry

            lax.fori_loop(1, n, send_row, 0)

    @pl.when(me > 0)
    def _():
        halo.wait_recv()

    bc_conv(0)
    for g in range(NG):
        bt = b_turned(g, 0)
        for hf in range(2):

            def first(i, carry, g=g, hf=hf, bt=bt):
                jj = hf * 4 + i
                j = g * TPG + jj
                ln = lanes(j)
                fresh = dnn(bt, x_conv(j, 0))
                r.fr[0, :, ln] = fresh
                put_state(
                    fwd[g][0], jj, n, (r.krow[1, :, ln] * fresh + r.fr[1, :, ln]).astype(BF16)
                )
                return carry

            lax.fori_loop(0, 4, first, 0, unroll=4)
            for cq in range(hf * ncq // 2, (hf + 1) * ncq // 2):
                send_pieces(n, cq, me, *fwd[g])

    def group_parts(g, c):
        return (
            r.bcc[blocks[c], g * 128 : (g + 1) * 128],
            r.bcc[blocks[c], 256 + g * 128 : 256 + (g + 1) * 128],
        )

    for g in range(NG):
        for c in range(2):
            bb, cc = group_parts(g, c)
            r.gm[...] = dnt(cc, bb)

            def inside(jj, carry, g=g, c=c):
                j = g * TPG + jj
                ln = lanes(j)
                rb2 = dnn(r.rs[blocks[c], :], spread_pair(j))
                ws = []
                for i in range(2):
                    h = 2 * j + i
                    lm = jnp.exp(
                        rb2[:, i * B : (i + 1) * B] - r.run[c, pl.ds(h, 1), :] + r.mask[c]
                    ) * r.dt[c, pl.ds(h, 1), :]
                    r.lm[2 * j + c, i * B : (i + 1) * B, :] = lm
                    wv = (r.gm[...] * lm).astype(BF16)
                    r.wm[2 * j + c, i * B : (i + 1) * B, :] = wv
                    ws.append(wv)
                xt = r.xc[blocks[c], ln]
                zero = jnp.zeros_like(xt)
                xbd = jnp.concatenate(
                    [jnp.where(half, xt, zero), jnp.where(half, zero, xt)], axis=0
                )
                r.y[blocks[c], ln] = dnn(jnp.concatenate(ws, axis=1), xbd)
                return carry

            lax.fori_loop(0, TPG, inside, 0, unroll=4)

    r.kb[me] = r.kr[lax.rem(me, ncq)]

    others = pl.ds(0, n - 1)
    rcopy(r.kb.at[others], r.kb.at[others], r.sk, r.rk, {"ctx": me}).wait_recv()
    owner_scan(n, halves[0], r.kb, *fwd[0], me, False)

    zcopy.wait()
    gcopy.wait()

    def prepare(j, carry):
        ln = lanes(j)
        zf = r.z[:, ln].astype(F32)
        sg = sigmoid(zf)
        r.gate[:, ln] = zf * sg
        r.dgate[:, ln] = sg * (1.0 + zf * (1.0 - sg))
        ext = r.ext.at[j % 4]
        ext[8 : 8 + T, :] = r.x[0, :, ln].astype(F32)
        ext[0:8, :] = r.hbuf[8:16, ln].astype(F32)
        for c in range(2):
            u = conv_input(ext, r.live, *x_weights(ln), c * B, B)
            sg = sigmoid(u)
            r.cdx[blocks[c], ln] = sg * (1.0 + u * (1.0 - sg))
        return carry

    lax.fori_loop(0, TPG, prepare, 0, unroll=2)
    owner_scan(n, halves[1], r.kb, *fwd[1], me, False)
    lax.fori_loop(TPG, NT, prepare, 0, unroll=2)

    r.sums_acc[...] = jnp.zeros_like(r.sums_acc)

    def skip_row(j):
        return jnp.where(lane1 < HEAD_DIM, r.skip[2 * j], r.skip[2 * j + 1])

    for g in range(NG):
        ccs = [group_parts(g, c)[1] for c in range(2)]
        take_pieces(n, me, *fwd[g])

        def outputs(jj, carry, g=g, ccs=ccs):
            j = g * TPG + jj
            ln = lanes(j)
            fs = dnn(r.mt[:, 2 * H : 4 * H], spread_two(j))
            sb0 = row_state(states[g], jj, n)
            sb1 = (r.krow[0, :, ln] * sb0.astype(F32) + r.fr[0, :, ln]).astype(BF16)
            r.sb1[:, ln] = sb1
            for c in range(2):
                sl = blocks[c]
                y = r.y[sl, ln] + dnn(ccs[c], sb0 if c == 0 else sb1) * fs[sl]
                r.y[sl, ln] = y
                mixed = (y + skip_row(j) * r.xc[sl, ln].astype(F32)).astype(BF16)
                r.mixed[sl, ln] = mixed
                gated = mixed.astype(F32) * r.gate[sl, ln]
                gained = r.go[sl, ln].astype(F32) * r.gain[0:1, ln]
                r.sums_acc[0, sl, :] += gated * gated
                r.sums_acc[1, sl, :] += gated * gained
            return carry

        lax.fori_loop(0, TPG, outputs, 0, unroll=4)
    ones = jnp.ones((8, 128), F32)
    r.sums[0:8, :] = dnt_full(ones, r.sums_acc[0])
    r.sums[8:16, :] = dnt_full(ones, r.sums_acc[1])
    copies = []
    for k in range(1, nh):
        copies.append(
            rcopy(r.sums, r.sbuf.at[k], r.hs.at[k], r.hr.at[k], {"head": lax.rem(hd + k, nh)})
        )
        copies[-1].start()
    for cp in copies:
        cp.wait()
    shares = [r.sums[...]] + [r.sbuf[k] for k in range(1, nh)]
    total = jnp.zeros_like(shares[0])
    for d in range(nh):
        for k in range(nh):
            total = total + jnp.where(lax.rem(hd - k + nh, nh) == d, shares[k], 0.0)
    inv = lax.rsqrt(total[0:8] / INNER + EPS)
    coef = inv * inv * inv * total[8:16] / INNER
    for c in range(2):
        sl = blocks[c]
        tr = jnp.concatenate([inv[:, sl], coef[:, sl], jnp.zeros((112, B), F32)], axis=0).T
        r.inv[sl, :] = jnp.broadcast_to(tr[:, 0:1], (B, 128))
        r.coef[sl, :] = jnp.broadcast_to(tr[:, 8:9], (B, 128))

    for g in range(NG):
        ct = [group_parts(g, c)[1].astype(F32).T.astype(BF16) for c in range(2)]
        for hf in range(2):

            def gates(i, carry, g=g, hf=hf, ct=ct):
                jj = hf * 4 + i
                j = g * TPG + jj
                ln = lanes(j)
                e2 = spread_two(j)
                grow = jnp.zeros((1, 128), F32)
                srow = jnp.zeros((1, 128), F32)
                ds = []
                for c in range(2):
                    sl = blocks[c]
                    m = r.mixed[sl, ln].astype(F32)
                    gt = r.gate[sl, ln]
                    gated = m * gt
                    gi = r.go[sl, ln].astype(F32) * r.inv[sl, :]
                    dg = gi * r.gain[0:1, ln] - gated * r.coef[sl, :]
                    grow = grow + jnp.sum(gi * gated, axis=0, keepdims=True)
                    r.dz[sl, ln] = (dg * m * r.dgate[sl, ln]).astype(BF16)
                    dm = (dg * gt).astype(BF16)
                    r.dy[sl, ln] = dm
                    dy = dm.astype(F32)
                    srow = srow + jnp.sum(dy * r.xc[sl, ln].astype(F32), axis=0, keepdims=True)
                    h0, h1 = head_rows(dy * r.y[sl, ln])
                    r.rho[c, pl.ds(2 * j, 1), :] = h0
                    r.rho[c, pl.ds(2 * j + 1, 1), :] = h1
                    fd = (dnn(r.mt[sl, 2 * H : 4 * H], e2) * dy).astype(BF16)
                    r.fd[sl, ln] = fd
                    ds.append(dnn(ct[c], fd).astype(BF16))
                r.dsb1[:, ln] = ds[1]
                put_state(
                    bwd[g][0], jj, n,
                    (r.krow[0, :, ln] * ds[1].astype(F32) + ds[0].astype(F32)).astype(BF16),
                )
                r.pk[j, 5:6, :] = grow
                r.pk[j, 6:8, :] = jnp.zeros((2, 128), F32)
                r.hsr[2:3, ln] = srow
                return carry

            lax.fori_loop(0, 4, gates, 0, unroll=4)
            for cq in range(hf * ncq // 2, (hf + 1) * ncq // 2):
                send_pieces(n, cq, me, *bwd[g])
    for g in range(NG):
        r.acc[...] = jnp.zeros_like(r.acc)

        def inner(jj, carry, g=g):
            j = g * TPG + jj
            ln = lanes(j)
            for c in range(2):
                sl = blocks[c]
                dyt = r.dy[sl, ln]
                zero = jnp.zeros_like(dyt)
                dybd = jnp.concatenate(
                    [jnp.where(half, dyt, zero), jnp.where(half, zero, dyt)], axis=0
                )
                dw = dnt(dybd, r.xc[sl, ln])
                i = 2 * j + c
                r.acc[0, c] += dw[0:B] * r.lm[i, 0:B, :] + dw[B : 2 * B] * r.lm[i, B : 2 * B, :]
                r.y[sl, ln] = dtn(r.wm[i], dybd)
                sp = row_state(states[g], jj, n) if c == 0 else r.sb1[:, ln]
                r.acc[1, c] += dnt(r.fd[sl, ln], sp)
            return carry

        lax.fori_loop(0, TPG, inner, 0, unroll=4)
        for c in range(2):
            bb, cc = group_parts(g, c)
            dg = r.acc[0, c].astype(BF16)
            r.dbc[blocks[c], g * 128 : (g + 1) * 128] = dtn(dg, cc)
            r.dbc[blocks[c], 256 + g * 128 : 256 + (g + 1) * 128] = r.acc[1, c] + dnn(dg, bb)
        owner_scan(n, halves[g], r.kb, *bwd[g], me, True)

    r.vk[:, :, 0:8, :] = jnp.zeros((2, CONV, 8, 128), F32)
    r.vk[:, :, 8 + T :, :] = jnp.zeros((2, CONV, 8, 128), F32)

    def is_owner(j):
        return (me == j) & (dp == lax.rem(j, ndp))

    def give_tile(j):
        @pl.when(jnp.logical_not(is_owner(j)))
        def _():
            rcopy(
                r.pk.at[j], r.prb.at[mine], r.ps, r.pr,
                {"dp": lax.rem(j, ndp), "ctx": j},
            ).start()

    def conv_back(c, ext, vk, w, deriv, dxc, rows):
        sl = blocks[c]
        lo = c * B
        du = dxc * deriv
        rows[0] = rows[0] + jnp.sum(du * ext[8 + lo : 8 + lo + B, :], axis=0, keepdims=True)
        rows[CONV] = rows[CONV] + jnp.sum(du, axis=0, keepdims=True)
        own = w[0] * du
        for k in range(1, CONV):
            v = du * r.live[k - 1, sl, :]
            rows[k] = rows[k] + jnp.sum(
                v * ext[8 - k + lo : 8 - k + lo + B, :], axis=0, keepdims=True
            )
            vk[k, 8 + lo : 8 + lo + B, :] = v
        for k in range(1, CONV):
            own = own + w[k] * vk[k, 8 + k + lo : 8 + k + lo + B, :]
        return own

    def before_rows(vk, w):
        prior = jnp.zeros((8, 128), F32)
        for k in range(1, CONV):
            prior = prior + w[k] * vk[k, k : k + 8, :]
        return prior

    for g in range(NG):
        r.acc[1] = jnp.zeros((2, B, 128), F32)
        take_pieces(n, me, *bwd[g])

        def outer(jj, carry, g=g):
            j = g * TPG + jj
            ln = lanes(j)
            e2 = spread_two(j)
            a1 = row_state(laters[g], jj, n).astype(F32)
            sk = skip_row(j)
            ext = r.ext.at[j % 4]
            ext[8 : 8 + T, :] = r.x[0, :, ln].astype(F32)
            ext[0:8, :] = r.hbuf[8:16, ln].astype(F32)
            vk = r.vk.at[j % 2]
            w = x_weights(ln)[0]
            rows = [jnp.zeros((1, 128), F32)] * (CONV + 1)
            for c in (1, 0):
                sl = blocks[c]
                if c == 1:
                    ds = a1
                    sp = r.sb1[:, ln]
                else:
                    ds = r.krow[1, :, ln] * a1 + r.dsb1[:, ln].astype(F32)
                    sp = row_state(states[g], jj, n)
                dsh = ds.astype(BF16)
                xf = r.xc[sl, ln].astype(F32)
                dxu = dnn(r.bcc[sl, g * 128 : (g + 1) * 128], dsh) * dnn(
                    r.mt[sl, 0 : 2 * H], e2
                )
                r.acc[1, c] += dnt(r.uu[sl, ln], dsh)
                dxs = r.y[sl, ln] + dxu
                ku = jnp.sum(xf * dxu, axis=0, keepdims=True)
                kd = jnp.sum(ds * sp.astype(F32), axis=0, keepdims=True) * r.krow[c, :, ln]
                r.hsr[c : c + 1, ln] = ku + kd
                h0, h1 = head_rows(xf * dxs)
                r.kap[c, pl.ds(2 * j, 1), :] = h0
                r.kap[c, pl.ds(2 * j + 1, 1), :] = h1
                own = conv_back(
                    c, ext, vk, w, r.cdx[sl, ln], dxs + sk * r.dy[sl, ln].astype(F32), rows
                )
                r.gx[sl, ln] = own.astype(BF16)
                if c == 1:
                    r.tails[:, ln] = own[B - 16 : B]
            r.hb[:, ln] = before_rows(vk, w)
            r.pk[j, 0 : CONV + 1, :] = jnp.concatenate(rows, axis=0)
            give_tile(j)
            return carry

        lax.fori_loop(0, TPG, outer, 0, unroll=2)
        for c in range(2):
            r.dbc[blocks[c], g * 128 : (g + 1) * 128] += r.acc[1, c]

    for j in range(4):
        sl = slice(j * 128, (j + 1) * 128)
        sd = slice(D + j * 128, D + (j + 1) * 128)
        ext = r.ext.at[j]
        ext[8 : 8 + T, :] = r.bc[:, sl].astype(F32)
        ext[0:8, :] = r.hbuf[8:16, sd].astype(F32)
        vk = r.vk.at[j % 2]
        w = bc_weights(j)[0]
        rows = [jnp.zeros((1, 128), F32)] * (CONV + 1)
        for c in (1, 0):
            own = conv_back(
                c, ext, vk, w, r.cdb[blocks[c], sl], r.dbc[blocks[c], sl], rows
            )
            r.gbc[blocks[c], sl] = own.astype(BF16)
            if c == 1:
                r.tails[:, sd] = own[B - 16 : B]
        r.hb[:, sd] = before_rows(vk, w)
        r.pk[NT + j, 0 : CONV + 1, :] = jnp.concatenate(rows, axis=0)
        r.pk[NT + j, 5:8, :] = jnp.zeros((3, 128), F32)
        give_tile(NT + j)
    back = rcopy(r.hb, r.bbuf, r.sb, r.rb_sem, {"ctx": lax.rem(me + n - 1, n)})

    @pl.when(me > 0)
    def _():
        back.start()

    of_head = (iota((H, D), 1) // HEAD_DIM == iota((H, D), 0)).astype(BF16)
    high = r.hsr[...].astype(BF16)
    low = (r.hsr[...] - high.astype(F32)).astype(BF16)
    hs = dnt(of_head, high) + dnt(of_head, low)
    rev = (iota((B, B), 0) >= iota((B, B), 1)).astype(F32)
    rate_sum = jnp.zeros((H, B), F32)
    bias_sum = jnp.zeros((H, B), F32)
    for c in range(2):
        sl = blocks[c]
        dtv = r.dt[c]
        kp = r.kap[c]
        rr = dnn_full(r.rho[c] - kp, rev) + hs[:, c : c + 1]
        gd = (kp / dtv - rate * rr) * sigmoid(r.dtr[0, :, sl].astype(F32) + bias)
        r.gdt[:, sl] = gd
        rate_sum = rate_sum - rate * dtv * rr
        bias_sum = bias_sum + gd
    skips = jnp.where(iota((H, B), 1) == 0, hs[:, 2:3], 0.0)
    r.pk[nt - 1] = dnt_full(
        ones, jnp.concatenate([rate_sum, bias_sum, skips, jnp.zeros((H, B), F32)], axis=0)
    )
    give_tile(nt - 1)

    @pl.when((me < nt) & (dp == lax.rem(me, ndp)))
    def _():
        r.prb[mine] = r.pk[me]

        alls = pl.ds(0, ne - 1)
        rcopy(r.prb.at[alls], r.prb.at[alls], r.ps, r.pr, {"ctx": me}).wait_recv()

        def collect(e, total):
            return total + r.prb[e]

        r.pob[me] = lax.fori_loop(0, ne, collect, jnp.zeros((8, 128), F32), unroll=8)

        def give(k, carry):
            e = lax.rem(mine + k, ne)
            rcopy(
                r.pob.at[me], r.pob.at[me], r.as_, r.ar,
                {"dp": e // n, "ctx": lax.rem(e, n)},
            ).start()
            return carry

        lax.fori_loop(1, ne, give, 0)

    @pl.when(me < n - 1)
    def _():
        halo.wait_send()
        back.wait_recv()

    @pl.when(me > 0)
    def _():
        back.wait_send()

    rcopy(r.kb.at[others], r.kb.at[others], r.sk, r.rk, {"ctx": me}).wait_send()
    for st, rb, pb, ob, s1, r1, s2, r2 in fwd + bwd:
        rcopy(st.at[others], rb.at[others], s1, r1, {"ctx": me}).wait_send()
        rcopy(pb.at[others], ob.at[others], s2, r2, {"ctx": me}).wait_send()

    owns = (me < nt) & (dp == lax.rem(me, ndp))

    @pl.when(owns)
    def _():
        alls = pl.ds(0, ne - 1)
        most = pl.ds(0, nt - 1)
        rcopy(r.prb.at[alls], r.prb.at[alls], r.as_, r.ar, {"ctx": me}).wait_send()
        rcopy(r.pk.at[most], r.pob.at[most], r.ps, r.ar, {"ctx": me}).wait()

    @pl.when(jnp.logical_not(owns))
    def _():
        rcopy(r.pk, r.pob, r.ps, r.ar, {"ctx": me}).wait()

    r.red[...] = r.pob[...]
    alike = r.cnt[T : T + 8, :] == r.cnt[T + 7 : T + 8, :]
    for j in range(NT + 4):
        sl = slice(j * 128, (j + 1) * 128)
        r.rh_o[:, sl] = jnp.where(alike, r.bbuf[:, sl], 0.0)


def k5_body(scale, red, rh, tail, gx_i, dz_i, gbc_i, gdt_i,
            gx_o, dz_o, gbc_o, gdt_o, cw_o, cb_o, bw_o, bb_o, al_o, db_o, sk_o, ga_o,
            gxt, gbs, sems):
    copies = [
        pltpu.make_async_copy(gx_i.at[0 : T - 16], gx_o.at[0 : T - 16], sems.at[0]),
        pltpu.make_async_copy(dz_i, dz_o, sems.at[1]),
    ]
    for cp in copies:
        cp.start()
    gdt_o[...] = gdt_i[...]
    gbs[...] = gbc_i[...]
    for j in range(NT + 4):
        sl = slice(j * 128, (j + 1) * 128)
        add = jnp.concatenate([jnp.zeros((8, 128), F32), rh[:, sl]], axis=0)
        v = (tail[:, sl] + add).astype(BF16)
        t = red[j] * scale
        if j < NT:
            gxt[:, sl] = v
            cw_o[:, sl] = t[0:4]
            cb_o[:, sl] = t[4:5]
            ga_o[:, sl] = t[5:6]
        else:
            m = j - NT
            gbs[T - 16 : T, m * 128 : (m + 1) * 128] = v
            sb = slice((m % 2) * 128, (m % 2) * 128 + 128)
            for k in range(CONV):
                bw_o[k, m // 2 : m // 2 + 1, sb] = t[k : k + 1]
            bb_o[m // 2 : m // 2 + 1, sb] = t[4:5]
    copies.append(pltpu.make_async_copy(gxt, gx_o.at[T - 16 : T], sems.at[2]))
    copies[-1].start()
    gbc_o[...] = gbs[...].reshape(T, 2, DB // 2)
    last_tile = red[NT + 4] * scale
    al_o[...] = last_tile[0:1, 0:H]
    db_o[...] = last_tile[0:1, H : 2 * H]
    sk_o[...] = last_tile[0:1, 2 * H : 3 * H]
    for cp in copies:
        cp.wait()


def sds(*shape, dtype=F32):
    return jax.ShapeDtypeStruct(shape, dtype)


def per_device(
    x_raw, bc_raw, z_gate, dt_raw, resets, conv_x_weight, conv_x_bias, conv_bc_weight,
    conv_bc_bias, a_log, dt_bias, skip_weight, norm_gain, grad_out,
):
    n = lax.axis_size("ctx")
    nh = lax.axis_size("head")
    ndp = lax.axis_size("dp")
    ncq = n // 8
    w = D // ncq
    nt = NT + 5
    ne = n * ndp
    HB = pl.BlockSpec(memory_space=pltpu.HBM)
    taken = [
        ("x", x_raw), ("bc_raw", bc_raw), ("dtr", dt_raw), ("flg", resets),
        ("alog", a_log.reshape(1, H)), ("dtb", dt_bias.reshape(1, H)), ("cxw", conv_x_weight),
        ("cxb", conv_x_bias.reshape(1, D)), ("cbw", conv_bc_weight), ("cbb", conv_bc_bias),
        ("gain", norm_gain.reshape(1, D)), ("skip", skip_weight),
    ]
    fed = [k for k, v in taken]
    held = lambda v: pltpu.with_memory_space_constraint(v, pltpu.HBM)
    ins = [(k + "_in", held(v), HB) for k, v in taken]
    ins += [("z_hbm", held(z_gate), HB), ("go_hbm", held(grad_out), HB)]
    outs = [
        ("gx", sds(T, D, dtype=BF16)), ("dz", sds(T, D, dtype=BF16)),
        ("gbc", sds(T, DB, dtype=BF16)), ("gdt", sds(H, T)), ("tails", sds(16, D + DB)),
        ("red", sds(nt, 8, 128)), ("rh_o", sds(8, D + DB)),
    ]
    V = pltpu.VMEM
    dma = pltpu.SemaphoreType.DMA
    state = V((n, ROWS, w // NG), BF16)
    scratch = [
        ("z", V((T, D), BF16)), ("go", V((T, D), BF16)), ("zs", dma), ("gs", dma),
        ("ext", V((4, T + 8, 128), F32)), ("cnt", V((T + 8, 128), F32)),
        ("live", V((CONV - 1, T, 128), F32)), ("mask", V((2, B, B), F32)),
        ("dt", V((2, H, B), F32)), ("run", V((2, H, B), F32)), ("mt", V((T, 128), BF16)),
        ("rs", V((T, 128), BF16)), ("tail", V((16, D + DB), BF16)),
        ("hbuf", V((16, D + DB), BF16)), ("xc", V((T, D), BF16)), ("bcc", V((T, DB), BF16)),
        ("cdb", V((T, DB), F32)), ("cdx", V((T, D), F32)), ("fr", V((2, NSTATE, D), F32)),
        ("kr", V((ncq, 1, w), F32)), ("kb", V((n, 1, w), F32)), ("krow", V((2, 1, D), F32)),
        ("uu", V((T, D), BF16)), ("bc", V((T, DB), BF16)), ("hsr", V((8, D), F32)),
 ("gm", V((B, B), F32)),
        ("lm", V((2 * NT, 2 * B, B), F32)), ("wm", V((2 * NT, 2 * B, B), BF16)),
        ("y", V((T, D), F32)), ("gate", V((T, D), F32)), ("dgate", V((T, D), F32)),
        ("mixed", V((T, D), BF16)), ("sb1", V((NSTATE, D), BF16)),
        ("sums_acc", V((2, T, 128), F32)), ("sums", V((16, T), F32)),
        ("sbuf", V((nh, 16, T), F32)), ("inv", V((T, 128), F32)), ("coef", V((T, 128), F32)),
        ("rho", V((2, H, B), F32)), ("dy", V((T, D), BF16)),
        ("fd", V((T, D), BF16)), ("dsb1", V((NSTATE, D), BF16)), ("acc", V((2, 2, B, 128), F32)),
        ("dbc", V((T, DB), F32)), ("kap", V((2, H, B), F32)),
        ("vk", V((2, CONV, T + 16, 128), F32)), ("pk", V((nt, 8, 128), F32)),
        ("prb", V((ne, 8, 128), F32)), ("pob", V((nt, 8, 128), F32)),
        ("hb", V((8, D + DB), F32)), ("bbuf", V((8, D + DB), F32)),
        ("sh", dma), ("rh", dma), ("sb", dma), ("rb_sem", dma),
        ("hs", dma((nh,))), ("hr", dma((nh,))),
    ]
    scratch += [
        (k, dma)
        for k in (
            "sk", "rk", "ps", "ar", "pr", "as_",
        )
    ]
    scratch += [
        (k, (pltpu.SMEM if k == "skip" else V)(v.shape, v.dtype)) for k, v in taken
    ] + [("ins", dma((len(taken),)))]
    for way in ("f0", "f1", "b0", "b1"):
        scratch += [(k + way, state) for k in ("st", "rb", "pb", "ob")]
        scratch += [(k + way, dma) for k in ("s1", "r1", "s2", "r2")]
    names = [v[0] for v in ins] + [v[0] for v in outs] + [v[0] for v in scratch]
    gx, dz, gbc, gdt, tails, red, rh = pl.pallas_call(
        functools.partial(main_body, n, nh, ndp, nt, names, fed),
        out_shape=[v[1] for v in outs],
        in_specs=[v[2] for v in ins],
        out_specs=[VM] * len(outs),
        scratch_shapes=[v[1] for v in scratch],
        compiler_params=pltpu.CompilerParams(
            vmem_limit_bytes=VMAIN, collective_id=0, has_side_effects=True
        ),
    )(*[v[1] for v in ins])
    scale = float(ndp * n * T) ** (-0.5)
    outs = pl.pallas_call(
        functools.partial(k5_body, scale),
        out_shape=(
            sds(T, D, dtype=BF16), sds(T, D, dtype=BF16), sds(T, 2, DB // 2, dtype=BF16),
            sds(H, T), sds(CONV, D), sds(1, D), sds(CONV, 2, DB // 2), sds(2, DB // 2),
            sds(1, H), sds(1, H), sds(1, H), sds(1, D),
        ),
        in_specs=[VM] * 7,
        out_specs=[HB, HB] + [VM] * 10,
        scratch_shapes=[V((16, D), BF16), V((T, DB), BF16), dma((3,))],
        compiler_params=pltpu.CompilerParams(vmem_limit_bytes=16 * 1024 * 1024),
    )(red, rh, tails, gx, dz, gbc, gdt)
    gx, dz, gbc, gdt, cw, cb, bw, bb, al, db, sk, ga = outs
    return (
        gx[None], gbc[None], dz[None], gdt[None], cw, cb.reshape(D),
        bw, bb, al.reshape(H), db.reshape(H), sk.reshape(H), ga.reshape(D),
    )


def solution(mesh):
    return jax.shard_map(
        per_device,
        mesh=mesh,
        in_specs=(
            P("dp", "ctx", "head"),
            P("dp", "ctx", None, "head"),
            P("dp", "ctx", "head"),
            P("dp", "head", "ctx"),
            P("dp", "ctx"),
            P(None, "head"),
            P("head"),
            P(None, None, "head"),
            P(None, "head"),
            P("head"),
            P("head"),
            P("head"),
            P("head"),
            P("dp", "ctx", "head"),
        ),
        out_specs=(
            P("dp", "ctx", "head"),
            P("dp", "ctx", None, "head"),
            P("dp", "ctx", "head"),
            P("dp", "head", "ctx"),
            P(None, "head"),
            P("head"),
            P(None, None, "head"),
            P(None, "head"),
            P("head"),
            P("head"),
            P("head"),
            P("head"),
        ),
        check_vma=False,
    )
```
